128 devices in a mesh: space: 16 (over y, x), vel: 8 (over z, core).
Axes of the slice: x: 4, y: 4, z: 4, core: 2. Of those that a mesh axis runs over, the one named last changes fastest.
Arguments:
- space_factor: float32 [32, 64, 16, 128], P(None, 'space'), may hold values from -16 to 16
- core_matrix: float32 [32, 32], replicated, may hold values from -0.5 to 3
- velocity_factor: float32 [32, 110592], P(None, 'vel'), may hold values from -5 to 5
- collision_rates: float32 [64, 16, 128], P('space'), may hold values from 0.05 to 0.5
Outputs:
- space_next: float32 [32, 64, 16, 128], P(None, 'space')
- core_next: float32 [32, 32], replicated
- velocity_next: float32 [32, 110592], P(None, 'vel')
The draws below stay inside these ranges and needn't reach their ends.
All inputs are finite; a program needn't handle non-finite values.
Results may differ from the reference program's by a relative error of at most 0.0003.
Values sent between devices are 32-bit elements; how exact they have to be, the bound alone decides.
No kernel may reach another device: no remote copies, remote signals or barrier semaphores. Data moves between devices by JAX's collectives and lax.ppermute only.
A program may use at most 128 MiB of HBM per device.

```python
import math
import jax
import jax.numpy as jnp
from jax import lax

RANK = 32
NY = 16
NZ = 128
NVD = 48
SUB = 3
STEPS = 1
NX = 64
NV = 110592
CELLS = 131072


def draw_space_factor(key, part):
    base_key, factor_key, random_key = jax.random.split(key, 3)
    position = (jnp.arange(NX, dtype=jnp.float32) + 0.5) / NX
    plane_base = jnp.clip(jax.random.normal(base_key, (RANK, 1, NY, NZ), jnp.float32), -4.0, 4.0)
    random_part = 0.5 * jnp.clip(jax.random.normal(random_key, (RANK, NX, NY, NZ), jnp.float32), -4.0, 4.0)
    amplitude = 0.5 + 1.5 * position
    factor = jax.random.uniform(factor_key, (RANK, NX, NY, NZ), jnp.float32, 0.5, 1.5)
    return (plane_base * factor + random_part) * amplitude[None, :, None, None]


def draw_velocity_factor(key, part):
    random_key, offset_key = jax.random.split(key)
    points = jnp.arange(NV, dtype=jnp.int32)
    position = ((points // (NVD * NVD)).astype(jnp.float32) + 0.5) / NVD
    offsets = jax.random.uniform(offset_key, (RANK, 1), jnp.float32, -0.5, 0.5)
    random_part = jnp.clip(jax.random.normal(random_key, (RANK, NV), jnp.float32), -4.0, 4.0)
    amplitude = 0.5 + 1.5 * position
    return random_part + offsets * amplitude[None, :]


def draw_core_matrix(key, part):
    diagonal_key, spread_key = jax.random.split(key)
    diagonal = jax.random.uniform(diagonal_key, (RANK,), jnp.float32, 1.5, 3.0)
    spread = jnp.clip(0.1 * jax.random.normal(spread_key, (RANK, RANK), jnp.float32), -0.5, 0.5)
    mask_off = 1.0 - jnp.eye(RANK, dtype=jnp.float32)
    return spread * mask_off + jnp.diag(diagonal)


def shard_levels(stream_key, shape, cuts, smallest, largest):
    def one(axis_at, parts):
        draws = jax.random.uniform(jax.random.fold_in(jax.random.fold_in(stream_key, 6), axis_at), (parts,), jnp.float32, smallest / len(cuts), largest / len(cuts))
        return jnp.repeat(jnp.exp(draws), shape[axis_at] // parts).reshape((-1,) + (1,) * (len(shape) - axis_at - 1))

    level = one(*cuts[0])
    for cut in cuts[1:]:
        level = level * one(*cut)
    return level


def setup_inputs(seed: int = 0) -> dict:
    seeds = jax.random.split(jax.random.key(seed), 5)
    space_factor = draw_space_factor(jax.random.fold_in(seeds[4], 71), 0)
    core_matrix = draw_core_matrix(jax.random.fold_in(seeds[4], 71), 0)
    velocity_factor = draw_velocity_factor(jax.random.fold_in(seeds[4], 71), 0)
    collision_rates = jnp.clip(jnp.exp(math.log(0.5) - 2.3025851 * jax.random.uniform(seeds[3], (NX, NY, NZ), jnp.float32) ** shard_levels(seeds[3], (NX, NY, NZ), ((0, 16),), -0.2, 0.2)), 0.05, 0.5)
    return {"space_factor": space_factor, "core_matrix": core_matrix, "velocity_factor": velocity_factor, "collision_rates": collision_rates}


highest = lax.Precision.HIGHEST
velocity_extent = 0.25
thermal_speed = 0.125
time_step = 1.0

def velocity_grid(first_point, length):
    points = first_point + jnp.arange(length, dtype=jnp.int32)
    digits = [points // (NVD * NVD), points // NVD % NVD, points % NVD]
    components = [velocity_extent * ((2 * numeral + 1).astype(jnp.float32) / NVD - 1.0) for numeral in digits]
    axis_points = velocity_extent * ((2 * jnp.arange(NVD, dtype=jnp.int32) + 1).astype(jnp.float32) / NVD - 1.0)
    twice_variance = 2.0 * thermal_speed * thermal_speed
    line_mean = jnp.mean(jnp.exp(-axis_points * axis_points / twice_variance))
    squared_speed = components[0] * components[0] + components[1] * components[1] + components[2] * components[2]
    profile = jnp.exp(-squared_speed / twice_variance) / (line_mean * line_mean * line_mean)
    return (jnp.stack(components), profile)

def products(leading, others, divisor):
    return lax.dot_general(leading, others, (((1,), (1,)), ((), ())), precision=highest) / divisor

def flatten_rows(values):
    return values.reshape(values.shape[0], -1)

def apply_rows(matrix, values):
    return jnp.dot(matrix, flatten_rows(values), precision=highest).reshape((matrix.shape[0],) + values.shape[1:])

def triangular_inverse(gram_matrix):
    factor = jnp.linalg.cholesky(gram_matrix)
    identity = jnp.eye(gram_matrix.shape[0], dtype=gram_matrix.dtype)
    return jax.scipy.linalg.solve_triangular(factor, identity, lower=True)

def lower_differences(values, lower_plane):
    shifted = jnp.concatenate([lower_plane, values[:, :-1]], axis=1)
    return [values - shifted, values - jnp.roll(values, 1, 2), values - jnp.roll(values, 1, 3)]

def velocity_stack(values, velocity):
    positive = jnp.maximum(velocity, 0.0)
    negative = jnp.minimum(velocity, 0.0)
    rank_count = values.shape[0]
    forward = (values[None] * positive[:, None]).reshape(3 * rank_count, -1)
    backward = (values[None] * negative[:, None]).reshape(3 * rank_count, -1)
    return jnp.concatenate([forward, backward], axis=0)

def mixing(space_terms):
    rank_count = space_terms.shape[0]
    backward = [space_terms[:, dimension * rank_count:(dimension + 1) * rank_count] for dimension in range(3)]
    forward = [-section.T for section in backward]
    return jnp.concatenate(backward + forward + [space_terms[:, 3 * rank_count:4 * rank_count]], axis=1)

def kinetic_update(padded, rates, flux_blocks, weights, moments):
    center = padded[:, 1:-1]
    backward = [center - padded[:, :-2], center - jnp.roll(center, 1, 2), center - jnp.roll(center, 1, 3)]
    forward = [padded[:, 2:] - center, jnp.roll(center, -1, 2) - center, jnp.roll(center, -1, 3) - center]
    stacked = jnp.concatenate(backward + forward, axis=0).reshape(6 * center.shape[0], -1)
    flat_center = flatten_rows(center)
    transport = jnp.dot(flux_blocks, stacked, precision=highest)
    density = jnp.dot(weights, flat_center, precision=highest)
    change = -transport + rates.reshape(1, -1) * (moments[:, None] * density[None, :] - flat_center)
    return (flat_center + time_step * change).reshape(center.shape)

def velocity_update(values, mixing_blocks, velocity, profile, column_means):
    rank_count = values.shape[0]
    stacked = jnp.concatenate([velocity_stack(values, velocity), values], axis=0)
    change = -jnp.dot(mixing_blocks, stacked, precision=highest)
    source = jnp.dot(mixing_blocks[:, 6 * rank_count:], column_means, precision=highest)
    return values + time_step * (change + source[:, None] * profile[None, :])

def core_update(current, space_terms, point_terms, weights, moments):
    rank_count = current.shape[0]
    scaled = jnp.dot(space_terms[:, 3 * rank_count:4 * rank_count], current, precision=highest)
    change = -scaled + jnp.outer(jnp.dot(scaled, weights, precision=highest), moments)
    for dimension in range(3):
        section = space_terms[:, dimension * rank_count:(dimension + 1) * rank_count]
        plus_block = point_terms[:, dimension * rank_count:(dimension + 1) * rank_count]
        minus_block = point_terms[:, (dimension + 3) * rank_count:(dimension + 4) * rank_count]
        change = change - jnp.dot(jnp.dot(section, current, precision=highest), plus_block.T, precision=highest)
        change = change + jnp.dot(jnp.dot(section.T, current, precision=highest), minus_block.T, precision=highest)
    return current + time_step * change

def project(space_state, space_old, point_state, point_old, rates, velocity, profile):
    space_inverse = triangular_inverse(products(flatten_rows(space_state), flatten_rows(space_state), CELLS))
    point_inverse = triangular_inverse(products(point_state, point_state, NV))
    space_new = apply_rows(space_inverse, space_state)
    point_new = jnp.dot(point_inverse, point_state, precision=highest)
    space_items = lower_differences(space_new, space_new[:, -1:]) + [rates[None] * space_new, space_old]
    space_others = jnp.concatenate([flatten_rows(member) for member in space_items], axis=0)
    space_terms = products(flatten_rows(space_new), space_others, CELLS)
    point_others = jnp.concatenate([velocity_stack(point_new, velocity), point_old], axis=0)
    point_terms = products(point_new, point_others, NV)
    weights = jnp.mean(point_new, axis=1)
    moments = jnp.dot(point_new, profile, precision=highest) / NV
    return (space_new, point_new, space_terms, point_terms, weights, moments)

def reference(space_factor, core_matrix, velocity_factor, collision_rates):
    rank_count = core_matrix.shape[0]
    velocity, profile = velocity_grid(0, NV)
    basis_space, basis_point, space_terms, point_terms, weights, moments = project(space_factor, space_factor, velocity_factor, velocity_factor, collision_rates, velocity, profile)
    current = jnp.dot(jnp.dot(space_terms[:, 4 * rank_count:], core_matrix, precision=highest), point_terms[:, 6 * rank_count:].T, precision=highest)
    for step_number in range(STEPS):
        kinetic = apply_rows(current.T, basis_space)
        for substep in range(SUB):
            padded = jnp.concatenate([kinetic[:, -1:], kinetic, kinetic[:, :1]], axis=1)
            kinetic = kinetic_update(padded, collision_rates, point_terms[:, :6 * rank_count], weights, moments)
        mixing_blocks = mixing(space_terms)
        spread_point = jnp.dot(current, basis_point, precision=highest)
        for substep in range(SUB):
            spread_point = velocity_update(spread_point, mixing_blocks, velocity, profile, jnp.mean(spread_point, axis=1))
        fresh_space, fresh_point, space_terms, point_terms, weights, moments = project(kinetic, basis_space, spread_point, basis_point, collision_rates, velocity, profile)
        current = jnp.dot(jnp.dot(space_terms[:, 4 * rank_count:], current, precision=highest), point_terms[:, 6 * rank_count:].T, precision=highest)
        for substep in range(SUB):
            current = core_update(current, space_terms, point_terms, weights, moments)
        basis_space, basis_point = (fresh_space, fresh_point)
    return (basis_space, current, basis_point)
```

```python
import jax
import jax.numpy as jnp
from jax import lax
from jax.sharding import PartitionSpec as P

NVD = 48
SUB = 3
LOW = SUB + 1
HIGH = SUB

highest = lax.Precision.HIGHEST
velocity_extent = 0.25
thermal_speed = 0.125
time_step = 1.0


def mm(a, b):
    return jnp.dot(a, b, precision=highest)


def gram(a, b):
    return lax.dot_general(a, b, (((1,), (1,)), ((), ())), precision=highest)


def velocity_grid(first_point, length):
    points = first_point + jnp.arange(length, dtype=jnp.int32)
    digits = [points // (NVD * NVD), points // NVD % NVD, points % NVD]
    components = [
        velocity_extent * ((2 * numeral + 1).astype(jnp.float32) / NVD - 1.0) for numeral in digits
    ]
    axis_points = velocity_extent * (
        (2 * jnp.arange(NVD, dtype=jnp.int32) + 1).astype(jnp.float32) / NVD - 1.0
    )
    twice_variance = 2.0 * thermal_speed * thermal_speed
    line_mean = jnp.mean(jnp.exp(-axis_points * axis_points / twice_variance))
    squared_speed = (
        components[0] * components[0]
        + components[1] * components[1]
        + components[2] * components[2]
    )
    profile = jnp.exp(-squared_speed / twice_variance) / (line_mean * line_mean * line_mean)
    velocity = jnp.stack(components)
    return jnp.concatenate([jnp.maximum(velocity, 0.0), jnp.minimum(velocity, 0.0)], axis=0), profile


def profile_moments():
    t = velocity_extent * ((2 * jnp.arange(NVD, dtype=jnp.int32) + 1).astype(jnp.float32) / NVD - 1.0)
    shape = jnp.exp(-t * t / (2.0 * thermal_speed * thermal_speed))
    shape = shape / jnp.mean(shape)
    plus = jnp.mean(shape * jnp.maximum(t, 0.0))
    minus = jnp.mean(shape * jnp.minimum(t, 0.0))
    one = jnp.mean(shape)
    square = one * one
    return jnp.stack([square * one] + [square * plus] * 3 + [square * minus] * 3)


def axis_sum_steps(values, axis, routes):
    moved = [lax.ppermute(values, axis, route) for route in routes]
    if len(moved) == 1:
        return values + moved[0]
    return (values + moved[1]) + (moved[0] + moved[2])


def routes_x():
    return [[(4 * y + x, 4 * y + (x + d) % 4) for y in range(4) for x in range(4)] for d in (1, 2, 3)]


def routes_y():
    return [[(4 * y + x, 4 * ((y + d) % 4) + x) for y in range(4) for x in range(4)] for d in (1, 2, 3)]


def routes_z():
    return [[(2 * z + c, 2 * ((z + d) % 4) + c) for z in range(4) for c in range(2)] for d in (1, 2, 3)]


def routes_core():
    return [[(2 * z + c, 2 * z + 1 - c) for z in range(4) for c in range(2)]]


def total(space_part, point_part):
    space_part = axis_sum_steps(space_part, "space", routes_x())
    point_part = axis_sum_steps(point_part, "vel", routes_z())
    space_part = axis_sum_steps(space_part, "space", routes_y())
    point_part = axis_sum_steps(point_part, "vel", routes_core())
    return space_part, point_part


def triangular(gram_matrix):
    factor = jnp.linalg.cholesky(gram_matrix)
    identity = jnp.eye(gram_matrix.shape[0], dtype=gram_matrix.dtype)
    return factor, jax.scipy.linalg.solve_triangular(factor, identity, lower=True)


def flat(values):
    return values.reshape(values.shape[0], -1)


def space_sums(lower, values, rates, extra):
    padded = jnp.concatenate([lower, values], axis=1)
    items = [
        values,
        values - padded[:, :-1],
        values - jnp.roll(values, 1, 2),
        values - jnp.roll(values, 1, 3),
        rates[None] * values,
    ] + extra
    return gram(flat(values), jnp.concatenate([flat(item) for item in items], axis=0))


def coefficients(space, point, rank):
    base, base_inverse = triangular(space[:, :rank])
    cv, cv_inverse = triangular(point[:, :rank])
    turned = [
        mm(mm(base_inverse, space[:, (1 + d) * rank : (2 + d) * rank]), base_inverse.T) for d in range(4)
    ]
    flux = [mm(mm(cv_inverse, point[:, (1 + k) * rank : (2 + k) * rank]), cv_inverse.T) for k in range(6)]
    return base, base_inverse, cv, cv_inverse, turned[:3], turned[3], flux


def per_device(space_factor, core_matrix, velocity_factor, collision_rates):
    rank = core_matrix.shape[0]
    planes = space_factor.shape[1]
    devices = lax.axis_size("space")
    up = [(i, (i + 1) % devices) for i in range(devices)]
    down = [((i + 1) % devices, i) for i in range(devices)]
    below = lax.ppermute(space_factor[:, planes - LOW :], "space", up)
    above = lax.ppermute(space_factor[:, :HIGH], "space", down)
    rates_below = lax.ppermute(collision_rates[planes - LOW + 1 :], "space", up)
    rates_above = lax.ppermute(collision_rates[: HIGH - 1], "space", down)
    point_rows = velocity_factor.shape[1]
    cells_total = planes * space_factor.shape[2] * space_factor.shape[3] * devices
    points_total = point_rows * lax.axis_size("vel")
    shifts, profile = velocity_grid(lax.axis_index("vel") * point_rows, point_rows)
    ones = jnp.ones_like(profile)
    seven = jnp.concatenate([ones[None], shifts], axis=0)
    products = (seven[:, None] * seven[None]).reshape(49, -1)

    space = space_sums(below[:, -1:], space_factor, collision_rates, []) / cells_total
    stack = jnp.concatenate(
        [velocity_factor] + [shifts[k][None] * velocity_factor for k in range(6)] + [products, profile[None]], axis=0
    )
    point = gram(velocity_factor, stack) / points_total
    space, point = total(space, point)

    base, base_inverse, cv, cv_inverse, a, e, flux = coefficients(space, point, rank)
    raw_moments = point[:, 7 * rank :]
    weights = mm(cv_inverse, raw_moments[:, 0])
    moments = mm(cv_inverse, raw_moments[:, 49])
    to_kinetic = mm(core_matrix, cv).T
    to_spread = mm(base.T, core_matrix)
    mixers = a + [-member.T for member in a]
    gm = profile_moments()
    m0 = mm(to_spread, raw_moments[:, :49])
    means = [m0[:, 0]]
    first = m0[:, :7] - mm(e, m0[:, :7]) + jnp.outer(mm(e, means[0]), gm)
    for k in range(6):
        first = first - mm(mixers[k], m0[:, 7 * (k + 1) : 7 * (k + 2)])
    means.append(first[:, 0])
    second = first[:, 0] - mm(e, first[:, 0]) + mm(e, means[1]) * gm[0]
    for k in range(6):
        second = second - mm(mixers[k], first[:, k + 1])
    means.append(second)

    wide = jnp.concatenate([below, space_factor, above], axis=1)
    rates = jnp.concatenate([rates_below, collision_rates, rates_above], axis=0)
    kinetic = mm(to_kinetic, flat(wide)).reshape(wide.shape)
    flux_blocks = jnp.concatenate(flux, axis=1)
    for substep in range(SUB):
        center = kinetic[:, 1:-1]
        here = rates[substep : rates.shape[0] - substep]
        differences = [
            center - kinetic[:, :-2],
            center - jnp.roll(center, 1, 2),
            center - jnp.roll(center, 1, 3),
            kinetic[:, 2:] - center,
            jnp.roll(center, -1, 2) - center,
            jnp.roll(center, -1, 3) - center,
        ]
        transport = mm(flux_blocks, jnp.concatenate([flat(d) for d in differences], axis=0))
        fc = flat(center)
        density = mm(weights, fc)
        change = -transport + here.reshape(1, -1) * (moments[:, None] * density[None, :] - fc)
        kinetic = (fc + time_step * change).reshape(center.shape)
    lower_plane, kinetic = kinetic[:, :1], kinetic[:, 1:]

    spread = mm(to_spread, velocity_factor)
    mixing = jnp.concatenate(mixers + [e], axis=1)
    for substep in range(SUB):
        stack = jnp.concatenate([shifts[k][None] * spread for k in range(6)] + [spread], axis=0)
        source = mm(e, means[substep])
        spread = spread + time_step * (source[:, None] * profile[None] - mm(mixing, stack))

    space = space_sums(lower_plane, kinetic, collision_rates, [space_factor]) / cells_total
    stack = jnp.concatenate(
        [spread] + [shifts[k][None] * spread for k in range(6)] + [velocity_factor, ones[None], profile[None]], axis=0
    )
    point = gram(spread, stack) / points_total
    space, point = total(space, point)
    base, base_inverse, cv, cv_inverse, a, e, flux = coefficients(space, point, rank)
    weights = mm(cv_inverse, point[:, 8 * rank])
    moments = mm(cv_inverse, point[:, 8 * rank + 1])
    left = mm(base_inverse, space[:, 5 * rank :])
    right = mm(cv_inverse, point[:, 7 * rank : 8 * rank])
    current = mm(mm(left, core_matrix), right.T)
    for substep in range(SUB):
        scaled = mm(e, current)
        change = -scaled + jnp.outer(mm(scaled, weights), moments)
        for d in range(3):
            change = change - mm(mm(a[d], current), flux[d].T) + mm(mm(a[d].T, current), flux[d + 3].T)
        current = current + time_step * change
    fresh_space = mm(base_inverse, flat(kinetic)).reshape(kinetic.shape)
    fresh_point = mm(cv_inverse, spread)
    return (fresh_space, current, fresh_point)


def solution(mesh):
    return jax.shard_map(
        per_device,
        mesh=mesh,
        in_specs=(P(None, "space", None, None), P(), P(None, "vel"), P("space", None, None)),
        out_specs=(P(None, "space", None, None), P(), P(None, "vel")),
        check_vma=False,
    )
```

```python
import jax
import jax.numpy as jnp
import numpy as np
from jax import lax
from jax.experimental import pallas as pl
from jax.experimental.pallas import tpu as pltpu
from jax.sharding import PartitionSpec as P

RANK = 32
NVD = 48
SUB = 3
LOW = SUB + 1
HIGH = SUB
NY = 16
NZ = 128
OWN = 4
Q1 = 6
HALF = NVD * NVD // 2
PLANE = NY * NZ
PAD = PLANE + 2 * NZ
WIDE = LOW + OWN + HIGH
INTERPRET = False

f32 = jnp.float32
bf16 = jnp.bfloat16
highest = lax.Precision.HIGHEST


def tables():
    t = np.float32(0.25) * ((2 * np.arange(NVD) + 1).astype(np.float32) / np.float32(NVD) - np.float32(1.0))
    t = t.astype(np.float32)
    shape = np.exp(-(t.astype(np.float64) ** 2) / (2.0 * 0.125 * 0.125))
    shape = shape / shape.mean()
    plus, minus = np.maximum(t, 0), np.minimum(t, 0)
    u2, u3 = np.repeat(t, NVD), np.tile(t, NVD)
    g23 = np.repeat(shape, NVD) * np.tile(shape, NVD)
    sides = [(1, "p"), (2, "p"), (3, "p"), (1, "m"), (2, "m"), (3, "m")]
    names = [()] + [(s,) for s in sides]
    where = {(): 0}
    for k in range(6):
        where[(k,)] = k + 1
    for j in range(6):
        for k in range(j, 6):
            if k != j and sides[j][0] == sides[k][0]:
                continue
            where[(j, k)] = len(names)
            names.append((sides[j], sides[k]))
    base = np.zeros((2, 32, HALF))
    scale = np.zeros((NVD, 128))
    value = {"p": np.maximum, "m": np.minimum}
    for row, name in enumerate(names):
        b = np.ones(NVD * NVD)
        c = np.ones(NVD)
        for d, sign in name:
            if d == 1:
                c = c * value[sign](t.astype(np.float64), 0)
            elif d == 2:
                b = b * value[sign](u2.astype(np.float64), 0)
            else:
                b = b * value[sign](u3.astype(np.float64), 0)
        base[:, row] = b.reshape(2, HALF)
        scale[:, row] = c
    last = len(names)
    base[:, last] = g23.reshape(2, HALF)
    scale[:, last] = shape
    select = np.zeros((32, 7 * 128), np.float32)
    for j in range(7):
        for k in range(7):
            pair = tuple(sorted([i - 1 for i in (j, k) if i > 0]))
            if pair in where:
                select[where[pair], j * 128 + k] = 1.0
    means = np.zeros((8, 128), np.float32)
    means[:, 0] = 1.0
    means[:, 1:4] = (shape * plus).mean()
    means[:, 4:7] = (shape * minus).mean()
    rows = np.zeros((2, 8, HALF), np.float32)
    rows[:, 0] = u2.reshape(2, HALF)
    rows[:, 1] = np.maximum(u3, 0).reshape(2, HALF)
    rows[:, 2] = np.minimum(u3, 0).reshape(2, HALF)
    rows[:, 3] = g23.reshape(2, HALF)
    speeds = np.concatenate([plus, minus, shape]).astype(np.float32)
    return rows, base.astype(np.float32), scale.astype(np.float32), select, means, speeds, last


ROWS, PHI, PHI_SCALE, SELECT, MEANS, SPEEDS, LAST = tables()


def split(x):
    hi = x.astype(bf16)
    return hi, (x - hi.astype(f32)).astype(bf16)


def dot(a, b):
    return jnp.dot(a, b, preferred_element_type=f32)


def dot_t(a, b):
    return lax.dot_general(a, b, (((1,), (1,)), ((), ())), preferred_element_type=f32)


def mm(a, b):
    return jnp.dot(a, b, precision=highest, preferred_element_type=f32)


def mm_t(a, b):
    return lax.dot_general(a, b, (((1,), (1,)), ((), ())), precision=highest, preferred_element_type=f32)


def lanes(shape):
    return lax.broadcasted_iota(jnp.int32, shape, len(shape) - 1)


def sublanes(shape):
    return lax.broadcasted_iota(jnp.int32, shape, len(shape) - 2)


def eye():
    return (lanes((RANK, RANK)) == sublanes((RANK, RANK))).astype(f32)


def call(kernel, outs, ins, args, scratch=(), name=None):
    spaces = {"v": pltpu.VMEM, "s": pltpu.SMEM}
    return pl.pallas_call(
        kernel,
        out_shape=[jax.ShapeDtypeStruct(s, d) for s, d in outs],
        in_specs=[pl.BlockSpec(memory_space=spaces[c]) for c in ins],
        out_specs=[pl.BlockSpec(memory_space=pltpu.VMEM) for _ in outs],
        scratch_shapes=list(scratch),
        compiler_params=pltpu.CompilerParams(vmem_limit_bytes=58 * 1024 * 1024),
        interpret=INTERPRET,
        name=name,
    )(*args)


def point_tiles(first, second, y, positive, extra):
    lane = lanes((RANK, 128))
    middle = (lane >= 32) & (lane < 64)
    tile_a = first + jnp.where(middle, 0.0, second)
    y = jnp.where(lane < 32, y, 0.0)
    y = jnp.where(positive, pltpu.roll(y, 64, 1) if not INTERPRET else jnp.roll(y, 64, 1), y)
    return tile_a, jnp.where(middle, second, 0.0) + y + extra


def roll_lanes(x, shift):
    return jnp.roll(x, shift, 1) if INTERPRET else pltpu.roll(x, shift % x.shape[1], 1)


def stacked(values, rows, h):
    return jnp.concatenate(
        [values, values * rows[h, 0:1, :], values * rows[h, 1:2, :], values * rows[h, 2:3, :]], axis=0
    )


def point_sums_kernel(v_ref, speeds, rows, phi, scale, values, out):
    q0 = v_ref[0] * Q1
    phi_parts = [split(phi[h]) for h in range(2)]

    def body(b, carry):
        sums, y, moments = list(carry[:2]), carry[2], carry[3]
        u = speeds[q0 + b] + speeds[NVD + q0 + b]
        for h in range(2):
            start = pl.multiple_of(b * (2 * HALF) + h * HALF, 128)
            sh, sl = split(stacked(values[:, pl.ds(start, HALF)], rows, h))
            lh, ll = sh[:RANK], sl[:RANK]
            ph, plo = phi_parts[h]
            both = jnp.concatenate([lh, ll], axis=0)
            t = dot_t(both, sh)
            t = t[:RANK] + t[RANK:] + dot_t(lh, sl)
            m = dot_t(both, ph)
            m = m[:RANK] + m[RANK:] + dot_t(lh, plo)
            sums[h] = sums[h] + t
            y = y + u * t
            moments = moments + m * scale[pl.ds(q0 + b, 1), :RANK]
        return sums[0], sums[1], y, moments

    zero = jnp.zeros((RANK, 128), f32)
    first, second, y, moments = lax.fori_loop(0, Q1, body, (zero, zero, zero, jnp.zeros((RANK, RANK), f32)))
    moments = jnp.concatenate([jnp.zeros((RANK, 96), f32), moments], axis=1)
    tile_a, tile_b = point_tiles(first, second, y, v_ref[0] >= 4, moments)
    out[:, :128] = tile_a
    out[:, 128:] = tile_b


def point_sums(v, values):
    return call(
        point_sums_kernel, [((RANK, 256), f32)], "ssvvvv",
        (v, SPEEDS, ROWS, PHI, PHI_SCALE, values), name="point_sums",
    )[0]


def space_sums_kernel(values, below, rates, out, hi, lo, zh, zl, ch, cl):
    for y in range(NY):
        a, b = split(below[pl.ds(y, RANK, stride=NY), :])
        hi[:, y * NZ : (y + 1) * NZ] = a
        lo[:, y * NZ : (y + 1) * NZ] = b

    def load(p, carry):
        for y in range(NY):
            block = values[pl.ds(p * NY + y, RANK, stride=OWN * NY), :]
            at = pl.multiple_of(p * PLANE + y * NZ, 128)
            a, b = split(block)
            hi[:, pl.ds(at + PLANE, NZ)] = a
            lo[:, pl.ds(at + PLANE, NZ)] = b
            a, b = split(roll_lanes(block, 1))
            zh[:, pl.ds(at, NZ)] = a
            zl[:, pl.ds(at, NZ)] = b
            a, b = split(block * rates[pl.ds(p * NY + y, 1), :])
            ch[:, pl.ds(at, NZ)] = a
            cl[:, pl.ds(at, NZ)] = b
        return carry

    lax.fori_loop(0, OWN, load, 0)

    def body(p, carry):
        t, c = carry
        at = pl.multiple_of(p * PLANE, 128)

        def stack(main, turned):
            here = main[:, pl.ds(at + PLANE, PLANE)]
            wrapped = jnp.concatenate([here[:, PLANE - NZ :], here[:, : PLANE - NZ]], axis=1)
            return jnp.concatenate(
                [here, main[:, pl.ds(at, PLANE)], wrapped, turned[:, pl.ds(at, PLANE)]], axis=0
            )

        sh, sl = stack(hi, zh), stack(lo, zl)
        both = jnp.concatenate([sh[:RANK], sl[:RANK]], axis=0)
        part = dot_t(both, sh)
        t = t + part[:RANK] + part[RANK:] + dot_t(sh[:RANK], sl)
        part = dot_t(both, ch[:, pl.ds(at, PLANE)])
        c = c + part[:RANK] + part[RANK:] + dot_t(sh[:RANK], cl[:, pl.ds(at, PLANE)])
        return t, c

    t, c = lax.fori_loop(0, OWN, body, (jnp.zeros((RANK, 128), f32), jnp.zeros((RANK, RANK), f32)))
    out[:, :128] = t
    out[:, 128:] = jnp.concatenate([c, jnp.zeros((RANK, 96), f32)], axis=1)


def space_sums(values, below, rates):
    own = (RANK, OWN * PLANE)
    return call(
        space_sums_kernel, [((RANK, 256), f32)], "vvv", (values, below, rates),
        [pltpu.VMEM((RANK, (OWN + 1) * PLANE), bf16)] * 2 + [pltpu.VMEM(own, bf16)] * 4, name="space_sums",
    )[0]


def factor_pair(first, second):
    zeros = jnp.zeros((RANK, 64), f32)
    works = [jnp.concatenate([g, eye(), zeros], axis=1) for g in (first, second)]
    row = sublanes((RANK, 128))
    for k in range(RANK):
        for n in range(2):
            w = works[n]
            scale = lax.rsqrt(w[k : k + 1, k : k + 1])
            lead = w[k : k + 1, :] * scale
            column = w[:, k : k + 1] * scale
            works[n] = jnp.where(row > k, w - column * lead, jnp.where(row == k, lead, w))
    return [(w[:, :RANK], w[:, RANK : 2 * RANK]) for w in works]


def transposed(x):
    return mm_t(eye(), x)


def point_blocks(tiles, points_total):
    t = tiles * (1.0 / points_total)
    gram = t[:, 0:32]
    plus = [t[:, 192:224], t[:, 160:192], t[:, 64:96]]
    minus = [t[:, 128:160], t[:, 32:64], t[:, 96:128]]
    return gram, plus, minus, t[:, 224:256]


def congruent(inverse, blocks):
    inverse_t = transposed(inverse)
    half = mm(jnp.concatenate(blocks, axis=0), inverse_t)
    return [mm(inverse, half[k * RANK : (k + 1) * RANK]) for k in range(len(blocks))]


def small_first_kernel(cells_total, points_total, space, point, core, select, means, wk, wl, src):
    s = space[...] * (1.0 / cells_total)
    gram = s[:, 0:32]
    gram_v, plus, minus, raw = point_blocks(point[...], points_total)
    (upper, inverse), (upper_v, inverse_v) = factor_pair(gram, gram_v)
    identity = eye()
    raw_a = [gram - s[:, 32 * (d + 1) : 32 * (d + 2)] for d in range(3)]
    to_spread = mm(upper, core[...])
    to_kinetic_t = mm_t(core[...], upper_v)
    zeros = jnp.zeros((RANK, 32), f32)
    inverse_t = transposed(inverse)
    triple = jnp.concatenate([inverse_t] * 3 + [zeros], axis=1)
    left = (
        [mm(inverse, s[:, 128:160])] + [mm(inverse, a) for a in raw_a] + [mm_t(inverse, a) for a in raw_a]
    )
    turned = mm(jnp.concatenate(left, axis=0), triple)
    one = jnp.concatenate([identity] * 3 + [zeros], axis=1)
    e_wide = turned[:RANK]
    mixers = [one - e_wide] + [-turned[RANK * (d + 1) : RANK * (d + 2)] for d in range(3)]
    mixers = mixers + [turned[RANK * (d + 4) : RANK * (d + 5)] for d in range(3)]
    stack = jnp.concatenate(mixers, axis=0)
    wl[1] = stack
    wl[0] = mm(stack[:, :RANK], jnp.concatenate([to_spread] * 3 + [zeros], axis=1))
    square = [m[:, :RANK] for m in mixers]
    e = e_wide[:, :RANK]
    moved = mm(mm(to_spread, raw), select[...])
    groups = [moved[:, 128 * j : 128 * (j + 1)] for j in range(7)]
    lane = lanes((RANK, 128))
    source = [mm(e, groups[0])[:, 0:1]]
    following = mm(square[0], groups[0]) + source[0] * means[0:1, :]
    for j in range(1, 7):
        following = following + mm(square[j], groups[j])
    source.append(mm(e, following)[:, 0:1])
    third = mm(square[0], jnp.where(lane == 0, following, 0.0))
    for j in range(1, 7):
        third = third + mm(square[j], jnp.where(lane == j, following, 0.0))
    third = jnp.sum(third, axis=1, keepdims=True) + source[1] * means[0:1, 0:1]
    source.append(mm(e, jnp.broadcast_to(third, (RANK, 128)))[:, 0:1])
    for n in range(3):
        src[n] = jnp.where((lane >= 96) & (lane < 99), source[n], 0.0)
    flux = congruent(inverse_v, plus + minus)
    turned_raw = mm(inverse_v, raw)
    weights = turned_raw[:, 0:1]
    moments_row = transposed(turned_raw)[LAST : LAST + 1, :]
    center = identity
    blocks = []
    for d in range(3):
        center = center - flux[d] + flux[d + 3]
        blocks += [flux[d], -flux[d + 3]]
    blocks = [center] + blocks
    relax_t = weights * moments_row - identity
    empty = jnp.zeros((RANK, 6 * RANK), f32)
    for kind in range(2):
        if kind == 0:
            parts = [mm(to_kinetic_t, block) for block in blocks]
            relax = mm(to_kinetic_t, relax_t)
        else:
            parts, relax = blocks, relax_t
        wk[kind, :RANK, :] = transposed(jnp.concatenate(parts, axis=0))
        wk[kind, RANK:, :] = jnp.concatenate([transposed(relax), empty], axis=1)


def small_first(space, point, core, cells_total, points_total):
    def kernel(*refs):
        small_first_kernel(cells_total, points_total, *refs)

    return call(
        kernel, [((2, 64, 224), f32), ((2, 224, 128), f32), ((3, RANK, 128), f32)], "vvvvv",
        (space, point, core, SELECT, MEANS), name="small_first",
    )


def evolve_point_kernel(v_ref, speeds, rows, wl, src, values, new, out):
    q0 = v_ref[0] * Q1
    lane_w = lanes((RANK, 128))
    low_lane = ((lane_w >= 64) & (lane_w < 96)) | (lane_w == 97)

    def weights_of(w):
        hi = w.astype(bf16).astype(f32)
        return jnp.where(low_lane, w - hi, hi).astype(bf16)

    def piece(kind, n):
        return wl[kind, n * RANK : (n + 1) * RANK, :]

    fixed = [
        [jnp.concatenate([weights_of(piece(kind, n)) for n in ((5, 3, 6) if h == 0 else (2, 3, 6))], axis=0) for h in range(2)]
        for kind in range(2)
    ]
    tops = []
    aux = []
    for h in range(2):
        gh, gl = split(rows[h, 3:4, :])
        row = sublanes((16, HALF))
        gh, gl = gh.astype(f32), gl.astype(f32)
        tops.append(jnp.where(row < 2, gh, jnp.where(row == 2, gl, 0.0)).astype(bf16))
        aux.append(jnp.where(row == 0, 1.0, jnp.where(row == 1, gh, jnp.where(row == 2, gl, 0.0))).astype(bf16))

    def body(b, carry):
        sums, y, cross, ones_sum = list(carry[:2]), carry[2], carry[3], carry[4]
        up = speeds[q0 + b]
        um = speeds[NVD + q0 + b]
        g1 = speeds[2 * NVD + q0 + b]
        u = up + um
        moving = [piece(kind, 0) + up * piece(kind, 1) + um * piece(kind, 4) for kind in range(2)]
        heads = [weights_of(moving[min(n, 1)] + g1 * src[n]) for n in range(3)]
        for h in range(2):
            start = pl.multiple_of(b * (2 * HALF) + h * HALF, 128)
            state = values[:, pl.ds(start, HALF)]
            raw_hi, raw_lo = split(state)
            hi, lo = raw_hi, raw_lo
            for n in range(SUB):
                if n > 0:
                    hi, lo = split(state)
                w = jnp.concatenate([heads[n], fixed[min(n, 1)][h]], axis=0)[:, :112]
                mixed = dot(w, jnp.concatenate([hi, lo, hi, tops[h]], axis=0))
                state = (
                    mixed[:RANK]
                    + rows[h, 0:1, :] * mixed[RANK : 2 * RANK]
                    + rows[h, 1:2, :] * mixed[2 * RANK : 3 * RANK]
                    + rows[h, 2:3, :] * mixed[3 * RANK :]
                )
            new[:, pl.ds(start, HALF)] = state
            sh, sl = split(stacked(state, rows, h))
            lh, ll = sh[:RANK], sl[:RANK]
            t = dot_t(jnp.concatenate([lh, ll, aux[h]], axis=0), sh)
            t2 = dot_t(jnp.concatenate([lh, aux[h]], axis=0), sl)
            t_main = t[:RANK] + t[RANK : 2 * RANK] + t2[:RANK]
            cross_part = dot_t(jnp.concatenate([lh, ll], axis=0), raw_hi)
            cross = cross + cross_part[:RANK] + cross_part[RANK:] + dot_t(lh, raw_lo)
            a = t[2 * RANK : 2 * RANK + 8]
            a2 = t2[RANK : RANK + 8]
            row8 = sublanes((8, 128))
            a = a + jnp.where(row8 < 2, a2, 0.0)
            ones_sum = ones_sum + jnp.where(row8 == 0, a, a * g1)
            sums[h] = sums[h] + t_main
            y = y + u * t_main
        return sums[0], sums[1], y, cross, ones_sum

    zero = jnp.zeros((RANK, 128), f32)
    first, second, y, cross, ones_sum = lax.fori_loop(
        0, Q1, body, (zero, zero, zero, jnp.zeros((RANK, RANK), f32), jnp.zeros((8, 128), f32))
    )
    cross = jnp.concatenate([jnp.zeros((RANK, 96), f32), cross], axis=1)
    tile_a, tile_b = point_tiles(first, second, y, v_ref[0] >= 4, cross)
    out[:RANK, :128] = tile_a
    out[:RANK, 128:] = tile_b
    out[RANK:, :128] = ones_sum
    out[RANK:, 128:] = jnp.zeros((8, 128), f32)


def evolve_point(v, wl, src, values):
    return call(
        evolve_point_kernel, [(values.shape, f32), ((RANK + 8, 256), f32)], "ssvvvv",
        (v, SPEEDS, ROWS, wl, src, values), name="evolve_point",
    )


CHUNK = 512


def evolve_space_kernel(wk, values, below3, below1, above3, rates, rates_below, rates_above, new, out, raw_hi, raw_lo, rates_all, ch, cl, *bufs):
    rates_all[: (LOW - 1) * NY, :] = rates_below[...]
    rates_all[(LOW - 1) * NY : (LOW - 1 + OWN) * NY, :] = rates[...]
    rates_all[(LOW - 1 + OWN) * NY :, :] = rates_above[...]
    sets = [bufs[0:6], bufs[6:12]]

    def store(dst, t, y, block, rolled):
        hi, lo, mh, ml, ph, plo = dst
        at = pl.multiple_of(t * PAD + (y + 1) * NZ, 128)
        a, b = split(block)
        hi[:, pl.ds(at, NZ)] = a
        lo[:, pl.ds(at, NZ)] = b
        if y == 0:
            other = pl.multiple_of(t * PAD + (NY + 1) * NZ, 128)
            hi[:, pl.ds(other, NZ)] = a
            lo[:, pl.ds(other, NZ)] = b
        if y == NY - 1:
            other = pl.multiple_of(t * PAD, 128)
            hi[:, pl.ds(other, NZ)] = a
            lo[:, pl.ds(other, NZ)] = b
        if rolled:
            c, d = split(roll_lanes(block, 1))
            mh[:, pl.ds(at, NZ)] = c
            ml[:, pl.ds(at, NZ)] = d
        if rolled == 2:
            c, d = split(roll_lanes(block, -1))
            ph[:, pl.ds(at, NZ)] = c
            plo[:, pl.ds(at, NZ)] = d
        return a, b

    def fill(source, planes, first, keep):
        def load(p, carry):
            for y in range(NY):
                block = source[pl.ds(p * NY + y, RANK, stride=planes * NY), :]
                a, b = store(sets[0], p + first, y, block, 2)
                if keep:
                    at = pl.multiple_of(p * PLANE + y * NZ, 128)
                    raw_hi[:, pl.ds(at, NZ)] = a
                    raw_lo[:, pl.ds(at, NZ)] = b
            return carry

        lax.fori_loop(0, planes, load, 0)

    fill(below3, LOW - 1, 0, False)
    fill(below1, 1, LOW - 1, False)
    fill(values, OWN, LOW, True)
    fill(above3, HIGH, LOW + OWN, False)

    for n in range(SUB):
        whi, wlo = split(wk[min(n, 1)])
        wboth = jnp.concatenate([whi, wlo], axis=0)
        src, dst = sets[n % 2], sets[(n + 1) % 2]
        final = n == SUB - 1

        def step(t, carry, src=src, dst=dst, whi=whi, wboth=wboth, final=final):
            for c in range(PLANE // CHUNK):
                at = pl.multiple_of(t * PAD + NZ + c * CHUNK, 128)

                def stack(main, minus, plus):
                    return jnp.concatenate(
                        [
                            main[:, pl.ds(at, CHUNK)],
                            main[:, pl.ds(pl.multiple_of(at - PAD, 128), CHUNK)],
                            main[:, pl.ds(pl.multiple_of(at + PAD, 128), CHUNK)],
                            main[:, pl.ds(pl.multiple_of(at - NZ, 128), CHUNK)],
                            main[:, pl.ds(pl.multiple_of(at + NZ, 128), CHUNK)],
                            minus[:, pl.ds(at, CHUNK)],
                            plus[:, pl.ds(at, CHUNK)],
                        ],
                        axis=0,
                    )

                mixed = dot(wboth, stack(src[0], src[2], src[4]))
                mixed = mixed[:64] + mixed[64:] + dot(whi, stack(src[1], src[3], src[5]))
                for i in range(CHUNK // NZ):
                    y = c * (CHUNK // NZ) + i
                    cell = slice(i * NZ, (i + 1) * NZ)
                    rate = rates_all[pl.ds((t - 1) * NY + y, 1), :]
                    block = mixed[:RANK, cell] + rate * mixed[RANK:, cell]
                    store(dst, t, y, block, 1 if final else 2)
                    if final:
                        spot = pl.multiple_of((t - LOW + 1) * PLANE + y * NZ, 128)
                        new[:, pl.ds(spot, NZ)] = block
                        a, b = split(block * rate)
                        ch[:, pl.ds(spot, NZ)] = a
                        cl[:, pl.ds(spot, NZ)] = b
            return carry

        lax.fori_loop(1 + n, WIDE - 1 - n, step, 0)

    done = sets[SUB % 2]

    def body(p, carry):
        t, c = carry
        at = pl.multiple_of((p + LOW) * PAD + NZ, 128)
        own = pl.multiple_of(p * PLANE, 128)
        spot = pl.multiple_of((p + 1) * PLANE, 128)

        def stack(main, minus):
            return jnp.concatenate(
                [
                    main[:, pl.ds(at, PLANE)],
                    main[:, pl.ds(pl.multiple_of(at - PAD, 128), PLANE)],
                    main[:, pl.ds(pl.multiple_of(at - NZ, 128), PLANE)],
                    minus[:, pl.ds(at, PLANE)],
                ],
                axis=0,
            )

        sh, sl = stack(done[0], done[2]), stack(done[1], done[3])
        both = jnp.concatenate([sh[:RANK], sl[:RANK]], axis=0)
        part = dot_t(both, sh)
        t = t + part[:RANK] + part[RANK:] + dot_t(sh[:RANK], sl)
        oh = jnp.concatenate([ch[:, pl.ds(spot, PLANE)], raw_hi[:, pl.ds(own, PLANE)]], axis=0)
        ol = jnp.concatenate([cl[:, pl.ds(spot, PLANE)], raw_lo[:, pl.ds(own, PLANE)]], axis=0)
        part = dot_t(both, oh)
        c = c + part[:RANK] + part[RANK:] + dot_t(sh[:RANK], ol)
        return t, c

    t, c = lax.fori_loop(0, OWN, body, (jnp.zeros((RANK, 128), f32), jnp.zeros((RANK, 64), f32)))
    out[:, :128] = t
    out[:, 128:] = jnp.concatenate([c, jnp.zeros((RANK, 64), f32)], axis=1)


def evolve_space(wk, values, below3, below1, above3, rates, rates_below, rates_above):
    return call(
        evolve_space_kernel, [((RANK, (OWN + 1) * PLANE), f32), ((RANK, 256), f32)], "vvvvvvvv",
        (wk, values, below3, below1, above3, rates, rates_below, rates_above),
        [pltpu.VMEM((RANK, OWN * PLANE), bf16)] * 2
        + [pltpu.VMEM(((WIDE - 2) * NY, NZ), f32)]
        + [pltpu.VMEM((RANK, (OWN + 1) * PLANE), bf16)] * 2
        + [pltpu.VMEM((RANK, WIDE * PAD), bf16)] * 12,
        name="evolve_space",
    )


def finish_kernel(cells_total, points_total, space, point, core, kinetic, spread, fresh_space, fresh_core, fresh_point):
    s = space[...] * (1.0 / cells_total)
    gram = s[:, 0:32]
    gram_v, plus, minus, cross_v = point_blocks(point[:RANK, :], points_total)
    (_, inverse), (_, inverse_v) = factor_pair(gram, gram_v)
    zeros = jnp.zeros((RANK, 32), f32)
    lane = lanes((RANK, 128))

    def wide(matrix):
        w = jnp.concatenate([matrix] * 3 + [zeros], axis=1)
        hi = w.astype(bf16).astype(f32)
        return jnp.where((lane >= 64) & (lane < 96), w - hi, hi).astype(bf16)[:, :96]

    w_space, w_point = wide(inverse), wide(inverse_v)

    def out_space(p, carry):
        for half in range(2):
            size = PLANE // 2
            at = pl.multiple_of((p + 1) * PLANE + half * size, 128)
            hi, lo = split(kinetic[:, pl.ds(at, size)])
            made = dot(w_space, jnp.concatenate([hi, lo, hi], axis=0))
            for y in range(NY // 2):
                fresh_space[pl.ds(p * NY + half * (NY // 2) + y, RANK, stride=OWN * NY), :] = made[:, y * NZ : (y + 1) * NZ]
        return carry

    lax.fori_loop(0, OWN, out_space, 0)

    def out_point(i, carry):
        at = pl.multiple_of(i * HALF, 128)
        hi, lo = split(spread[:, pl.ds(at, HALF)])
        fresh_point[:, pl.ds(at, HALF)] = dot(w_point, jnp.concatenate([hi, lo, hi], axis=0))
        return carry

    lax.fori_loop(0, 2 * Q1, out_point, 0)

    inverse_t = transposed(inverse)
    inverse_vt = transposed(inverse_v)
    aux = mm(point[RANK:, 0:32] * (1.0 / points_total), inverse_vt)
    weights_row = aux[0:1, :]
    moments_row = aux[1:2, :] + aux[2:3, :]
    raw_a = [gram - s[:, 32 * (d + 1) : 32 * (d + 2)] for d in range(3)]
    space_half = mm(jnp.concatenate(raw_a + [s[:, 128:160]], axis=0), inverse_t)
    a = [mm(inverse, space_half[d * RANK : (d + 1) * RANK]) for d in range(4)]
    e = a[3]
    a_t = [transposed(a[d]) for d in range(3)]
    flux = congruent(inverse_v, plus + minus)
    left = mm(inverse, s[:, 160:192])
    right = mm(inverse_v, cross_v)
    current = mm_t(mm(left, core[...]), right)
    for _ in range(SUB):
        scaled = mm(e, current)
        change = -scaled + jnp.sum(scaled * weights_row, axis=1, keepdims=True) * moments_row
        for d in range(3):
            change = change - mm(mm(a[d], current), flux[d]) + mm(mm(a_t[d], current), flux[d + 3])
        current = current + change
    fresh_core[...] = current


def finish(space, point, core, kinetic, spread, cells_total, points_total):
    def kernel(*refs):
        finish_kernel(cells_total, points_total, *refs)

    return call(
        kernel, [((RANK * OWN * NY, NZ), f32), ((RANK, RANK), f32), (spread.shape, f32)], "vvvvv",
        (space, point, core, kinetic, spread), name="finish",
    )


def axis_sum(values, axis, routes):
    moved = [lax.ppermute(values, axis, route) for route in routes]
    if len(moved) == 1:
        return values + moved[0]
    return (values + moved[1]) + (moved[0] + moved[2])


def routes_x():
    return [[(4 * y + x, 4 * y + (x + d) % 4) for y in range(4) for x in range(4)] for d in (1, 2, 3)]


def routes_y():
    return [[(4 * y + x, 4 * ((y + d) % 4) + x) for y in range(4) for x in range(4)] for d in (1, 2, 3)]


def routes_z():
    return [[(2 * z + c, 2 * ((z + d) % 4) + c) for z in range(4) for c in range(2)] for d in (1, 2, 3)]


def routes_core():
    return [[(2 * z + c, 2 * z + 1 - c) for z in range(4) for c in range(2)]]


def total(space_part, point_part):
    space_part = axis_sum(space_part, "space", routes_x())
    point_part = axis_sum(point_part, "vel", routes_z())
    space_part = axis_sum(space_part, "space", routes_y())
    point_part = axis_sum(point_part, "vel", routes_core())
    return space_part, point_part


def per_device(space_factor, core_matrix, velocity_factor, collision_rates):
    devices = lax.axis_size("space")
    up = [(i, (i + 1) % devices) for i in range(devices)]
    down = [((i + 1) % devices, i) for i in range(devices)]
    below1 = lax.ppermute(space_factor[:, OWN - 1 :], "space", up).reshape(-1, NZ)
    below3 = lax.ppermute(space_factor[:, : OWN - 1], "space", up).reshape(-1, NZ)
    above3 = lax.ppermute(space_factor[:, :HIGH], "space", down).reshape(-1, NZ)
    rates_below = lax.ppermute(collision_rates[1:], "space", up).reshape(-1, NZ)
    rates_above = lax.ppermute(collision_rates[: HIGH - 1], "space", down).reshape(-1, NZ)
    rates = collision_rates.reshape(-1, NZ)
    values = space_factor.reshape(-1, NZ)
    cells_total = OWN * PLANE * devices
    points_total = velocity_factor.shape[1] * lax.axis_size("vel")
    v = lax.axis_index("vel").astype(jnp.int32).reshape(1)

    point = point_sums(v, velocity_factor)
    space = space_sums(values, below1, rates)
    space, point = total(space, point)
    wk, wl, src = small_first(space, point, core_matrix, cells_total, points_total)
    spread, point = evolve_point(v, wl, src, velocity_factor)
    kinetic, space = evolve_space(wk, values, below3, below1, above3, rates, rates_below, rates_above)
    space, point = total(space, point)
    fresh_space, fresh_core, fresh_point = finish(
        space, point, core_matrix, kinetic, spread, cells_total, points_total
    )
    return fresh_space.reshape(space_factor.shape), fresh_core, fresh_point


def solution(mesh):
    return jax.shard_map(
        per_device,
        mesh=mesh,
        in_specs=(P(None, "space", None, None), P(), P(None, "vel"), P("space", None, None)),
        out_specs=(P(None, "space", None, None), P(), P(None, "vel")),
        check_vma=False,
    )
```

```python
import jax
import jax.numpy as jnp
import numpy as np
from jax import lax
from jax.experimental import pallas as pl
from jax.experimental.pallas import tpu as pltpu
from jax.sharding import PartitionSpec as P

RANK = 32
NVD = 48
SUB = 3
LOW = SUB + 1
HIGH = SUB
NY = 16
NZ = 128
OWN = 4
Q1 = 6
HALF = NVD * NVD // 2
PLANE = NY * NZ
PAD = PLANE + 2 * NZ
WIDE = LOW + OWN + HIGH
INTERPRET = False

f32 = jnp.float32
bf16 = jnp.bfloat16
highest = lax.Precision.HIGHEST


def tables():
    t = np.float32(0.25) * ((2 * np.arange(NVD) + 1).astype(np.float32) / np.float32(NVD) - np.float32(1.0))
    t = t.astype(np.float32)
    shape = np.exp(-(t.astype(np.float64) ** 2) / (2.0 * 0.125 * 0.125))
    shape = shape / shape.mean()
    plus, minus = np.maximum(t, 0), np.minimum(t, 0)
    u2, u3 = np.repeat(t, NVD), np.tile(t, NVD)
    g23 = np.repeat(shape, NVD) * np.tile(shape, NVD)
    sides = [(1, "p"), (2, "p"), (3, "p"), (1, "m"), (2, "m"), (3, "m")]
    names = [()] + [(s,) for s in sides]
    where = {(): 0}
    for k in range(6):
        where[(k,)] = k + 1
    for j in range(6):
        for k in range(j, 6):
            if k != j and sides[j][0] == sides[k][0]:
                continue
            where[(j, k)] = len(names)
            names.append((sides[j], sides[k]))
    base = np.zeros((2, 32, HALF))
    scale = np.zeros((NVD, 128))
    value = {"p": np.maximum, "m": np.minimum}
    for row, name in enumerate(names):
        b = np.ones(NVD * NVD)
        c = np.ones(NVD)
        for d, sign in name:
            if d == 1:
                c = c * value[sign](t.astype(np.float64), 0)
            elif d == 2:
                b = b * value[sign](u2.astype(np.float64), 0)
            else:
                b = b * value[sign](u3.astype(np.float64), 0)
        base[:, row] = b.reshape(2, HALF)
        scale[:, row] = c
    last = len(names)
    base[:, last] = g23.reshape(2, HALF)
    scale[:, last] = shape
    select = np.zeros((32, 7 * 128), np.float32)
    for j in range(7):
        for k in range(7):
            pair = tuple(sorted([i - 1 for i in (j, k) if i > 0]))
            if pair in where:
                select[where[pair], j * 128 + k] = 1.0
    means = np.zeros((8, 128), np.float32)
    means[:, 0] = 1.0
    means[:, 1:4] = (shape * plus).mean()
    means[:, 4:7] = (shape * minus).mean()
    rows = np.zeros((2, 8, HALF), np.float32)
    rows[:, 0] = u2.reshape(2, HALF)
    rows[:, 1] = np.maximum(u3, 0).reshape(2, HALF)
    rows[:, 2] = np.minimum(u3, 0).reshape(2, HALF)
    rows[:, 3] = g23.reshape(2, HALF)
    speeds = np.concatenate([plus, minus, shape]).astype(np.float32)
    return rows, base.astype(np.float32), scale.astype(np.float32), select, means, speeds, last


ROWS, PHI, PHI_SCALE, SELECT, MEANS, SPEEDS, LAST = tables()


def split(x):
    hi = x.astype(bf16)
    return hi, (x - hi.astype(f32)).astype(bf16)


def dot(a, b):
    return jnp.dot(a, b, preferred_element_type=f32)


def dot_t(a, b):
    return lax.dot_general(a, b, (((1,), (1,)), ((), ())), preferred_element_type=f32)


def mm(a, b):
    return jnp.dot(a, b, precision=highest, preferred_element_type=f32)


def mm_t(a, b):
    return lax.dot_general(a, b, (((1,), (1,)), ((), ())), precision=highest, preferred_element_type=f32)


def lanes(shape):
    return lax.broadcasted_iota(jnp.int32, shape, len(shape) - 1)


def sublanes(shape):
    return lax.broadcasted_iota(jnp.int32, shape, len(shape) - 2)


def eye():
    return (lanes((RANK, RANK)) == sublanes((RANK, RANK))).astype(f32)


def call(kernel, outs, ins, args, scratch=(), name=None):
    spaces = {"v": pltpu.VMEM, "s": pltpu.SMEM, "a": pl.ANY}
    return pl.pallas_call(
        kernel,
        out_shape=[jax.ShapeDtypeStruct(s, d) for s, d in outs],
        in_specs=[pl.BlockSpec(memory_space=spaces[c]) for c in ins],
        out_specs=[pl.BlockSpec(memory_space=pltpu.VMEM) for _ in outs],
        scratch_shapes=list(scratch),
        compiler_params=pltpu.CompilerParams(vmem_limit_bytes=58 * 1024 * 1024),
        interpret=INTERPRET,
        name=name,
    )(*args)


def point_tiles(first, second, y, positive, extra):
    lane = lanes((RANK, 128))
    middle = (lane >= 32) & (lane < 64)
    tile_a = first + jnp.where(middle, 0.0, second)
    y = jnp.where(lane < 32, y, 0.0)
    y = jnp.where(positive, pltpu.roll(y, 64, 1) if not INTERPRET else jnp.roll(y, 64, 1), y)
    return tile_a, jnp.where(middle, second, 0.0) + y + extra


def roll_lanes(x, shift):
    return jnp.roll(x, shift, 1) if INTERPRET else pltpu.roll(x, shift % x.shape[1], 1)


def stacked(values, rows, h):
    return jnp.concatenate(
        [values, values * rows[h, 0:1, :], values * rows[h, 1:2, :], values * rows[h, 2:3, :]], axis=0
    )


def point_sums_kernel(v_ref, speeds, rows, phi, scale, values, after, out):
    q0 = v_ref[0] * Q1
    phi_parts = [split(phi[h]) for h in range(2)]

    def body(b, carry):
        sums, y, moments = list(carry[:2]), carry[2], carry[3]
        u = speeds[q0 + b] + speeds[NVD + q0 + b]
        for h in range(2):
            start = pl.multiple_of(b * (2 * HALF) + h * HALF, 128)
            sh, sl = split(stacked(values[:, pl.ds(start, HALF)], rows, h))
            lh, ll = sh[:RANK], sl[:RANK]
            ph, plo = phi_parts[h]
            both = jnp.concatenate([lh, ll], axis=0)
            t = dot_t(both, sh)
            t = t[:RANK] + t[RANK:] + dot_t(lh, sl)
            m = dot_t(both, ph)
            m = m[:RANK] + m[RANK:] + dot_t(lh, plo)
            sums[h] = sums[h] + t
            y = y + u * t
            moments = moments + m * scale[pl.ds(q0 + b, 1), :RANK]
        return sums[0], sums[1], y, moments

    zero = jnp.zeros((RANK, 128), f32)
    first, second, y, moments = lax.fori_loop(0, Q1, body, (zero, zero, zero, jnp.zeros((RANK, RANK), f32)))
    moments = jnp.concatenate([jnp.zeros((RANK, 96), f32), moments], axis=1)
    tile_a, tile_b = point_tiles(first, second, y, v_ref[0] >= 4, moments)
    out[:, :128] = tile_a
    out[:, 128:] = tile_b


def point_sums(v, values, after):
    return call(
        point_sums_kernel, [((RANK, 256), f32)], "ssvvvva",
        (v, SPEEDS, ROWS, PHI, PHI_SCALE, values, after), name="point_sums",
    )[0]


def space_sums_kernel(values, rates, out, hi, lo, zh, zl, ch, cl):
    def load(p, carry):
        for y in range(NY):
            block = values[pl.ds(p * NY + y, RANK, stride=OWN * NY), :]
            at = pl.multiple_of(p * PLANE + y * NZ, 128)
            a, b = split(block)
            hi[:, pl.ds(at + PLANE, NZ)] = a
            lo[:, pl.ds(at + PLANE, NZ)] = b
            a, b = split(roll_lanes(block, 1))
            zh[:, pl.ds(at, NZ)] = a
            zl[:, pl.ds(at, NZ)] = b
            a, b = split(block * rates[pl.ds(p * NY + y, 1), :])
            ch[:, pl.ds(at, NZ)] = a
            cl[:, pl.ds(at, NZ)] = b
        return carry

    hi[:, :PLANE] = jnp.zeros((RANK, PLANE), bf16)
    lo[:, :PLANE] = jnp.zeros((RANK, PLANE), bf16)
    lax.fori_loop(0, OWN, load, 0)

    def body(p, carry):
        t, c = carry
        at = pl.multiple_of(p * PLANE, 128)

        def stack(main, turned):
            here = main[:, pl.ds(at + PLANE, PLANE)]
            wrapped = jnp.concatenate([here[:, PLANE - NZ :], here[:, : PLANE - NZ]], axis=1)
            return jnp.concatenate(
                [here, main[:, pl.ds(at, PLANE)], wrapped, turned[:, pl.ds(at, PLANE)]], axis=0
            )

        sh, sl = stack(hi, zh), stack(lo, zl)
        both = jnp.concatenate([sh[:RANK], sl[:RANK]], axis=0)
        part = dot_t(both, sh)
        t = t + part[:RANK] + part[RANK:] + dot_t(sh[:RANK], sl)
        part = dot_t(both, ch[:, pl.ds(at, PLANE)])
        c = c + part[:RANK] + part[RANK:] + dot_t(sh[:RANK], cl[:, pl.ds(at, PLANE)])
        return t, c

    t, c = lax.fori_loop(0, OWN, body, (jnp.zeros((RANK, 128), f32), jnp.zeros((RANK, RANK), f32)))
    out[:, :128] = t
    out[:, 128:] = jnp.concatenate([c, jnp.zeros((RANK, 96), f32)], axis=1)


def space_sums(values, rates):
    own = (RANK, OWN * PLANE)
    return call(
        space_sums_kernel, [((RANK, 256), f32)], "vv", (values, rates),
        [pltpu.VMEM((RANK, (OWN + 1) * PLANE), bf16)] * 2 + [pltpu.VMEM(own, bf16)] * 4, name="space_sums",
    )[0]


def edge_sums_kernel(values, below, inner, out):
    t = jnp.zeros((RANK, 64), f32)
    empty = jnp.zeros((RANK, PLANE), bf16)
    first = jnp.concatenate([values[pl.ds(y, RANK, stride=OWN * NY), :] for y in range(NY)], axis=1)
    other = jnp.concatenate([below[pl.ds(y, RANK, stride=NY), :] for y in range(NY)], axis=1)
    lh, ll = split(first)
    oh, ol = split(other)
    part = dot_t(jnp.concatenate([lh, ll], axis=0), jnp.concatenate([empty, oh], axis=0))
    t = part[:RANK] + part[RANK:] + dot_t(lh, jnp.concatenate([empty, ol], axis=0))
    out[:, :128] = inner[:, :128] + jnp.concatenate([t, jnp.zeros((RANK, 64), f32)], axis=1)
    out[:, 128:] = inner[:, 128:]


def edge_sums(values, below, inner):
    return call(edge_sums_kernel, [((RANK, 256), f32)], "vvv", (values, below, inner), name="edge_sums")[0]


def factor_pair(first, second):
    zeros = jnp.zeros((RANK, 64), f32)
    works = [jnp.concatenate([g, eye(), zeros], axis=1) for g in (first, second)]
    pivots = [jnp.ones((RANK, 128), f32)] * 2
    row = sublanes((RANK, 128))
    for k in range(0, RANK, 2):
        for n in range(2):
            w = works[n]
            c0 = jnp.broadcast_to(w[:, k : k + 1], (RANK, 128))
            c1 = jnp.broadcast_to(w[:, k + 1 : k + 2], (RANK, 128))
            r0, r1 = w[k : k + 1, :], w[k + 1 : k + 2, :]
            a, b, d = c0[k : k + 1, :], c1[k : k + 1, :], c1[k + 1 : k + 2, :]
            over = 1.0 / a
            ratio = b * over
            d = d - b * ratio
            r1 = r1 - ratio * r0
            c1 = c1 - ratio * c0
            step = w - c0 * (r0 * over) - c1 * (r1 * (1.0 / d))
            works[n] = jnp.where(row > k + 1, step, jnp.where(row == k + 1, r1, w))
            pivots[n] = jnp.where(row == k, a, jnp.where(row == k + 1, d, pivots[n]))
    done = [works[n] * lax.rsqrt(pivots[n]) for n in range(2)]
    return [(w[:, :RANK], w[:, RANK : 2 * RANK]) for w in done]


def transposed(x):
    return mm_t(eye(), x)


def point_blocks(tiles, points_total):
    t = tiles * (1.0 / points_total)
    gram = t[:, 0:32]
    plus = [t[:, 192:224], t[:, 160:192], t[:, 64:96]]
    minus = [t[:, 128:160], t[:, 32:64], t[:, 96:128]]
    return gram, plus, minus, t[:, 224:256]


def congruent(inverse, blocks):
    inverse_t = transposed(inverse)
    half = mm(jnp.concatenate(blocks, axis=0), inverse_t)
    return [mm(inverse, half[k * RANK : (k + 1) * RANK]) for k in range(len(blocks))]


def four(parts):
    return (parts[0][...] + parts[2][...]) + (parts[1][...] + parts[3][...])


def small_first_kernel(cells_total, points_total, p0, p1, p2, p3, core, select, means, after, wk, wl, src):
    both = four((p0, p1, p2, p3))
    s = both[:RANK] * (1.0 / cells_total)
    gram = s[:, 0:32]
    gram_v, plus, minus, raw = point_blocks(both[RANK:], points_total)
    (upper, inverse), (upper_v, inverse_v) = factor_pair(gram, gram_v)
    identity = eye()
    raw_a = [gram - s[:, 32 * (d + 1) : 32 * (d + 2)] for d in range(3)]
    to_spread = mm(upper, core[...])
    to_kinetic_t = mm_t(core[...], upper_v)
    zeros = jnp.zeros((RANK, 32), f32)
    inverse_t = transposed(inverse)
    triple = jnp.concatenate([inverse_t] * 3 + [zeros], axis=1)
    left = (
        [mm(inverse, s[:, 128:160])] + [mm(inverse, a) for a in raw_a] + [mm_t(inverse, a) for a in raw_a]
    )
    turned = mm(jnp.concatenate(left, axis=0), triple)
    one = jnp.concatenate([identity] * 3 + [zeros], axis=1)
    e_wide = turned[:RANK]
    mixers = [one - e_wide] + [-turned[RANK * (d + 1) : RANK * (d + 2)] for d in range(3)]
    mixers = mixers + [turned[RANK * (d + 4) : RANK * (d + 5)] for d in range(3)]
    stack = jnp.concatenate(mixers, axis=0)
    wl[1] = stack
    wl[0] = mm(stack[:, :RANK], jnp.concatenate([to_spread] * 3 + [zeros], axis=1))
    square = [m[:, :RANK] for m in mixers]
    e = e_wide[:, :RANK]
    moved = mm(mm(to_spread, raw), select[...])
    groups = [moved[:, 128 * j : 128 * (j + 1)] for j in range(7)]
    lane = lanes((RANK, 128))
    source = [mm(e, groups[0])[:, 0:1]]
    following = mm(square[0], groups[0]) + source[0] * means[0:1, :]
    for j in range(1, 7):
        following = following + mm(square[j], groups[j])
    source.append(mm(e, following)[:, 0:1])
    third = mm(square[0], jnp.where(lane == 0, following, 0.0))
    for j in range(1, 7):
        third = third + mm(square[j], jnp.where(lane == j, following, 0.0))
    third = jnp.sum(third, axis=1, keepdims=True) + source[1] * means[0:1, 0:1]
    source.append(mm(e, jnp.broadcast_to(third, (RANK, 128)))[:, 0:1])
    for n in range(3):
        src[n] = jnp.where((lane >= 96) & (lane < 99), source[n], 0.0)
    flux = congruent(inverse_v, plus + minus)
    turned_raw = mm(inverse_v, raw)
    weights = turned_raw[:, 0:1]
    moments_row = transposed(turned_raw)[LAST : LAST + 1, :]
    center = identity
    blocks = []
    for d in range(3):
        center = center - flux[d] + flux[d + 3]
        blocks += [flux[d], -flux[d + 3]]
    blocks = [center] + blocks
    relax_t = weights * moments_row - identity
    empty = jnp.zeros((RANK, 6 * RANK), f32)
    for kind in range(2):
        if kind == 0:
            parts = [mm(to_kinetic_t, block) for block in blocks]
            relax = mm(to_kinetic_t, relax_t)
        else:
            parts, relax = blocks, relax_t
        wk[kind, :RANK, :] = transposed(jnp.concatenate(parts, axis=0))
        wk[kind, RANK:, :] = jnp.concatenate([transposed(relax), empty], axis=1)


def small_first(parts, core, after, cells_total, points_total):
    def kernel(*refs):
        small_first_kernel(cells_total, points_total, *refs)

    return call(
        kernel, [((2, 64, 224), f32), ((2, 224, 128), f32), ((3, RANK, 128), f32)], "vvvvvvva",
        (*parts, core, SELECT, MEANS, after), name="small_first",
    )


def evolve_point_kernel(v_ref, speeds, rows, wl, src, values, after, new, out):
    q0 = v_ref[0] * Q1
    lane_w = lanes((RANK, 128))
    low_lane = ((lane_w >= 64) & (lane_w < 96)) | (lane_w == 97)

    def weights_of(w):
        hi = w.astype(bf16).astype(f32)
        return jnp.where(low_lane, w - hi, hi).astype(bf16)

    def piece(kind, n):
        return wl[kind, n * RANK : (n + 1) * RANK, :]

    fixed = [
        [jnp.concatenate([weights_of(piece(kind, n)) for n in ((5, 3, 6) if h == 0 else (2, 3, 6))], axis=0) for h in range(2)]
        for kind in range(2)
    ]
    tops = []
    aux = []
    for h in range(2):
        gh, gl = split(rows[h, 3:4, :])
        row = sublanes((16, HALF))
        gh, gl = gh.astype(f32), gl.astype(f32)
        tops.append(jnp.where(row < 2, gh, jnp.where(row == 2, gl, 0.0)).astype(bf16))
        aux.append(jnp.where(row == 0, 1.0, jnp.where(row == 1, gh, jnp.where(row == 2, gl, 0.0))).astype(bf16))

    def body(b, carry):
        sums, y, cross, ones_sum = list(carry[:2]), carry[2], carry[3], carry[4]
        up = speeds[q0 + b]
        um = speeds[NVD + q0 + b]
        g1 = speeds[2 * NVD + q0 + b]
        u = up + um
        moving = [piece(kind, 0) + up * piece(kind, 1) + um * piece(kind, 4) for kind in range(2)]
        heads = [weights_of(moving[min(n, 1)] + g1 * src[n]) for n in range(3)]
        for h in range(2):
            start = pl.multiple_of(b * (2 * HALF) + h * HALF, 128)
            state = values[:, pl.ds(start, HALF)]
            raw_hi, raw_lo = split(state)
            hi, lo = raw_hi, raw_lo
            for n in range(SUB):
                if n > 0:
                    hi, lo = split(state)
                w = jnp.concatenate([heads[n], fixed[min(n, 1)][h]], axis=0)[:, :112]
                mixed = dot(w, jnp.concatenate([hi, lo, hi, tops[h]], axis=0))
                state = (
                    mixed[:RANK]
                    + rows[h, 0:1, :] * mixed[RANK : 2 * RANK]
                    + rows[h, 1:2, :] * mixed[2 * RANK : 3 * RANK]
                    + rows[h, 2:3, :] * mixed[3 * RANK :]
                )
            new[:, pl.ds(start, HALF)] = state
            sh, sl = split(stacked(state, rows, h))
            lh, ll = sh[:RANK], sl[:RANK]
            t = dot_t(jnp.concatenate([lh, ll, aux[h]], axis=0), sh)
            t2 = dot_t(jnp.concatenate([lh, aux[h]], axis=0), sl)
            t_main = t[:RANK] + t[RANK : 2 * RANK] + t2[:RANK]
            cross_part = dot_t(jnp.concatenate([lh, ll], axis=0), raw_hi)
            cross = cross + cross_part[:RANK] + cross_part[RANK:] + dot_t(lh, raw_lo)
            a = t[2 * RANK : 2 * RANK + 8]
            a2 = t2[RANK : RANK + 8]
            row8 = sublanes((8, 128))
            a = a + jnp.where(row8 < 2, a2, 0.0)
            ones_sum = ones_sum + jnp.where(row8 == 0, a, a * g1)
            sums[h] = sums[h] + t_main
            y = y + u * t_main
        return sums[0], sums[1], y, cross, ones_sum

    zero = jnp.zeros((RANK, 128), f32)
    first, second, y, cross, ones_sum = lax.fori_loop(
        0, Q1, body, (zero, zero, zero, jnp.zeros((RANK, RANK), f32), jnp.zeros((8, 128), f32))
    )
    cross = jnp.concatenate([jnp.zeros((RANK, 96), f32), cross], axis=1)
    tile_a, tile_b = point_tiles(first, second, y, v_ref[0] >= 4, cross)
    out[:RANK, :128] = tile_a
    out[:RANK, 128:] = tile_b
    out[RANK:, :128] = ones_sum
    out[RANK:, 128:] = jnp.zeros((8, 128), f32)


def evolve_point(v, wl, src, values, after):
    return call(
        evolve_point_kernel, [(values.shape, f32), ((RANK + 8, 256), f32)], "ssvvvva",
        (v, SPEEDS, ROWS, wl, src, values, after), name="evolve_point",
    )


CHUNK = 512


def store(dst, t, y, block, rolled):
    hi, lo, mh, ml, ph, plo = dst
    at = pl.multiple_of(t * PAD + (y + 1) * NZ, 128)
    a, b = split(block)
    hi[:, pl.ds(at, NZ)] = a
    lo[:, pl.ds(at, NZ)] = b
    if y == 0:
        other = pl.multiple_of(t * PAD + (NY + 1) * NZ, 128)
        hi[:, pl.ds(other, NZ)] = a
        lo[:, pl.ds(other, NZ)] = b
    if y == NY - 1:
        other = pl.multiple_of(t * PAD, 128)
        hi[:, pl.ds(other, NZ)] = a
        lo[:, pl.ds(other, NZ)] = b
    if rolled:
        c, d = split(roll_lanes(block, 1))
        mh[:, pl.ds(at, NZ)] = c
        ml[:, pl.ds(at, NZ)] = d
    if rolled == 2:
        c, d = split(roll_lanes(block, -1))
        ph[:, pl.ds(at, NZ)] = c
        plo[:, pl.ds(at, NZ)] = d


def fill_kernel(values, below3, below1, above3, after, *dst):
    def fill(source, planes, first):
        def load(p, carry):
            for y in range(NY):
                store(dst, p + first, y, source[pl.ds(p * NY + y, RANK, stride=planes * NY), :], 2)
            return carry

        lax.fori_loop(0, planes, load, 0)

    fill(below3, LOW - 1, 0)
    fill(below1, 1, LOW - 1)
    fill(values, OWN, LOW)
    fill(above3, HIGH, LOW + OWN)


def fill_planes(values, below3, below1, above3, after):
    return call(
        fill_kernel, [((RANK, WIDE * PAD), bf16)] * 6, "vvvva", (values, below3, below1, above3, after), name="fill_planes",
    )


def evolve_space_kernel(wk, *refs):
    raw = refs[0:6]
    rates, rates_below, rates_above, new, out, rates_all, ch, cl = refs[6:14]
    sets = [raw, refs[14:20], refs[20:26]]
    order = [0, 1, 2, 1]
    rates_all[: (LOW - 1) * NY, :] = rates_below[RANK * (LOW - 1) * NY :, :]
    rates_all[(LOW - 1) * NY : (LOW - 1 + OWN) * NY, :] = rates[...]
    rates_all[(LOW - 1 + OWN) * NY :, :] = rates_above[RANK * HIGH * NY : RANK * HIGH * NY + (HIGH - 1) * NY, :]

    for n in range(SUB):
        whi, wlo = split(wk[min(n, 1)])
        wboth = jnp.concatenate([whi, wlo], axis=0)
        src, dst = sets[order[n]], sets[order[n + 1]]
        final = n == SUB - 1

        def step(t, carry, src=src, dst=dst, whi=whi, wboth=wboth, final=final):
            for c in range(PLANE // CHUNK):
                at = pl.multiple_of(t * PAD + NZ + c * CHUNK, 128)

                def stack(main, minus, plus):
                    return jnp.concatenate(
                        [
                            main[:, pl.ds(at, CHUNK)],
                            main[:, pl.ds(pl.multiple_of(at - PAD, 128), CHUNK)],
                            main[:, pl.ds(pl.multiple_of(at + PAD, 128), CHUNK)],
                            main[:, pl.ds(pl.multiple_of(at - NZ, 128), CHUNK)],
                            main[:, pl.ds(pl.multiple_of(at + NZ, 128), CHUNK)],
                            minus[:, pl.ds(at, CHUNK)],
                            plus[:, pl.ds(at, CHUNK)],
                        ],
                        axis=0,
                    )

                mixed = dot(wboth, stack(src[0], src[2], src[4]))
                mixed = mixed[:64] + mixed[64:] + dot(whi, stack(src[1], src[3], src[5]))
                for i in range(CHUNK // NZ):
                    y = c * (CHUNK // NZ) + i
                    cell = slice(i * NZ, (i + 1) * NZ)
                    rate = rates_all[pl.ds((t - 1) * NY + y, 1), :]
                    block = mixed[:RANK, cell] + rate * mixed[RANK:, cell]
                    store(dst, t, y, block, 1 if final else 2)
                    if final:
                        spot = pl.multiple_of((t - LOW + 1) * PLANE + y * NZ, 128)
                        new[:, pl.ds(spot, NZ)] = block
                        a, b = split(block * rate)
                        ch[:, pl.ds(spot, NZ)] = a
                        cl[:, pl.ds(spot, NZ)] = b
            return carry

        lax.fori_loop(1 + n, WIDE - 1 - n, step, 0)

    done = sets[order[SUB]]

    def body(p, carry):
        t, c = carry
        at = pl.multiple_of((p + LOW) * PAD + NZ, 128)
        spot = pl.multiple_of((p + 1) * PLANE, 128)

        def stack(main, minus):
            return jnp.concatenate(
                [
                    main[:, pl.ds(at, PLANE)],
                    main[:, pl.ds(pl.multiple_of(at - PAD, 128), PLANE)],
                    main[:, pl.ds(pl.multiple_of(at - NZ, 128), PLANE)],
                    minus[:, pl.ds(at, PLANE)],
                ],
                axis=0,
            )

        sh, sl = stack(done[0], done[2]), stack(done[1], done[3])
        both = jnp.concatenate([sh[:RANK], sl[:RANK]], axis=0)
        part = dot_t(both, sh)
        t = t + part[:RANK] + part[RANK:] + dot_t(sh[:RANK], sl)
        oh = jnp.concatenate([ch[:, pl.ds(spot, PLANE)], raw[0][:, pl.ds(at, PLANE)]], axis=0)
        ol = jnp.concatenate([cl[:, pl.ds(spot, PLANE)], raw[1][:, pl.ds(at, PLANE)]], axis=0)
        part = dot_t(both, oh)
        c = c + part[:RANK] + part[RANK:] + dot_t(sh[:RANK], ol)
        return t, c

    t, c = lax.fori_loop(0, OWN, body, (jnp.zeros((RANK, 128), f32), jnp.zeros((RANK, 64), f32)))
    out[:, :128] = t
    out[:, 128:] = jnp.concatenate([c, jnp.zeros((RANK, 64), f32)], axis=1)


def evolve_space(wk, filled, rates, rates_below, rates_above):
    return call(
        evolve_space_kernel, [((RANK, (OWN + 1) * PLANE), f32), ((RANK, 256), f32)], "v" * 10,
        (wk, *filled, rates, rates_below, rates_above),
        [pltpu.VMEM(((WIDE - 2) * NY, NZ), f32)]
        + [pltpu.VMEM((RANK, (OWN + 1) * PLANE), bf16)] * 2
        + [pltpu.VMEM((RANK, WIDE * PAD), bf16)] * 12,
        name="evolve_space",
    )


def finish_kernel(cells_total, points_total, p0, p1, p2, p3, core, kinetic, spread, fresh_space, fresh_core, fresh_point):
    both = four((p0, p1, p2, p3))
    s = both[:RANK] * (1.0 / cells_total)
    gram = s[:, 0:32]
    gram_v, plus, minus, cross_v = point_blocks(both[RANK : 2 * RANK], points_total)
    (_, inverse), (_, inverse_v) = factor_pair(gram, gram_v)
    zeros = jnp.zeros((RANK, 32), f32)
    lane = lanes((RANK, 128))

    def wide(matrix):
        w = jnp.concatenate([matrix] * 3 + [zeros], axis=1)
        hi = w.astype(bf16).astype(f32)
        return jnp.where((lane >= 64) & (lane < 96), w - hi, hi).astype(bf16)[:, :96]

    w_space, w_point = wide(inverse), wide(inverse_v)

    def out_space(p, carry):
        for half in range(2):
            size = PLANE // 2
            at = pl.multiple_of((p + 1) * PLANE + half * size, 128)
            hi, lo = split(kinetic[:, pl.ds(at, size)])
            made = dot(w_space, jnp.concatenate([hi, lo, hi], axis=0))
            for y in range(NY // 2):
                fresh_space[pl.ds(p * NY + half * (NY // 2) + y, RANK, stride=OWN * NY), :] = made[:, y * NZ : (y + 1) * NZ]
        return carry

    lax.fori_loop(0, OWN, out_space, 0)

    def out_point(i, carry):
        at = pl.multiple_of(i * HALF, 128)
        hi, lo = split(spread[:, pl.ds(at, HALF)])
        fresh_point[:, pl.ds(at, HALF)] = dot(w_point, jnp.concatenate([hi, lo, hi], axis=0))
        return carry

    lax.fori_loop(0, 2 * Q1, out_point, 0)

    inverse_t = transposed(inverse)
    inverse_vt = transposed(inverse_v)
    aux = mm(both[2 * RANK :, 0:32] * (1.0 / points_total), inverse_vt)
    weights_row = aux[0:1, :]
    moments_row = aux[1:2, :] + aux[2:3, :]
    raw_a = [gram - s[:, 32 * (d + 1) : 32 * (d + 2)] for d in range(3)]
    space_half = mm(jnp.concatenate(raw_a + [s[:, 128:160]], axis=0), inverse_t)
    a = [mm(inverse, space_half[d * RANK : (d + 1) * RANK]) for d in range(4)]
    e = a[3]
    a_t = [transposed(a[d]) for d in range(3)]
    flux = congruent(inverse_v, plus + minus)
    left = mm(inverse, s[:, 160:192])
    right = mm(inverse_v, cross_v)
    current = mm_t(mm(left, core[...]), right)
    for _ in range(SUB):
        scaled = mm(e, current)
        change = -scaled + jnp.sum(scaled * weights_row, axis=1, keepdims=True) * moments_row
        for d in range(3):
            change = change - mm(mm(a[d], current), flux[d]) + mm(mm(a_t[d], current), flux[d + 3])
        current = current + change
    fresh_core[...] = current


def finish(parts, core, kinetic, spread, cells_total, points_total):
    def kernel(*refs):
        finish_kernel(cells_total, points_total, *refs)

    return call(
        kernel, [((RANK * OWN * NY, NZ), f32), ((RANK, RANK), f32), (spread.shape, f32)], "vvvvvvv",
        (*parts, core, kinetic, spread), name="finish",
    )


def spread_pairs(space_part):
    moved = []
    for k in range(2):
        route = [((s ^ (2 * v + k)) * 8 + v, s * 8 + v) for s in range(16) for v in range(8)]
        moved.append(lax.ppermute(space_part, ("space", "vel"), route))
    return moved


def vel_parts(moved, point_part):
    joint = jnp.concatenate([moved[0] + moved[1], point_part], axis=0)
    pair = [(2 * z + c, 2 * z + 1 - c) for z in range(4) for c in range(2)]
    joint = joint + lax.ppermute(joint, "vel", pair)
    routes = [[(2 * z + c, 2 * ((z + d) % 4) + c) for z in range(4) for c in range(2)] for d in (1, 2, 3)]
    return [joint] + [lax.ppermute(joint, "vel", route) for route in routes]


def per_device(space_factor, core_matrix, velocity_factor, collision_rates):
    devices = lax.axis_size("space")
    up = [(i, (i + 1) % devices) for i in range(devices)]
    down = [((i + 1) % devices, i) for i in range(devices)]
    below1 = lax.ppermute(space_factor[:, OWN - 1 :], "space", up).reshape(-1, NZ)
    lower = jnp.concatenate([space_factor[:, : OWN - 1], collision_rates[None, 1:]], axis=0)
    upper = jnp.concatenate([space_factor[:, :HIGH], collision_rates[None, :HIGH]], axis=0)
    lower = lax.ppermute(lower, "space", up).reshape(-1, NZ)
    upper = lax.ppermute(upper, "space", down).reshape(-1, NZ)
    rates = collision_rates.reshape(-1, NZ)
    values = space_factor.reshape(-1, NZ)
    cells_total = OWN * PLANE * devices
    points_total = velocity_factor.shape[1] * lax.axis_size("vel")
    v = lax.axis_index("vel").astype(jnp.int32).reshape(1)

    inner = space_sums(values, rates)
    space = edge_sums(values, below1, inner)
    moved = spread_pairs(space)
    point = point_sums(v, velocity_factor, space)
    parts = vel_parts(moved, point)
    filled = fill_planes(values, lower, below1, upper, parts[0])
    wk, wl, src = small_first(parts, core_matrix, filled[0], cells_total, points_total)
    kinetic, space = evolve_space(wk, filled, rates, lower, upper)
    moved = spread_pairs(space)
    spread, point = evolve_point(v, wl, src, velocity_factor, space)
    parts = vel_parts(moved, point)
    fresh_space, fresh_core, fresh_point = finish(parts, core_matrix, kinetic, spread, cells_total, points_total)
    return fresh_space.reshape(space_factor.shape), fresh_core, fresh_point


def solution(mesh):
    return jax.shard_map(
        per_device,
        mesh=mesh,
        in_specs=(P(None, "space", None, None), P(), P(None, "vel"), P("space", None, None)),
        out_specs=(P(None, "space", None, None), P(), P(None, "vel")),
        check_vma=False,
    )
```

```python
import jax
import jax.numpy as jnp
import numpy as np
from jax import lax
from jax.experimental import pallas as pl
from jax.experimental.pallas import tpu as pltpu
from jax.sharding import PartitionSpec as P


RANK = 32
NVD = 48
SUB = 3
LOW = SUB + 1
HIGH = SUB
NY = 16
NZ = 128
OWN = 4
Q1 = 6
HALF = NVD * NVD // 2
PLANE = NY * NZ
WIDE = LOW + OWN + HIGH
INTERPRET = False

f32 = jnp.float32
bf16 = jnp.bfloat16
highest = lax.Precision.HIGHEST


def tables():
    t = np.float32(0.25) * ((2 * np.arange(NVD) + 1).astype(np.float32) / np.float32(NVD) - np.float32(1.0))
    t = t.astype(np.float32)
    shape = np.exp(-(t.astype(np.float64) ** 2) / (2.0 * 0.125 * 0.125))
    shape = shape / shape.mean()
    plus, minus = np.maximum(t, 0), np.minimum(t, 0)
    u2, u3 = np.repeat(t, NVD), np.tile(t, NVD)
    g23 = np.repeat(shape, NVD) * np.tile(shape, NVD)
    sides = [(1, "p"), (2, "p"), (3, "p"), (1, "m"), (2, "m"), (3, "m")]
    names = [()] + [(s,) for s in sides]
    where = {(): 0}
    for k in range(6):
        where[(k,)] = k + 1
    for j in range(6):
        for k in range(j, 6):
            if k != j and sides[j][0] == sides[k][0]:
                continue
            where[(j, k)] = len(names)
            names.append((sides[j], sides[k]))
    base = np.zeros((2, 32, HALF))
    scale = np.zeros((NVD, 128))
    value = {"p": np.maximum, "m": np.minimum}
    for row, name in enumerate(names):
        b = np.ones(NVD * NVD)
        c = np.ones(NVD)
        for d, sign in name:
            if d == 1:
                c = c * value[sign](t.astype(np.float64), 0)
            elif d == 2:
                b = b * value[sign](u2.astype(np.float64), 0)
            else:
                b = b * value[sign](u3.astype(np.float64), 0)
        base[:, row] = b.reshape(2, HALF)
        scale[:, row] = c
    last = len(names)
    base[:, last] = g23.reshape(2, HALF)
    scale[:, last] = shape
    select = np.zeros((32, 7 * 128), np.float32)
    for j in range(7):
        for k in range(7):
            pair = tuple(sorted([i - 1 for i in (j, k) if i > 0]))
            if pair in where:
                select[where[pair], j * 128 + k] = 1.0
    means = np.zeros((8, 128), np.float32)
    means[:, 0] = 1.0
    means[:, 1:4] = (shape * plus).mean()
    means[:, 4:7] = (shape * minus).mean()
    rows = np.zeros((2, 8, HALF), np.float32)
    rows[:, 0] = u2.reshape(2, HALF)
    rows[:, 1] = np.maximum(u3, 0).reshape(2, HALF)
    rows[:, 2] = np.minimum(u3, 0).reshape(2, HALF)
    rows[:, 3] = g23.reshape(2, HALF)
    speeds = np.concatenate([plus, minus, shape]).astype(np.float32)
    return rows, base.astype(np.float32), scale.astype(np.float32), select, means, speeds, last


ROWS, PHI, PHI_SCALE, SELECT, MEANS, SPEEDS, LAST = tables()


def split(x):
    hi = x.astype(bf16)
    return hi, (x - hi.astype(f32)).astype(bf16)


def dot(a, b):
    return jnp.dot(a, b, preferred_element_type=f32)


def dot_t(a, b):
    return lax.dot_general(a, b, (((1,), (1,)), ((), ())), preferred_element_type=f32)


def mm(a, b):
    return jnp.dot(a, b, precision=highest, preferred_element_type=f32)


def mm_t(a, b):
    return lax.dot_general(a, b, (((1,), (1,)), ((), ())), precision=highest, preferred_element_type=f32)


def lanes(shape):
    return lax.broadcasted_iota(jnp.int32, shape, len(shape) - 1)


def sublanes(shape):
    return lax.broadcasted_iota(jnp.int32, shape, len(shape) - 2)


def eye():
    return (lanes((RANK, RANK)) == sublanes((RANK, RANK))).astype(f32)


def call(kernel, outs, ins, args, scratch=(), mib=8):
    spaces = {"v": pltpu.VMEM, "s": pltpu.SMEM, "a": pl.ANY}
    return pl.pallas_call(
        kernel,
        out_shape=[jax.ShapeDtypeStruct(s, d) for s, d in outs],
        in_specs=[pl.BlockSpec(memory_space=spaces[c]) for c in ins],
        out_specs=[pl.BlockSpec(memory_space=pltpu.VMEM) for _ in outs],
        scratch_shapes=list(scratch),
        compiler_params=pltpu.CompilerParams(vmem_limit_bytes=mib * 1024 * 1024),
        interpret=INTERPRET,
    )(*args)


def point_tiles(first, second, y, positive, extra):
    lane = lanes((RANK, 128))
    middle = (lane >= 32) & (lane < 64)
    tile_a = first + jnp.where(middle, 0.0, second)
    y = jnp.where(lane < 32, y, 0.0)
    y = jnp.where(positive, pltpu.roll(y, 64, 1) if not INTERPRET else jnp.roll(y, 64, 1), y)
    return tile_a, jnp.where(middle, second, 0.0) + y + extra


def roll_lanes(x, shift):
    return jnp.roll(x, shift, 1) if INTERPRET else pltpu.roll(x, shift % x.shape[1], 1)


def stacked(values, rows, h):
    return jnp.concatenate(
        [values, values * rows[h, 0:1, :], values * rows[h, 1:2, :], values * rows[h, 2:3, :]], axis=0
    )


def point_sums_kernel(v_ref, speeds, rows, phi, scale, values, after, out):
    q0 = v_ref[0] * Q1
    phi_parts = [split(phi[h]) for h in range(2)]

    def body(b, carry):
        sums, y, moments = list(carry[:2]), carry[2], carry[3]
        u = speeds[q0 + b] + speeds[NVD + q0 + b]
        for h in range(2):
            start = pl.multiple_of(b * (2 * HALF) + h * HALF, 128)
            sh, sl = split(stacked(values[:, pl.ds(start, HALF)], rows, h))
            lh, ll = sh[:RANK], sl[:RANK]
            ph, plo = phi_parts[h]
            both = jnp.concatenate([lh, ll], axis=0)
            t = dot_t(both, sh)
            t = t[:RANK] + t[RANK:] + dot_t(lh, sl)
            m = dot_t(both, ph)
            m = m[:RANK] + m[RANK:] + dot_t(lh, plo)
            sums[h] = sums[h] + t
            y = y + u * t
            moments = moments + m * scale[pl.ds(q0 + b, 1), :RANK]
        return sums[0], sums[1], y, moments

    zero = jnp.zeros((RANK, 128), f32)
    first, second, y, moments = lax.fori_loop(0, Q1, body, (zero, zero, zero, jnp.zeros((RANK, RANK), f32)))
    moments = jnp.concatenate([jnp.zeros((RANK, 96), f32), moments], axis=1)
    tile_a, tile_b = point_tiles(first, second, y, v_ref[0] >= 4, moments)
    out[:, :128] = tile_a
    out[:, 128:] = tile_b


def point_sums(v, values, after):
    return call(
        point_sums_kernel, [((RANK, 256), f32)], "ssvvvva",
        (v, SPEEDS, ROWS, PHI, PHI_SCALE, values, after), mib=12,
    )[0]


def space_sums_kernel(values, rates, out, own_hi, own_lo, hi, lo, zh, zl, ch, cl):
    def load(p, carry):
        for y in range(NY):
            block = values[pl.ds(p * NY + y, RANK, stride=OWN * NY), :]
            at = pl.multiple_of(p * PLANE + y * NZ, 128)
            a, b = split(block)
            hi[:, pl.ds(at + PLANE, NZ)] = a
            lo[:, pl.ds(at + PLANE, NZ)] = b
            own_hi[:, pl.ds(at, NZ)] = a
            own_lo[:, pl.ds(at, NZ)] = b
            a, b = split(roll_lanes(block, 1))
            zh[:, pl.ds(at, NZ)] = a
            zl[:, pl.ds(at, NZ)] = b
            a, b = split(block * rates[pl.ds(p * NY + y, 1), :])
            ch[:, pl.ds(at, NZ)] = a
            cl[:, pl.ds(at, NZ)] = b
        return carry

    hi[:, :PLANE] = jnp.zeros((RANK, PLANE), bf16)
    lo[:, :PLANE] = jnp.zeros((RANK, PLANE), bf16)
    lax.fori_loop(0, OWN, load, 0)

    def body(p, carry):
        t, c = carry
        at = pl.multiple_of(p * PLANE, 128)

        def stack(main, turned):
            here = main[:, pl.ds(at + PLANE, PLANE)]
            wrapped = jnp.concatenate([here[:, PLANE - NZ :], here[:, : PLANE - NZ]], axis=1)
            return jnp.concatenate(
                [here, main[:, pl.ds(at, PLANE)], wrapped, turned[:, pl.ds(at, PLANE)]], axis=0
            )

        sh, sl = stack(hi, zh), stack(lo, zl)
        both = jnp.concatenate([sh[:RANK], sl[:RANK]], axis=0)
        part = dot_t(both, sh)
        t = t + part[:RANK] + part[RANK:] + dot_t(sh[:RANK], sl)
        part = dot_t(both, ch[:, pl.ds(at, PLANE)])
        c = c + part[:RANK] + part[RANK:] + dot_t(sh[:RANK], cl[:, pl.ds(at, PLANE)])
        return t, c

    t, c = lax.fori_loop(0, OWN, body, (jnp.zeros((RANK, 128), f32), jnp.zeros((RANK, RANK), f32)))
    out[:, :128] = t
    out[:, 128:] = jnp.concatenate([c, jnp.zeros((RANK, 96), f32)], axis=1)


def space_sums(values, rates):
    own = (RANK, OWN * PLANE)
    return call(
        space_sums_kernel, [((RANK, 256), f32), (own, bf16), (own, bf16)], "vv", (values, rates),
        [pltpu.VMEM((RANK, (OWN + 1) * PLANE), bf16)] * 2 + [pltpu.VMEM(own, bf16)] * 4, mib=12,
    )


def edge_sums_kernel(own_hi, own_lo, below, inner, out, edge_hi, edge_lo):
    empty = jnp.zeros((RANK, PLANE), bf16)
    oh, ol = split(jnp.concatenate([below[pl.ds(y, RANK, stride=NY), :] for y in range(NY)], axis=1))
    edge_hi[...] = oh
    edge_lo[...] = ol
    lh, ll = own_hi[:, :PLANE], own_lo[:, :PLANE]
    part = dot_t(jnp.concatenate([lh, ll], axis=0), jnp.concatenate([empty, oh], axis=0))
    t = part[:RANK] + part[RANK:] + dot_t(lh, jnp.concatenate([empty, ol], axis=0))
    out[:, :128] = inner[:, :128] + jnp.concatenate([t, jnp.zeros((RANK, 64), f32)], axis=1)
    out[:, 128:] = inner[:, 128:]


def edge_sums(own_hi, own_lo, below, inner):
    plane = ((RANK, PLANE), bf16)
    return call(edge_sums_kernel, [((RANK, 256), f32), plane, plane], "vvvv", (own_hi, own_lo, below, inner))


def factor_pair(first, second):
    zeros = jnp.zeros((RANK, 64), f32)
    works = [jnp.concatenate([g, eye(), zeros], axis=1) for g in (first, second)]
    pivots = [jnp.ones((RANK, 128), f32)] * 2
    row = sublanes((RANK, 128))
    for k in range(0, RANK, 2):
        for n in range(2):
            w = works[n]
            c0 = jnp.broadcast_to(w[:, k : k + 1], (RANK, 128))
            c1 = jnp.broadcast_to(w[:, k + 1 : k + 2], (RANK, 128))
            r0, r1 = w[k : k + 1, :], w[k + 1 : k + 2, :]
            a, b, d = c0[k : k + 1, :], c1[k : k + 1, :], c1[k + 1 : k + 2, :]
            over = 1.0 / a
            ratio = b * over
            d = d - b * ratio
            r1 = r1 - ratio * r0
            c1 = c1 - ratio * c0
            step = w - c0 * (r0 * over) - c1 * (r1 * (1.0 / d))
            works[n] = jnp.where(row > k + 1, step, jnp.where(row == k + 1, r1, w))
            pivots[n] = jnp.where(row == k, a, jnp.where(row == k + 1, d, pivots[n]))
    done = [works[n] * lax.rsqrt(pivots[n]) for n in range(2)]
    return [(w[:, :RANK], w[:, RANK : 2 * RANK]) for w in done]


def transposed(x):
    return mm_t(eye(), x)


def point_blocks(tiles, points_total):
    t = tiles * (1.0 / points_total)
    gram = t[:, 0:32]
    plus = [t[:, 192:224], t[:, 160:192], t[:, 64:96]]
    minus = [t[:, 128:160], t[:, 32:64], t[:, 96:128]]
    return gram, plus, minus, t[:, 224:256]


def congruent(inverse, blocks):
    inverse_t = transposed(inverse)
    half = mm(jnp.concatenate(blocks, axis=0), inverse_t)
    return [mm(inverse, half[k * RANK : (k + 1) * RANK]) for k in range(len(blocks))]


def four(parts):
    return (parts[0][...] + parts[2][...]) + (parts[1][...] + parts[3][...])


def small_first_kernel(cells_total, points_total, p0, p1, p2, p3, core, select, means, after, wk, wl, src):
    both = four((p0, p1, p2, p3))
    s = both[:RANK] * (1.0 / cells_total)
    gram = s[:, 0:32]
    gram_v, _, _, raw = point_blocks(both[RANK:], points_total)
    (upper, inverse), (upper_v, inverse_v) = factor_pair(gram, gram_v)
    identity = eye()
    raw_a = [gram - s[:, 32 * (d + 1) : 32 * (d + 2)] for d in range(3)]
    to_spread = mm(upper, core[...])
    to_kinetic_t = mm_t(core[...], upper_v)
    zeros = jnp.zeros((RANK, 32), f32)
    inverse_t = transposed(inverse)
    triple = jnp.concatenate([inverse_t] * 3 + [zeros], axis=1)
    left = (
        [mm(inverse, s[:, 128:160])] + [mm(inverse, a) for a in raw_a] + [mm_t(inverse, a) for a in raw_a]
    )
    turned = mm(jnp.concatenate(left, axis=0), triple)
    one = jnp.concatenate([identity] * 3 + [zeros], axis=1)
    e_wide = turned[:RANK]
    mixers = [one - e_wide] + [-turned[RANK * (d + 1) : RANK * (d + 2)] for d in range(3)]
    mixers = mixers + [turned[RANK * (d + 4) : RANK * (d + 5)] for d in range(3)]
    stack = jnp.concatenate(mixers, axis=0)
    wl[1] = stack
    wl[0] = mm(stack[:, :RANK], jnp.concatenate([to_spread] * 3 + [zeros], axis=1))
    square = [m[:, :RANK] for m in mixers]
    e = e_wide[:, :RANK]
    moved = mm(mm(to_spread, raw), select[...])
    groups = [moved[:, 128 * j : 128 * (j + 1)] for j in range(7)]
    lane = lanes((RANK, 128))
    source = [mm(e, groups[0])[:, 0:1]]
    following = mm(square[0], groups[0]) + source[0] * means[0:1, :]
    for j in range(1, 7):
        following = following + mm(square[j], groups[j])
    source.append(mm(e, following)[:, 0:1])
    third = mm(square[0], jnp.where(lane == 0, following, 0.0))
    for j in range(1, 7):
        third = third + mm(square[j], jnp.where(lane == j, following, 0.0))
    third = jnp.sum(third, axis=1, keepdims=True) + source[1] * means[0:1, 0:1]
    source.append(mm(e, jnp.broadcast_to(third, (RANK, 128)))[:, 0:1])
    for n in range(3):
        src[n] = jnp.where((lane >= 96) & (lane < 99), source[n], 0.0)
    half = mm(inverse_v, both[RANK:, :] * (1.0 / points_total))
    turned_raw = half[:, 224:256]
    weights_row = transposed(turned_raw)[0:1, :]
    blocks = [half[:, 192:224], half[:, 128:160], half[:, 160:192], half[:, 32:64], half[:, 64:96], half[:, 96:128]]
    flux = mm(jnp.concatenate(blocks, axis=0), transposed(inverse_v))
    flux = [flux[k * RANK : (k + 1) * RANK] * (1.0 if k % 2 == 0 else -1.0) for k in range(6)]
    center = identity
    for block in flux:
        center = center - block
    relax = turned_raw[:, LAST : LAST + 1] * weights_row - identity
    column = jnp.concatenate([center, relax] + flux, axis=0)
    to_kinetic = transposed(to_kinetic_t)
    wk[0] = mm(column, jnp.concatenate([to_kinetic] * 3 + [zeros], axis=1))
    wk[1] = jnp.concatenate([column] * 3 + [jnp.zeros((8 * RANK, 32), f32)], axis=1)


def small_first(parts, core, after, cells_total, points_total):
    def kernel(*refs):
        small_first_kernel(cells_total, points_total, *refs)

    return call(
        kernel, [((2, 8 * RANK, 128), f32), ((2, 224, 128), f32), ((3, RANK, 128), f32)], "vvvvvvva",
        (*parts, core, SELECT, MEANS, after),
    )


def evolve_point_kernel(v_ref, speeds, rows, wl, src, values, after, new, out):
    q0 = v_ref[0] * Q1
    lane_w = lanes((RANK, 128))
    low_lane = ((lane_w >= 64) & (lane_w < 96)) | (lane_w == 97)

    def weights_of(w):
        hi = w.astype(bf16).astype(f32)
        return jnp.where(low_lane, w - hi, hi).astype(bf16)

    def piece(kind, n):
        return wl[kind, n * RANK : (n + 1) * RANK, :]

    fixed = [
        [jnp.concatenate([weights_of(piece(kind, n)) for n in ((5, 3, 6) if h == 0 else (2, 3, 6))], axis=0) for h in range(2)]
        for kind in range(2)
    ]
    tops = []
    aux = []
    for h in range(2):
        gh, gl = split(rows[h, 3:4, :])
        row = sublanes((16, HALF))
        gh, gl = gh.astype(f32), gl.astype(f32)
        tops.append(jnp.where(row < 2, gh, jnp.where(row == 2, gl, 0.0)).astype(bf16))
        aux.append(jnp.where(row == 0, 1.0, jnp.where(row == 1, gh, jnp.where(row == 2, gl, 0.0))).astype(bf16))

    def body(b, carry):
        sums, y, cross, ones_sum = list(carry[:2]), carry[2], carry[3], carry[4]
        up = speeds[q0 + b]
        um = speeds[NVD + q0 + b]
        g1 = speeds[2 * NVD + q0 + b]
        u = up + um
        moving = [piece(kind, 0) + up * piece(kind, 1) + um * piece(kind, 4) for kind in range(2)]
        heads = [weights_of(moving[min(n, 1)] + g1 * src[n]) for n in range(3)]
        for h in range(2):
            start = pl.multiple_of(b * (2 * HALF) + h * HALF, 128)
            state = values[:, pl.ds(start, HALF)]
            raw_hi, raw_lo = split(state)
            hi, lo = raw_hi, raw_lo
            for n in range(SUB):
                if n > 0:
                    hi, lo = split(state)
                w = jnp.concatenate([heads[n], fixed[min(n, 1)][h]], axis=0)[:, :112]
                mixed = dot(w, jnp.concatenate([hi, lo, hi, tops[h]], axis=0))
                state = (
                    mixed[:RANK]
                    + rows[h, 0:1, :] * mixed[RANK : 2 * RANK]
                    + rows[h, 1:2, :] * mixed[2 * RANK : 3 * RANK]
                    + rows[h, 2:3, :] * mixed[3 * RANK :]
                )
            new[:, pl.ds(start, HALF)] = state
            sh, sl = split(stacked(state, rows, h))
            lh, ll = sh[:RANK], sl[:RANK]
            t = dot_t(jnp.concatenate([lh, ll, aux[h]], axis=0), sh)
            t2 = dot_t(jnp.concatenate([lh, aux[h]], axis=0), sl)
            t_main = t[:RANK] + t[RANK : 2 * RANK] + t2[:RANK]
            cross_part = dot_t(jnp.concatenate([lh, ll], axis=0), raw_hi)
            cross = cross + cross_part[:RANK] + cross_part[RANK:] + dot_t(lh, raw_lo)
            a = t[2 * RANK : 2 * RANK + 8]
            a2 = t2[RANK : RANK + 8]
            row8 = sublanes((8, 128))
            a = a + jnp.where(row8 < 2, a2, 0.0)
            ones_sum = ones_sum + jnp.where(row8 == 0, a, a * g1)
            sums[h] = sums[h] + t_main
            y = y + u * t_main
        return sums[0], sums[1], y, cross, ones_sum

    zero = jnp.zeros((RANK, 128), f32)
    first, second, y, cross, ones_sum = lax.fori_loop(
        0, Q1, body, (zero, zero, zero, jnp.zeros((RANK, RANK), f32), jnp.zeros((8, 128), f32))
    )
    cross = jnp.concatenate([jnp.zeros((RANK, 96), f32), cross], axis=1)
    tile_a, tile_b = point_tiles(first, second, y, v_ref[0] >= 4, cross)
    out[:RANK, :128] = tile_a
    out[:RANK, 128:] = tile_b
    out[RANK:, :128] = ones_sum
    out[RANK:, 128:] = jnp.zeros((8, 128), f32)


def evolve_point(v, wl, src, values, after):
    return call(
        evolve_point_kernel, [(values.shape, f32), ((RANK + 8, 256), f32)], "ssvvvva",
        (v, SPEEDS, ROWS, wl, src, values, after), mib=16,
    )


RATES = (LOW - 1 + OWN + HIGH - 1) * NY
HALO = RANK * HIGH * NY


def fill_kernel(v_ref, own_hi, own_lo, edge_hi, edge_lo, mine, other, after, hi, lo, rates_low, rates_high):
    core = v_ref[0] % 2
    hi[:, LOW * PLANE : (LOW + OWN) * PLANE] = own_hi[...]
    lo[:, LOW * PLANE : (LOW + OWN) * PLANE] = own_lo[...]
    hi[:, (LOW - 1) * PLANE : LOW * PLANE] = edge_hi[...]
    lo[:, (LOW - 1) * PLANE : LOW * PLANE] = edge_lo[...]
    for source, place in ((mine, core), (other, 1 - core)):

        def load(p, carry, source=source, place=place):
            for y in range(NY):
                a, b = split(source[pl.ds(p * NY + y, RANK, stride=HIGH * NY), :])
                at = pl.multiple_of((p + place * (LOW + OWN)) * PLANE + y * NZ, 128)
                hi[:, pl.ds(at, NZ)] = a
                lo[:, pl.ds(at, NZ)] = b
            return carry

        lax.fori_loop(0, HIGH, load, 0)
    first, second = mine[HALO:, :], other[HALO:, :]
    rates_low[...] = jnp.where(core == 0, first, second)
    rates_high[...] = jnp.where(core == 0, second, first)


def fill_planes(v, own, edge, mine, other, after):
    wide = ((RANK, WIDE * PLANE), bf16)
    part = ((HIGH * NY, NZ), f32)
    return call(fill_kernel, [wide, wide, part, part], "svvvvvva", (v, *own, *edge, mine, other, after), mib=12)


def evolve_space_kernel(wk, raw_hi, raw_lo, rates, rates_low, rates_high, new, out, rates_all, partial, passed, *bufs):
    sets = [(raw_hi, raw_lo), bufs[0:2], bufs[2:4]]
    order = [0, 1, 2, 1]
    low, own = (LOW - 1) * NY, OWN * NY
    rates_all[:low, :] = rates_low[...]
    rates_all[low : low + own, :] = rates[...]
    rates_all[low + own :, :] = rates_high[: (HIGH - 1) * NY, :]
    lane = lanes((8 * RANK, 128))
    low_lane = (lane >= 64) & (lane < 96)

    for n in range(SUB):
        w = wk[min(n, 1)]
        w_hi = w.astype(bf16).astype(f32)
        w = jnp.where(low_lane, w - w_hi, w_hi).astype(bf16)[:, :96]
        src, dst = sets[order[n]], sets[order[n + 1]]
        final = n == SUB - 1
        begin, end = 1 + n, WIDE - 1 - n

        def tile(t, j, src=src):
            at = pl.multiple_of(t * PLANE + j * 256, 256)
            a, b = src[0][:, pl.ds(at, 256)], src[1][:, pl.ds(at, 256)]
            return jnp.concatenate([a, b, a], axis=0)

        def put(t, y, block, dst=dst, final=final):
            at = pl.multiple_of(t * PLANE + y * NZ, 128)
            a, b = split(block)
            dst[0][:, pl.ds(at, NZ)] = a
            dst[1][:, pl.ds(at, NZ)] = b
            if final:
                new[:, pl.ds(pl.multiple_of((t - 2) * PLANE + y * NZ, 128), NZ)] = block

        def step(t, carry, w=w, tile=tile, put=put):
            held = None
            first = None
            for j in range(NY // 2):
                mixed = dot(w, tile(t, j))
                for i in range(2):
                    y = 2 * j + i
                    cell = slice(y * NZ, (y + 1) * NZ)
                    part = [mixed[k * RANK : (k + 1) * RANK, i * NZ : (i + 1) * NZ] for k in range(8)]
                    put(t - 1, y, partial[:, cell] + part[3])
                    base = part[0] + rates_all[pl.ds((t - 1) * NY + y, 1), :] * part[1] + passed[:, cell]
                    passed[:, cell] = part[2]
                    base = base + roll_lanes(part[6], 1) + roll_lanes(part[7], -1)
                    if y == 0:
                        first = (base, part[5])
                    elif y == 1:
                        held_base = base + held[1]
                    else:
                        partial[:, (y - 1) * NZ : y * NZ] = held[0] + part[5]
                        held_base = base + held[1]
                    if y == 1:
                        first = (first[0] + part[5], first[1])
                    held = (held_base if y > 0 else base, part[4])
            partial[:, (NY - 1) * NZ :] = held[0] + first[1]
            partial[:, :NZ] = first[0] + held[1]
            return carry

        for j in range(NY // 2):
            passed[:, j * 256 : (j + 1) * 256] = dot(w[2 * RANK : 3 * RANK], tile(begin - 1, j))
        lax.fori_loop(begin, end, step, 0)
        for j in range(NY // 2):
            mixed = dot(w[3 * RANK : 4 * RANK], tile(end, j))
            for i in range(2):
                y = 2 * j + i
                put(end - 1, y, partial[:, y * NZ : (y + 1) * NZ] + mixed[:, i * NZ : (i + 1) * NZ])

    done = sets[order[SUB]]

    def body(p, carry):
        t, c = carry
        at = pl.multiple_of((p + LOW) * PLANE, 128)
        turned, relaxed = [], []
        for y in range(NY):
            block = new[:, pl.ds(pl.multiple_of((p + 2) * PLANE + y * NZ, 128), NZ)]
            turned.append(split(roll_lanes(block, 1)))
            relaxed.append(split(block * rates[pl.ds(p * NY + y, 1), :]))

        def stacks(k):
            here = done[k][:, pl.ds(at, PLANE)]
            wrapped = jnp.concatenate([here[:, PLANE - NZ :], here[:, : PLANE - NZ]], axis=1)
            behind = done[k][:, pl.ds(pl.multiple_of(at - PLANE, 128), PLANE)]
            rolled = jnp.concatenate([block[k] for block in turned], axis=1)
            scaled = jnp.concatenate([block[k] for block in relaxed], axis=1)
            old = (raw_hi, raw_lo)[k][:, pl.ds(at, PLANE)]
            return jnp.concatenate([here, behind, wrapped, rolled], axis=0), jnp.concatenate([scaled, old], axis=0)

        (sh, oh), (sl, ol) = stacks(0), stacks(1)
        both = jnp.concatenate([sh[:RANK], sl[:RANK]], axis=0)
        part = dot_t(both, sh)
        t = t + part[:RANK] + part[RANK:] + dot_t(sh[:RANK], sl)
        part = dot_t(both, oh)
        c = c + part[:RANK] + part[RANK:] + dot_t(sh[:RANK], ol)
        return t, c

    t, c = lax.fori_loop(0, OWN, body, (jnp.zeros((RANK, 128), f32), jnp.zeros((RANK, 64), f32)))
    out[:, :128] = t
    out[:, 128:] = jnp.concatenate([c, jnp.zeros((RANK, 64), f32)], axis=1)


def evolve_space(wk, filled, rates):
    return call(
        evolve_space_kernel, [((RANK, (OWN + 2) * PLANE), f32), ((RANK, 256), f32)], "v" * 6,
        (wk, filled[0], filled[1], rates, filled[2], filled[3]),
        [pltpu.VMEM((RATES, NZ), f32)]
        + [pltpu.VMEM((RANK, PLANE), f32)] * 2
        + [pltpu.VMEM((RANK, WIDE * PLANE), bf16)] * 4,
        mib=16,
    )


def finish_kernel(cells_total, points_total, p0, p1, p2, p3, core, kinetic, spread, fresh_space, fresh_core, fresh_point):
    both = four((p0, p1, p2, p3))
    s = both[:RANK] * (1.0 / cells_total)
    gram = s[:, 0:32]
    gram_v, plus, minus, cross_v = point_blocks(both[RANK : 2 * RANK], points_total)
    (_, inverse), (_, inverse_v) = factor_pair(gram, gram_v)
    zeros = jnp.zeros((RANK, 32), f32)
    lane = lanes((RANK, 128))

    def wide(matrix):
        w = jnp.concatenate([matrix] * 3 + [zeros], axis=1)
        hi = w.astype(bf16).astype(f32)
        return jnp.where((lane >= 64) & (lane < 96), w - hi, hi).astype(bf16)[:, :96]

    w_space, w_point = wide(inverse), wide(inverse_v)

    def out_space(p, carry):
        for half in range(2):
            size = PLANE // 2
            at = pl.multiple_of((p + 2) * PLANE + half * size, 128)
            hi, lo = split(kinetic[:, pl.ds(at, size)])
            made = dot(w_space, jnp.concatenate([hi, lo, hi], axis=0))
            for y in range(NY // 2):
                fresh_space[pl.ds(p * NY + half * (NY // 2) + y, RANK, stride=OWN * NY), :] = made[:, y * NZ : (y + 1) * NZ]
        return carry

    lax.fori_loop(0, OWN, out_space, 0)

    def out_point(i, carry):
        at = pl.multiple_of(i * HALF, 128)
        hi, lo = split(spread[:, pl.ds(at, HALF)])
        fresh_point[:, pl.ds(at, HALF)] = dot(w_point, jnp.concatenate([hi, lo, hi], axis=0))
        return carry

    lax.fori_loop(0, 2 * Q1, out_point, 0)

    inverse_t = transposed(inverse)
    inverse_vt = transposed(inverse_v)
    aux = mm(both[2 * RANK :, 0:32] * (1.0 / points_total), inverse_vt)
    weights_row = aux[0:1, :]
    moments_row = aux[1:2, :] + aux[2:3, :]
    raw_a = [gram - s[:, 32 * (d + 1) : 32 * (d + 2)] for d in range(3)]
    space_half = mm(jnp.concatenate(raw_a + [s[:, 128:160]], axis=0), inverse_t)
    a = [mm(inverse, space_half[d * RANK : (d + 1) * RANK]) for d in range(4)]
    e = a[3]
    a_t = [transposed(a[d]) for d in range(3)]
    flux = congruent(inverse_v, plus + minus)
    left = mm(inverse, s[:, 160:192])
    right = mm(inverse_v, cross_v)
    current = mm_t(mm(left, core[...]), right)
    for _ in range(SUB):
        scaled = mm(e, current)
        change = -scaled + jnp.sum(scaled * weights_row, axis=1, keepdims=True) * moments_row
        for d in range(3):
            change = change - mm(mm(a[d], current), flux[d]) + mm(mm(a_t[d], current), flux[d + 3])
        current = current + change
    fresh_core[...] = current


def finish(parts, core, kinetic, spread, cells_total, points_total):
    def kernel(*refs):
        finish_kernel(cells_total, points_total, *refs)

    return call(
        kernel, [((RANK * OWN * NY, NZ), f32), ((RANK, RANK), f32), (spread.shape, f32)], "vvvvvvv",
        (*parts, core, kinetic, spread), mib=12,
    )


def spread_pairs(space_part):
    moved = []
    for k in range(2):
        route = [((s ^ (2 * v + k)) * 8 + v, s * 8 + v) for s in range(16) for v in range(8)]
        moved.append(lax.ppermute(space_part, ("space", "vel"), route))
    return moved


def vel_parts(moved, point_part):
    joint = jnp.concatenate([moved[0] + moved[1], point_part], axis=0)
    pair = [(2 * z + c, 2 * z + 1 - c) for z in range(4) for c in range(2)]
    joint = joint + lax.ppermute(joint, "vel", pair)
    routes = [[(2 * z + c, 2 * ((z + d) % 4) + c) for z in range(4) for c in range(2)] for d in (1, 2, 3)]
    return [joint] + [lax.ppermute(joint, "vel", route) for route in routes]


def per_device(space_factor, core_matrix, velocity_factor, collision_rates):
    devices = lax.axis_size("space")
    up = [(i, (i + 1) % devices) for i in range(devices)]
    below1 = lax.ppermute(space_factor[:, OWN - 1 :], "space", up).reshape(-1, NZ)
    rates = collision_rates.reshape(-1, NZ)
    values = space_factor.reshape(-1, NZ)
    cells_total = OWN * PLANE * devices
    points_total = velocity_factor.shape[1] * lax.axis_size("vel")
    place = lax.axis_index("vel").astype(jnp.int32)
    v = place.reshape(1)
    planes = jnp.where(place % 2 == 0, space_factor[:, : OWN - 1], space_factor[:, :HIGH])
    lines = jnp.where(place % 2 == 0, collision_rates[1:], collision_rates[:HIGH])
    halo = jnp.concatenate([planes, lines[None]], axis=0)
    route = [(s * 8 + w, (s + 1 - 2 * (w % 2)) % devices * 8 + w) for s in range(devices) for w in range(8)]
    pair = [(w, w ^ 1) for w in range(8)]

    inner, own_hi, own_lo = space_sums(values, rates)
    halo, inner = lax.optimization_barrier((halo, inner))
    mine = lax.ppermute(halo, ("space", "vel"), route)
    space, *edge = edge_sums(own_hi, own_lo, below1, inner)
    moved = spread_pairs(space)
    point = point_sums(v, velocity_factor, space)
    mine, point = lax.optimization_barrier((mine, point))
    other = lax.ppermute(mine, "vel", pair)
    parts = vel_parts(moved, point)
    filled = fill_planes(v, (own_hi, own_lo), edge, mine.reshape(-1, NZ), other.reshape(-1, NZ), parts[0])
    wk, wl, src = small_first(parts, core_matrix, filled[0], cells_total, points_total)
    kinetic, space = evolve_space(wk, filled, rates)
    moved = spread_pairs(space)
    spread, point = evolve_point(v, wl, src, velocity_factor, space)
    parts = vel_parts(moved, point)
    fresh_space, fresh_core, fresh_point = finish(parts, core_matrix, kinetic, spread, cells_total, points_total)
    return fresh_space.reshape(space_factor.shape), fresh_core, fresh_point


def solution(mesh):
    return jax.shard_map(
        per_device,
        mesh=mesh,
        in_specs=(P(None, "space", None, None), P(), P(None, "vel"), P("space", None, None)),
        out_specs=(P(None, "space", None, None), P(), P(None, "vel")),
        check_vma=False,
    )
```

```python
import jax
import jax.numpy as jnp
import numpy as np
from jax import lax
from jax.experimental import pallas as pl
from jax.experimental.pallas import tpu as pltpu
from jax.sharding import PartitionSpec as P


RANK = 32
NVD = 48
SUB = 3
LOW = SUB + 1
HIGH = SUB
NY = 16
NZ = 128
OWN = 4
Q1 = 6
HALF = NVD * NVD // 2
PLANE = NY * NZ
WIDE = LOW + OWN + HIGH
ROWS_K = 7 * RANK + 16
INTERPRET = False

f32 = jnp.float32
bf16 = jnp.bfloat16


def tables():
    t = np.float32(0.25) * ((2 * np.arange(NVD) + 1).astype(np.float32) / np.float32(NVD) - np.float32(1.0))
    t = t.astype(np.float32)
    shape = np.exp(-(t.astype(np.float64) ** 2) / (2.0 * 0.125 * 0.125))
    shape = shape / shape.mean()
    plus, minus = np.maximum(t, 0), np.minimum(t, 0)
    u2, u3 = np.repeat(t, NVD), np.tile(t, NVD)
    g23 = np.repeat(shape, NVD) * np.tile(shape, NVD)
    sides = [(1, "p"), (2, "p"), (3, "p"), (1, "m"), (2, "m"), (3, "m")]
    names = [()] + [(s,) for s in sides]
    where = {(): 0}
    for k in range(6):
        where[(k,)] = k + 1
    for j in range(6):
        for k in range(j, 6):
            if k != j and sides[j][0] == sides[k][0]:
                continue
            where[(j, k)] = len(names)
            names.append((sides[j], sides[k]))
    base = np.zeros((2, 32, HALF))
    scale = np.zeros((NVD, 128))
    value = {"p": np.maximum, "m": np.minimum}
    for row, name in enumerate(names):
        b = np.ones(NVD * NVD)
        c = np.ones(NVD)
        for d, sign in name:
            if d == 1:
                c = c * value[sign](t.astype(np.float64), 0)
            elif d == 2:
                b = b * value[sign](u2.astype(np.float64), 0)
            else:
                b = b * value[sign](u3.astype(np.float64), 0)
        base[:, row] = b.reshape(2, HALF)
        scale[:, row] = c
    last = len(names)
    base[:, last] = g23.reshape(2, HALF)
    scale[:, last] = shape
    select = np.zeros((32, 7 * 128), np.float32)
    for j in range(7):
        for k in range(7):
            pair = tuple(sorted([i - 1 for i in (j, k) if i > 0]))
            if pair in where:
                select[where[pair], j * 128 + k] = 1.0
    means = np.zeros((8, 128), np.float32)
    means[:, 0] = 1.0
    means[:, 1:4] = (shape * plus).mean()
    means[:, 4:7] = (shape * minus).mean()
    rows = np.zeros((2, 8, HALF), np.float32)
    rows[:, 0] = u2.reshape(2, HALF)
    rows[:, 1] = np.maximum(u3, 0).reshape(2, HALF)
    rows[:, 2] = np.minimum(u3, 0).reshape(2, HALF)
    rows[:, 3] = g23.reshape(2, HALF)
    speeds = np.concatenate([plus, minus, shape]).astype(np.float32)
    return rows, base.astype(np.float32), scale.astype(np.float32), select, means, speeds, last


ROWS, PHI, PHI_SCALE, SELECT, MEANS, SPEEDS, LAST = tables()


def split(x):
    hi = x.astype(bf16)
    return hi, (x - hi.astype(f32)).astype(bf16)


def dot(a, b):
    return jnp.dot(a, b, preferred_element_type=f32)


def dot_t(a, b):
    return lax.dot_general(a, b, (((1,), (1,)), ((), ())), preferred_element_type=f32)


def mm(a, b, form=dot):
    rows = a.shape[0]
    ah, al = split(a)
    bh, bl = split(b)
    main = form(jnp.concatenate([ah, al], axis=0), bh)
    return main[:rows] + main[rows:] + form(ah, bl)


def mm_t(a, b):
    return mm(a, b, dot_t)


def lanes(shape):
    return lax.broadcasted_iota(jnp.int32, shape, len(shape) - 1)


def sublanes(shape):
    return lax.broadcasted_iota(jnp.int32, shape, len(shape) - 2)


def eye():
    return (lanes((RANK, RANK)) == sublanes((RANK, RANK))).astype(f32)


def call(kernel, outs, ins, args, scratch=(), mib=8, out_spaces=None):
    spaces = {"v": pltpu.VMEM, "s": pltpu.SMEM, "a": pl.ANY}
    out_spaces = out_spaces or "v" * len(outs)
    return pl.pallas_call(
        kernel,
        out_shape=[jax.ShapeDtypeStruct(s, d) for s, d in outs],
        in_specs=[pl.BlockSpec(memory_space=spaces[c]) for c in ins],
        out_specs=[pl.BlockSpec(memory_space=spaces[c]) for c in out_spaces],
        scratch_shapes=list(scratch),
        compiler_params=pltpu.CompilerParams(vmem_limit_bytes=mib * 1024 * 1024),
        interpret=INTERPRET,
    )(*args)


def point_tiles(first, second, y, positive, extra):
    lane = lanes((RANK, 128))
    middle = (lane >= 32) & (lane < 64)
    tile_a = first + jnp.where(middle, 0.0, second)
    y = jnp.where(lane < 32, y, 0.0)
    y = jnp.where(positive, pltpu.roll(y, 64, 1) if not INTERPRET else jnp.roll(y, 64, 1), y)
    return tile_a, jnp.where(middle, second, 0.0) + y + extra


def roll_lanes(x, shift):
    return jnp.roll(x, shift, 1) if INTERPRET else pltpu.roll(x, shift % x.shape[1], 1)


def stacked(values, rows, h):
    return jnp.concatenate(
        [values, values * rows[h, 0:1, :], values * rows[h, 1:2, :], values * rows[h, 2:3, :]], axis=0
    )


def point_sums_kernel(v_ref, speeds, rows, phi, scale, values, after, out):
    q0 = v_ref[0] * Q1
    phi_parts = [split(phi[h]) for h in range(2)]

    def body(b, carry):
        sums, y, moments = list(carry[:2]), carry[2], carry[3]
        u = speeds[q0 + b] + speeds[NVD + q0 + b]
        for h in range(2):
            start = pl.multiple_of(b * (2 * HALF) + h * HALF, 128)
            sh, sl = split(stacked(values[:, pl.ds(start, HALF)], rows, h))
            lh, ll = sh[:RANK], sl[:RANK]
            ph, plo = phi_parts[h]
            both = jnp.concatenate([lh, ll], axis=0)
            t = dot_t(both, jnp.concatenate([sh, ph], axis=0))
            t = t[:RANK] + t[RANK:] + dot_t(lh, jnp.concatenate([sl, plo], axis=0))
            t, m = t[:, :128], t[:, 128:]
            sums[h] = sums[h] + t
            y = y + u * t
            moments = moments + m * scale[pl.ds(q0 + b, 1), :RANK]
        return sums[0], sums[1], y, moments

    zero = jnp.zeros((RANK, 128), f32)
    first, second, y, moments = lax.fori_loop(0, Q1, body, (zero, zero, zero, jnp.zeros((RANK, RANK), f32)))
    moments = jnp.concatenate([jnp.zeros((RANK, 96), f32), moments], axis=1)
    tile_a, tile_b = point_tiles(first, second, y, v_ref[0] >= 4, moments)
    out[:, :128] = tile_a
    out[:, 128:] = tile_b


def point_sums(v, values, after):
    return call(
        point_sums_kernel, [((RANK, 256), f32)], "ssvvvva",
        (v, SPEEDS, ROWS, PHI, PHI_SCALE, values, after), mib=12,
    )[0]


def space_sums_kernel(values, rates, out, own, hi, lo, zh, zl, ch, cl):
    def load(p, carry):
        for y in range(NY):
            block = values[pl.ds(p * NY + y, RANK, stride=OWN * NY), :]
            at = pl.multiple_of(p * PLANE + y * NZ, 128)
            a, b = split(block)
            hi[:, pl.ds(at + PLANE, NZ)] = a
            lo[:, pl.ds(at + PLANE, NZ)] = b
            own[:, pl.ds(at, NZ)] = block
            a, b = split(roll_lanes(block, 1))
            zh[:, pl.ds(at, NZ)] = a
            zl[:, pl.ds(at, NZ)] = b
            a, b = split(block * rates[pl.ds(p * NY + y, 1), :])
            ch[:, pl.ds(at, NZ)] = a
            cl[:, pl.ds(at, NZ)] = b
        return carry

    hi[:, :PLANE] = jnp.zeros((RANK, PLANE), bf16)
    lo[:, :PLANE] = jnp.zeros((RANK, PLANE), bf16)
    lax.fori_loop(0, OWN, load, 0)

    def body(p, carry):
        t, c = carry
        at = pl.multiple_of(p * PLANE, 128)

        def stack(main, turned):
            here = main[:, pl.ds(at + PLANE, PLANE)]
            wrapped = jnp.concatenate([here[:, PLANE - NZ :], here[:, : PLANE - NZ]], axis=1)
            return jnp.concatenate(
                [here, main[:, pl.ds(at, PLANE)], wrapped, turned[:, pl.ds(at, PLANE)]], axis=0
            )

        sh, sl = stack(hi, zh), stack(lo, zl)
        both = jnp.concatenate([sh[:RANK], sl[:RANK]], axis=0)
        part = dot_t(both, jnp.concatenate([sh, ch[:, pl.ds(at, PLANE)]], axis=0))
        part = part[:RANK] + part[RANK:] + dot_t(sh[:RANK], jnp.concatenate([sl, cl[:, pl.ds(at, PLANE)]], axis=0))
        return t + part[:, :128], c + part[:, 128:]

    t, c = lax.fori_loop(0, OWN, body, (jnp.zeros((RANK, 128), f32), jnp.zeros((RANK, RANK), f32)))
    out[:, :128] = t
    out[:, 128:] = jnp.concatenate([c, jnp.zeros((RANK, 96), f32)], axis=1)


def space_sums(values, rates):
    own = (RANK, OWN * PLANE)
    return call(
        space_sums_kernel, [((RANK, 256), f32), (own, f32)], "vv", (values, rates),
        [pltpu.VMEM((RANK, (OWN + 1) * PLANE), bf16)] * 2 + [pltpu.VMEM(own, bf16)] * 4, mib=12,
    )


def edge_sums_kernel(own, below, inner, out, edge):
    empty = jnp.zeros((RANK, PLANE), bf16)
    other = jnp.concatenate([below[pl.ds(y, RANK, stride=NY), :] for y in range(NY)], axis=1)
    edge[...] = other
    oh, ol = split(other)
    lh, ll = split(own[:, :PLANE])
    part = dot_t(jnp.concatenate([lh, ll], axis=0), jnp.concatenate([empty, oh], axis=0))
    t = part[:RANK] + part[RANK:] + dot_t(lh, jnp.concatenate([empty, ol], axis=0))
    out[:, :128] = inner[:, :128] + jnp.concatenate([t, jnp.zeros((RANK, 64), f32)], axis=1)
    out[:, 128:] = inner[:, 128:]


def edge_sums(own, below, inner):
    return call(edge_sums_kernel, [((RANK, 256), f32), ((RANK, PLANE), f32)], "vvv", (own, below, inner))


def factor_pair(first, second):
    zeros = jnp.zeros((RANK, 64), f32)
    works = [jnp.concatenate([g, eye(), zeros], axis=1) for g in (first, second)]
    pivots = [jnp.ones((RANK, 128), f32)] * 2
    row = sublanes((RANK, 128))
    for k in range(0, RANK, 2):
        for n in range(2):
            w = works[n]
            c0 = jnp.broadcast_to(w[:, k : k + 1], (RANK, 128))
            c1 = jnp.broadcast_to(w[:, k + 1 : k + 2], (RANK, 128))
            r0, r1 = w[k : k + 1, :], w[k + 1 : k + 2, :]
            a, b, d = c0[k : k + 1, :], c1[k : k + 1, :], c1[k + 1 : k + 2, :]
            over = 1.0 / a
            ratio = b * over
            d = d - b * ratio
            r1 = r1 - ratio * r0
            c1 = c1 - ratio * c0
            step = w - c0 * (r0 * over) - c1 * (r1 * (1.0 / d))
            works[n] = jnp.where(row > k + 1, step, jnp.where(row == k + 1, r1, w))
            pivots[n] = jnp.where(row == k, a, jnp.where(row == k + 1, d, pivots[n]))
    done = [works[n] * lax.rsqrt(pivots[n]) for n in range(2)]
    return [(w[:, :RANK], w[:, RANK : 2 * RANK]) for w in done]


def transposed(x):
    return mm_t(eye(), x)


def point_blocks(tiles, points_total):
    t = tiles * (1.0 / points_total)
    gram = t[:, 0:32]
    plus = [t[:, 192:224], t[:, 160:192], t[:, 64:96]]
    minus = [t[:, 128:160], t[:, 32:64], t[:, 96:128]]
    return gram, plus, minus, t[:, 224:256]


def four(parts):
    return (parts[0][...] + parts[2][...]) + (parts[1][...] + parts[3][...])


def small_first_kernel(cells_total, points_total, p0, p1, p2, p3, core, select, means, after, wk, wl, src, moment):
    both = four((p0, p1, p2, p3))
    s = both[:RANK] * (1.0 / cells_total)
    gram = s[:, 0:32]
    gram_v, _, _, raw = point_blocks(both[RANK:], points_total)
    (upper, inverse), (upper_v, inverse_v) = factor_pair(gram, gram_v)
    identity = eye()
    raw_a = [gram - s[:, 32 * (d + 1) : 32 * (d + 2)] for d in range(3)]
    to_spread = mm(upper, core[...])
    to_kinetic_t = mm_t(core[...], upper_v)
    zeros = jnp.zeros((RANK, 32), f32)
    inverse_t = transposed(inverse)
    triple = jnp.concatenate([inverse_t] * 3 + [zeros], axis=1)
    left = (
        [mm(inverse, s[:, 128:160])] + [mm(inverse, a) for a in raw_a] + [mm_t(inverse, a) for a in raw_a]
    )
    turned = mm(jnp.concatenate(left, axis=0), triple)
    one = jnp.concatenate([identity] * 3 + [zeros], axis=1)
    e_wide = turned[:RANK]
    mixers = [one - e_wide] + [-turned[RANK * (d + 1) : RANK * (d + 2)] for d in range(3)]
    mixers = mixers + [turned[RANK * (d + 4) : RANK * (d + 5)] for d in range(3)]
    stack = jnp.concatenate(mixers, axis=0)
    wl[1] = stack
    wl[0] = mm(stack[:, :RANK], jnp.concatenate([to_spread] * 3 + [zeros], axis=1))
    square = [m[:, :RANK] for m in mixers]
    e = e_wide[:, :RANK]
    moved = mm(mm(to_spread, raw), select[...])
    groups = [moved[:, 128 * j : 128 * (j + 1)] for j in range(7)]
    lane = lanes((RANK, 128))
    source = [mm(e, groups[0])[:, 0:1]]
    following = mm(square[0], groups[0]) + source[0] * means[0:1, :]
    for j in range(1, 7):
        following = following + mm(square[j], groups[j])
    source.append(mm(e, following)[:, 0:1])
    third = mm(square[0], jnp.where(lane == 0, following, 0.0))
    for j in range(1, 7):
        third = third + mm(square[j], jnp.where(lane == j, following, 0.0))
    third = jnp.sum(third, axis=1, keepdims=True) + source[1] * means[0:1, 0:1]
    source.append(mm(e, jnp.broadcast_to(third, (RANK, 128)))[:, 0:1])
    for n in range(3):
        src[n] = jnp.where((lane >= 96) & (lane < 99), source[n], 0.0)
    half = mm(inverse_v, both[RANK:, :] * (1.0 / points_total))
    turned_raw = half[:, 224:256]
    weights_row = transposed(turned_raw)[0:1, :]
    blocks = [half[:, 192:224], half[:, 128:160], half[:, 160:192], half[:, 32:64], half[:, 64:96], half[:, 96:128]]
    flux = mm(jnp.concatenate(blocks, axis=0), transposed(inverse_v))
    flux = [flux[k * RANK : (k + 1) * RANK] * (1.0 if k % 2 == 0 else -1.0) for k in range(6)]
    row = sublanes((16, RANK))
    column = jnp.concatenate([identity] + flux + [jnp.where(row == 0, weights_row, 0.0)], axis=0)
    to_kinetic = transposed(to_kinetic_t)
    wk[0] = mm(column, jnp.concatenate([to_kinetic] * 3 + [zeros], axis=1))
    wk[1] = jnp.concatenate([column] * 3 + [jnp.zeros((ROWS_K, 32), f32)], axis=1)
    moment[...] = jnp.broadcast_to(turned_raw[:, LAST : LAST + 1], (RANK, 128))


def small_first(parts, core, after, cells_total, points_total):
    def kernel(*refs):
        small_first_kernel(cells_total, points_total, *refs)

    return call(
        kernel, [((2, ROWS_K, 128), f32), ((2, 224, 128), f32), ((3, RANK, 128), f32), ((RANK, 128), f32)], "vvvvvvva",
        (*parts, core, SELECT, MEANS, after),
    )


def evolve_point_kernel(v_ref, speeds, rows, wl, src, values, after, new, out):
    q0 = v_ref[0] * Q1
    lane_w = lanes((RANK, 128))
    low_lane = ((lane_w >= 64) & (lane_w < 96)) | (lane_w == 97)

    def weights_of(w):
        hi = w.astype(bf16).astype(f32)
        return jnp.where(low_lane, w - hi, hi).astype(bf16)

    def piece(kind, n):
        return wl[kind, n * RANK : (n + 1) * RANK, :]

    fixed = [
        [jnp.concatenate([weights_of(piece(kind, n)) for n in ((5, 3, 6) if h == 0 else (2, 3, 6))], axis=0) for h in range(2)]
        for kind in range(2)
    ]
    tops = []
    aux = []
    for h in range(2):
        gh, gl = split(rows[h, 3:4, :])
        row = sublanes((16, HALF))
        gh, gl = gh.astype(f32), gl.astype(f32)
        tops.append(jnp.where(row < 2, gh, jnp.where(row == 2, gl, 0.0)).astype(bf16))
        aux.append(jnp.where(row == 0, 1.0, jnp.where(row == 1, gh, jnp.where(row == 2, gl, 0.0))).astype(bf16))

    def body(b, carry):
        sums, y, cross, ones_sum = list(carry[:2]), carry[2], carry[3], carry[4]
        up = speeds[q0 + b]
        um = speeds[NVD + q0 + b]
        g1 = speeds[2 * NVD + q0 + b]
        u = up + um
        moving = [piece(kind, 0) + up * piece(kind, 1) + um * piece(kind, 4) for kind in range(2)]
        heads = [weights_of(moving[min(n, 1)] + g1 * src[n]) for n in range(3)]
        for h in range(2):
            start = pl.multiple_of(b * (2 * HALF) + h * HALF, 128)
            state = values[:, pl.ds(start, HALF)]
            raw_hi, raw_lo = split(state)
            hi, lo = raw_hi, raw_lo
            for n in range(SUB):
                if n > 0:
                    hi, lo = split(state)
                w = jnp.concatenate([heads[n], fixed[min(n, 1)][h]], axis=0)[:, :112]
                mixed = dot(w, jnp.concatenate([hi, lo, hi, tops[h]], axis=0))
                state = (
                    mixed[:RANK]
                    + rows[h, 0:1, :] * mixed[RANK : 2 * RANK]
                    + rows[h, 1:2, :] * mixed[2 * RANK : 3 * RANK]
                    + rows[h, 2:3, :] * mixed[3 * RANK :]
                )
            new[:, pl.ds(start, HALF)] = state
            sh, sl = split(stacked(state, rows, h))
            lh, ll = sh[:RANK], sl[:RANK]
            t = dot_t(jnp.concatenate([lh, ll, aux[h]], axis=0), jnp.concatenate([sh, raw_hi], axis=0))
            t2 = dot_t(jnp.concatenate([lh, aux[h]], axis=0), jnp.concatenate([sl, raw_lo], axis=0))
            t_main = t[:RANK] + t[RANK : 2 * RANK] + t2[:RANK]
            cross = cross + t_main[:, 128:]
            t_main = t_main[:, :128]
            a = t[2 * RANK : 2 * RANK + 8, :128]
            a2 = t2[RANK : RANK + 8, :128]
            row8 = sublanes((8, 128))
            a = a + jnp.where(row8 < 2, a2, 0.0)
            ones_sum = ones_sum + jnp.where(row8 == 0, a, a * g1)
            sums[h] = sums[h] + t_main
            y = y + u * t_main
        return sums[0], sums[1], y, cross, ones_sum

    zero = jnp.zeros((RANK, 128), f32)
    first, second, y, cross, ones_sum = lax.fori_loop(
        0, Q1, body, (zero, zero, zero, jnp.zeros((RANK, RANK), f32), jnp.zeros((8, 128), f32))
    )
    cross = jnp.concatenate([jnp.zeros((RANK, 96), f32), cross], axis=1)
    tile_a, tile_b = point_tiles(first, second, y, v_ref[0] >= 4, cross)
    out[:RANK, :128] = tile_a
    out[:RANK, 128:] = tile_b
    out[RANK:, :128] = ones_sum
    out[RANK:, 128:] = jnp.zeros((8, 128), f32)


def evolve_point(v, wl, src, values, after):
    return call(
        evolve_point_kernel, [(values.shape, f32), ((RANK + 8, 256), f32)], "ssvvvva",
        (v, SPEEDS, ROWS, wl, src, values, after), mib=16,
    )


RATES = (LOW - 1 + OWN + HIGH - 1) * NY
HALO = RANK * HIGH * NY


def fill_kernel(v_ref, own, edge, mine, other, after, state, rates_low, rates_high):
    core = v_ref[0] % 2
    state[:, LOW * PLANE : (LOW + OWN) * PLANE] = own[...]
    state[:, (LOW - 1) * PLANE : LOW * PLANE] = edge[...]
    for source, place in ((mine, core), (other, 1 - core)):

        def load(p, carry, source=source, place=place):
            for y in range(NY):
                at = pl.multiple_of((p + place * (LOW + OWN)) * PLANE + y * NZ, 128)
                state[:, pl.ds(at, NZ)] = source[pl.ds(p * NY + y, RANK, stride=HIGH * NY), :]
            return carry

        lax.fori_loop(0, HIGH, load, 0)
    first, second = mine[HALO:, :], other[HALO:, :]
    rates_low[...] = jnp.where(core == 0, first, second)
    rates_high[...] = jnp.where(core == 0, second, first)


def fill_planes(v, own, edge, mine, other, after):
    part = ((HIGH * NY, NZ), f32)
    return call(
        fill_kernel, [((RANK, WIDE * PLANE), f32), part, part], "svvvva", (v, own, edge, mine, other, after),
        mib=12,
    )


def evolve_space_kernel(wk, moment, raw, rates, rates_low, rates_high, new, out, rates_all, partial, passed, *bufs):
    sources, targets = [raw, bufs[0], bufs[1]], [bufs[0], bufs[1], new]
    low, own = (LOW - 1) * NY, OWN * NY
    rates_all[:low, :] = rates_low[...]
    rates_all[low : low + own, :] = rates[...]
    rates_all[low + own :, :] = rates_high[: (HIGH - 1) * NY, :]
    lane = lanes((ROWS_K, 128))
    low_lane = (lane >= 64) & (lane < 96)

    for n in range(SUB):
        w = wk[min(n, 1)]
        w_hi = w.astype(bf16).astype(f32)
        w = jnp.where(low_lane, w - w_hi, w_hi).astype(bf16)[:, :96]
        if n > 0:
            w = w[RANK:]
        skip = w.shape[0] - ROWS_K + RANK
        src, dst = sources[n], targets[n]
        shift = 2 if n == SUB - 1 else 0
        begin, end = 1 + n, WIDE - 1 - n

        def tile(t, j, src=src):
            cells = src[:, pl.ds(pl.multiple_of(t * PLANE + j * 256, 256), 256)]
            a, b = split(cells)
            return cells, jnp.concatenate([a, b, a], axis=0)

        def put(t, y, block, dst=dst, shift=shift):
            dst[:, pl.ds(pl.multiple_of((t - shift) * PLANE + y * NZ, 128), NZ)] = block

        def step(t, carry, w=w, tile=tile, put=put, skip=skip):
            scale = moment[...]
            bases, ups, downs = [], [], []
            for j in range(NY // 2):
                cells, operand = tile(t, j)
                mixed = dot(w, operand)
                for i in range(2):
                    y = 2 * j + i
                    cell = slice(y * NZ, (y + 1) * NZ)
                    half = slice(i * NZ, (i + 1) * NZ)
                    part = [mixed[skip + k * RANK : skip + (k + 1) * RANK, half] for k in range(6)]
                    here = mixed[:RANK, half] if skip else cells[:, half]
                    density = mixed[skip + 6 * RANK : skip + 6 * RANK + 1, half]
                    put(t - 1, y, partial[:, cell] + part[1])
                    rate = rates_all[pl.ds((t - 1) * NY + y, 1), :]
                    base = here + rate * (scale * density - here) + passed[:, cell]
                    passed[:, cell] = part[0]
                    base = base - ((part[0] + part[1]) + (part[2] + part[3]) + (part[4] + part[5]))
                    bases.append(base + roll_lanes(part[4], 1) + roll_lanes(part[5], -1))
                    ups.append(part[2])
                    downs.append(part[3])
                    if y >= 2:
                        partial[:, (y - 1) * NZ : y * NZ] = bases[y - 1] + ups[y - 2] + downs[y]
            partial[:, (NY - 1) * NZ :] = bases[NY - 1] + ups[NY - 2] + downs[0]
            partial[:, :NZ] = bases[0] + ups[NY - 1] + downs[1]
            return carry

        for j in range(NY // 2):
            passed[:, j * 256 : (j + 1) * 256] = dot(w[skip : skip + RANK], tile(begin - 1, j)[1])
        lax.fori_loop(begin, end, step, 0)
        for j in range(NY // 2):
            mixed = dot(w[skip + RANK : skip + 2 * RANK], tile(end, j)[1])
            for i in range(2):
                y = 2 * j + i
                put(end - 1, y, partial[:, y * NZ : (y + 1) * NZ] + mixed[:, i * NZ : (i + 1) * NZ])

    def body(p, carry):
        t, c = carry
        turned, relaxed = [], []
        for y in range(NY):
            block = new[:, pl.ds(pl.multiple_of((p + 2) * PLANE + y * NZ, 128), NZ)]
            turned.append(split(roll_lanes(block, 1)))
            relaxed.append(split(block * rates[pl.ds(p * NY + y, 1), :]))
        here = split(new[:, pl.ds(pl.multiple_of((p + 2) * PLANE, 128), PLANE)])
        behind = split(new[:, pl.ds(pl.multiple_of((p + 1) * PLANE, 128), PLANE)])
        old = split(raw[:, pl.ds(pl.multiple_of((p + LOW) * PLANE, 128), PLANE)])

        def stack(k):
            wrapped = jnp.concatenate([here[k][:, PLANE - NZ :], here[k][:, : PLANE - NZ]], axis=1)
            rolled = jnp.concatenate([block[k] for block in turned], axis=1)
            scaled = jnp.concatenate([block[k] for block in relaxed], axis=1)
            return jnp.concatenate([here[k], behind[k], wrapped, rolled, scaled, old[k]], axis=0)

        part = dot_t(jnp.concatenate(here, axis=0), stack(0))
        part = part[:RANK] + part[RANK:] + dot_t(here[0], stack(1))
        return t + part[:, :128], c + part[:, 128:]

    t, c = lax.fori_loop(0, OWN, body, (jnp.zeros((RANK, 128), f32), jnp.zeros((RANK, 64), f32)))
    out[:, :128] = t
    out[:, 128:] = jnp.concatenate([c, jnp.zeros((RANK, 64), f32)], axis=1)


def evolve_space(wk, moment, filled, rates):
    return call(
        evolve_space_kernel, [((RANK, (OWN + 2) * PLANE), f32), ((RANK, 256), f32)], "v" * 6,
        (wk, moment, filled[0], rates, filled[1], filled[2]),
        [pltpu.VMEM((RATES, NZ), f32)]
        + [pltpu.VMEM((RANK, PLANE), f32)] * 2
        + [pltpu.VMEM((RANK, WIDE * PLANE), f32)] * 2,
        mib=16,
    )


def finish_kernel(
    cells_total, points_total, p0, p1, p2, p3, core, kinetic, spread, space_out, fresh_core, point_out, fresh_space, fresh_point, sems
):
    both = four((p0, p1, p2, p3))
    s = both[:RANK] * (1.0 / cells_total)
    q = both[RANK:] * (1.0 / points_total)
    gram, gram_v = s[:, 0:32], q[:RANK, 0:32]
    (_, inverse), (_, inverse_v) = factor_pair(gram, gram_v)
    zeros = jnp.zeros((RANK, 32), f32)
    lane = lanes((RANK, 128))

    def wide(matrix):
        w = jnp.concatenate([matrix] * 3 + [zeros], axis=1)
        hi = w.astype(bf16).astype(f32)
        return jnp.where((lane >= 64) & (lane < 96), w - hi, hi).astype(bf16)[:, :96]

    w_space, w_point = wide(inverse), wide(inverse_v)

    def out_space(p, carry):
        for half in range(2):
            size = PLANE // 2
            at = pl.multiple_of((p + 2) * PLANE + half * size, 128)
            hi, lo = split(kinetic[:, pl.ds(at, size)])
            made = dot(w_space, jnp.concatenate([hi, lo, hi], axis=0))
            for y in range(NY // 2):
                fresh_space[pl.ds(p * NY + half * (NY // 2) + y, RANK, stride=OWN * NY), :] = made[:, y * NZ : (y + 1) * NZ]
        return carry

    lax.fori_loop(0, OWN, out_space, 0)
    copies = [pltpu.make_async_copy(fresh_space, space_out, sems.at[0])]
    copies[0].start()
    third = 2 * Q1 * HALF // 3

    def out_point(i, carry):
        at = pl.multiple_of(i * 1536, 512)
        hi, lo = split(spread[:, pl.ds(at, 1536)])
        fresh_point[:, pl.ds(at, 1536)] = dot(w_point, jnp.concatenate([hi, lo, hi], axis=0))
        return carry

    for k in range(3):
        lax.fori_loop(3 * k, 3 * k + 3, out_point, 0)
        cells = pl.ds(k * third, third)
        copies.append(pltpu.make_async_copy(fresh_point.at[:, cells], point_out.at[:, cells], sems.at[k + 1]))
        copies[-1].start()

    inverse_t = transposed(inverse)
    inverse_vt = transposed(inverse_v)
    turned = mm(inverse, s)
    turned_v = mm(inverse_v, q[:RANK])
    aux = mm(q[RANK:, 0:32], inverse_vt)
    weights_row = aux[0:1, :]
    moments_row = aux[1:2, :] + aux[2:3, :]
    left = [turned[:, 128:160]]
    for d in range(3):
        left.append(turned[:, 0:32] - turned[:, 32 * (d + 1) : 32 * (d + 2)])
    for d in range(3):
        left.append(mm_t(inverse, gram - s[:, 32 * (d + 1) : 32 * (d + 2)]))
    stack = mm(jnp.concatenate(left, axis=0), inverse_t)
    lines = [turned_v[:, 192:224], turned_v[:, 160:192], turned_v[:, 64:96]]
    lines += [-turned_v[:, 128:160], -turned_v[:, 32:64], -turned_v[:, 96:128]]
    flux = mm(jnp.concatenate(lines, axis=0), inverse_vt)
    current = mm_t(mm(turned[:, 160:192], core[...]), turned_v[:, 224:256])
    for _ in range(SUB):
        moved = mm(stack, current)
        scaled = moved[:RANK]
        change = -scaled + jnp.sum(scaled * weights_row, axis=1, keepdims=True) * moments_row
        across = jnp.concatenate([moved[(k + 1) * RANK : (k + 2) * RANK] for k in range(6)], axis=1)
        current = current + (change - mm(across, flux))
    fresh_core[...] = current
    for copy in copies:
        copy.wait()


def finish(parts, core, kinetic, spread, cells_total, points_total):
    def kernel(*refs):
        finish_kernel(cells_total, points_total, *refs)

    flat = (RANK * OWN * NY, NZ)
    return call(
        kernel, [(flat, f32), ((RANK, RANK), f32), (spread.shape, f32)], "vvvvvvv",
        (*parts, core, kinetic, spread),
        [pltpu.VMEM(flat, f32), pltpu.VMEM(spread.shape, f32), pltpu.SemaphoreType.DMA((4,))],
        mib=12, out_spaces="ava",
    )


def spread_pairs(space_part):
    moved = []
    for k in range(2):
        route = [((s ^ (2 * v + k)) * 8 + v, s * 8 + v) for s in range(16) for v in range(8)]
        moved.append(lax.ppermute(space_part, ("space", "vel"), route))
    return moved


def vel_parts(moved, point_part):
    joint = jnp.concatenate([moved[0] + moved[1], point_part], axis=0)
    pair = [(2 * z + c, 2 * z + 1 - c) for z in range(4) for c in range(2)]
    joint = joint + lax.ppermute(joint, "vel", pair)
    routes = [[(2 * z + c, 2 * ((z + d) % 4) + c) for z in range(4) for c in range(2)] for d in (1, 2, 3)]
    parts = [joint]
    for route in routes:
        parts.append(lax.ppermute(joint, "vel", route))
    return parts


def per_device(space_factor, core_matrix, velocity_factor, collision_rates):
    devices = lax.axis_size("space")
    up = [(i, (i + 1) % devices) for i in range(devices)]
    below1 = lax.ppermute(space_factor[:, OWN - 1 :], "space", up).reshape(-1, NZ)
    rates = collision_rates.reshape(-1, NZ)
    values = space_factor.reshape(-1, NZ)
    cells_total = OWN * PLANE * devices
    points_total = velocity_factor.shape[1] * lax.axis_size("vel")
    place = lax.axis_index("vel").astype(jnp.int32)
    v = place.reshape(1)
    planes = jnp.where(place % 2 == 0, space_factor[:, : OWN - 1], space_factor[:, :HIGH])
    lines = jnp.where(place % 2 == 0, collision_rates[1:], collision_rates[:HIGH])
    halo = jnp.concatenate([planes, lines[None]], axis=0)
    route = [(s * 8 + w, (s + 1 - 2 * (w % 2)) % devices * 8 + w) for s in range(devices) for w in range(8)]
    pair = [(w, w ^ 1) for w in range(8)]

    inner, own = space_sums(values, rates)
    point = point_sums(v, velocity_factor, inner)
    halo, point = lax.optimization_barrier((halo, point))
    mine = lax.ppermute(halo, ("space", "vel"), route)
    space, edge = edge_sums(own, below1, inner)
    moved = spread_pairs(space)
    parts = vel_parts(moved, point)
    mine, parts[0] = lax.optimization_barrier((mine, parts[0]))
    other = lax.ppermute(mine, "vel", pair)
    filled = fill_planes(v, own, edge, mine.reshape(-1, NZ), other.reshape(-1, NZ), parts[0])
    wk, wl, src, moment = small_first(parts, core_matrix, filled[0], cells_total, points_total)
    kinetic, space = evolve_space(wk, moment, filled, rates)
    moved = spread_pairs(space)
    spread, point = evolve_point(v, wl, src, velocity_factor, space)
    parts = vel_parts(moved, point)
    fresh_space, fresh_core, fresh_point = finish(parts, core_matrix, kinetic, spread, cells_total, points_total)
    return fresh_space.reshape(space_factor.shape), fresh_core, fresh_point


def solution(mesh):
    return jax.shard_map(
        per_device,
        mesh=mesh,
        in_specs=(P(None, "space", None, None), P(), P(None, "vel"), P("space", None, None)),
        out_specs=(P(None, "space", None, None), P(), P(None, "vel")),
        check_vma=False,
    )
```

```python
import jax
import jax.numpy as jnp
import numpy as np
from jax import lax
from jax.experimental import pallas as pl
from jax.experimental.pallas import tpu as pltpu
from jax.sharding import PartitionSpec as P


RANK = 32
NVD = 48
SUB = 3
LOW = SUB + 1
HIGH = SUB
NY = 16
NZ = 128
OWN = 4
Q1 = 6
HALF = NVD * NVD // 2
PLANE = NY * NZ
WIDE = LOW + OWN + HIGH
ROWS_K = 7 * RANK + 16
INTERPRET = False

f32 = jnp.float32
bf16 = jnp.bfloat16


def tables():
    t = np.float32(0.25) * ((2 * np.arange(NVD) + 1).astype(np.float32) / np.float32(NVD) - np.float32(1.0))
    t = t.astype(np.float32)
    shape = np.exp(-(t.astype(np.float64) ** 2) / (2.0 * 0.125 * 0.125))
    shape = shape / shape.mean()
    plus, minus = np.maximum(t, 0), np.minimum(t, 0)
    u2, u3 = np.repeat(t, NVD), np.tile(t, NVD)
    g23 = np.repeat(shape, NVD) * np.tile(shape, NVD)
    sides = [(1, "p"), (2, "p"), (3, "p"), (1, "m"), (2, "m"), (3, "m")]
    names = [()] + [(s,) for s in sides]
    where = {(): 0}
    for k in range(6):
        where[(k,)] = k + 1
    for j in range(6):
        for k in range(j, 6):
            if k != j and sides[j][0] == sides[k][0]:
                continue
            where[(j, k)] = len(names)
            names.append((sides[j], sides[k]))
    base = np.zeros((2, 32, HALF))
    scale = np.zeros((NVD, 128))
    value = {"p": np.maximum, "m": np.minimum}
    for row, name in enumerate(names):
        b = np.ones(NVD * NVD)
        c = np.ones(NVD)
        for d, sign in name:
            if d == 1:
                c = c * value[sign](t.astype(np.float64), 0)
            elif d == 2:
                b = b * value[sign](u2.astype(np.float64), 0)
            else:
                b = b * value[sign](u3.astype(np.float64), 0)
        base[:, row] = b.reshape(2, HALF)
        scale[:, row] = c
    last = len(names)
    base[:, last] = g23.reshape(2, HALF)
    scale[:, last] = shape
    select = np.zeros((32, 7 * 128), np.float32)
    for j in range(7):
        for k in range(7):
            pair = tuple(sorted([i - 1 for i in (j, k) if i > 0]))
            if pair in where:
                select[where[pair], j * 128 + k] = 1.0
    means = np.zeros((8, 128), np.float32)
    means[:, 0] = 1.0
    means[:, 1:4] = (shape * plus).mean()
    means[:, 4:7] = (shape * minus).mean()
    rows = np.zeros((2, 8, HALF), np.float32)
    rows[:, 0] = u2.reshape(2, HALF)
    rows[:, 1] = np.maximum(u3, 0).reshape(2, HALF)
    rows[:, 2] = np.minimum(u3, 0).reshape(2, HALF)
    rows[:, 3] = g23.reshape(2, HALF)
    speeds = np.concatenate([plus, minus, shape]).astype(np.float32)
    return rows, base.astype(np.float32), scale.astype(np.float32), select, means, speeds, last


ROWS, PHI, PHI_SCALE, SELECT, MEANS, SPEEDS, LAST = tables()


def split(x):
    hi = x.astype(bf16)
    return hi, (x - hi.astype(f32)).astype(bf16)


def dot(a, b):
    return jnp.dot(a, b, preferred_element_type=f32)


def dot_t(a, b):
    return lax.dot_general(a, b, (((1,), (1,)), ((), ())), preferred_element_type=f32)


def mm(a, b, form=dot):
    rows = a.shape[0]
    ah, al = split(a)
    bh, bl = split(b)
    main = form(jnp.concatenate([ah, al], axis=0), bh)
    return main[:rows] + main[rows:] + form(ah, bl)


def mm_t(a, b):
    return mm(a, b, dot_t)


def lanes(shape):
    return lax.broadcasted_iota(jnp.int32, shape, len(shape) - 1)


def sublanes(shape):
    return lax.broadcasted_iota(jnp.int32, shape, len(shape) - 2)


def eye():
    return (lanes((RANK, RANK)) == sublanes((RANK, RANK))).astype(f32)


def call(kernel, outs, ins, args, scratch=(), mib=8, out_spaces=None):
    spaces = {"v": pltpu.VMEM, "s": pltpu.SMEM, "a": pl.ANY}
    out_spaces = out_spaces or "v" * len(outs)
    return pl.pallas_call(
        kernel,
        out_shape=[jax.ShapeDtypeStruct(s, d) for s, d in outs],
        in_specs=[pl.BlockSpec(memory_space=spaces[c]) for c in ins],
        out_specs=[pl.BlockSpec(memory_space=spaces[c]) for c in out_spaces],
        scratch_shapes=list(scratch),
        compiler_params=pltpu.CompilerParams(vmem_limit_bytes=mib * 1024 * 1024),
        interpret=INTERPRET,
    )(*args)


def point_tiles(first, second, y, positive, extra):
    lane = lanes((RANK, 128))
    middle = (lane >= 32) & (lane < 64)
    tile_a = first + jnp.where(middle, 0.0, second)
    y = jnp.where(lane < 32, y, 0.0)
    y = jnp.where(positive, pltpu.roll(y, 64, 1) if not INTERPRET else jnp.roll(y, 64, 1), y)
    return tile_a, jnp.where(middle, second, 0.0) + y + extra


def roll_lanes(x, shift):
    return jnp.roll(x, shift, 1) if INTERPRET else pltpu.roll(x, shift % x.shape[1], 1)


def stacked(values, rows, h):
    return jnp.concatenate(
        [values, values * rows[h, 0:1, :], values * rows[h, 1:2, :], values * rows[h, 2:3, :]], axis=0
    )


def point_sums_kernel(v_ref, speeds, rows, phi, scale, values, after, out):
    q0 = v_ref[0] * Q1
    phi_parts = [split(phi[h]) for h in range(2)]

    def body(b, carry):
        sums, y, moments = list(carry[:2]), carry[2], carry[3]
        u = speeds[q0 + b] + speeds[NVD + q0 + b]
        for h in range(2):
            start = pl.multiple_of(b * (2 * HALF) + h * HALF, 128)
            sh, sl = split(stacked(values[:, pl.ds(start, HALF)], rows, h))
            lh, ll = sh[:RANK], sl[:RANK]
            ph, plo = phi_parts[h]
            both = jnp.concatenate([lh, ll], axis=0)
            t = dot_t(both, jnp.concatenate([sh, ph], axis=0))
            t = t[:RANK] + t[RANK:] + dot_t(lh, jnp.concatenate([sl, plo], axis=0))
            t, m = t[:, :128], t[:, 128:]
            sums[h] = sums[h] + t
            y = y + u * t
            moments = moments + m * scale[pl.ds(q0 + b, 1), :RANK]
        return sums[0], sums[1], y, moments

    zero = jnp.zeros((RANK, 128), f32)
    first, second, y, moments = lax.fori_loop(0, Q1, body, (zero, zero, zero, jnp.zeros((RANK, RANK), f32)))
    moments = jnp.concatenate([jnp.zeros((RANK, 96), f32), moments], axis=1)
    tile_a, tile_b = point_tiles(first, second, y, v_ref[0] >= 4, moments)
    out[:, :128] = tile_a
    out[:, 128:] = tile_b


def point_sums(v, values, after):
    return call(
        point_sums_kernel, [((RANK, 256), f32)], "ssvvvva",
        (v, SPEEDS, ROWS, PHI, PHI_SCALE, values, after), mib=12,
    )[0]


def space_sums_kernel(values, rates, out, own, hi, lo, zh, zl, ch, cl):
    def load(p, carry):
        for y in range(NY):
            block = values[pl.ds(p * NY + y, RANK, stride=OWN * NY), :]
            at = pl.multiple_of(p * PLANE + y * NZ, 128)
            a, b = split(block)
            hi[:, pl.ds(at + PLANE, NZ)] = a
            lo[:, pl.ds(at + PLANE, NZ)] = b
            own[:, pl.ds(at, NZ)] = block
            a, b = split(roll_lanes(block, 1))
            zh[:, pl.ds(at, NZ)] = a
            zl[:, pl.ds(at, NZ)] = b
            a, b = split(block * rates[pl.ds(p * NY + y, 1), :])
            ch[:, pl.ds(at, NZ)] = a
            cl[:, pl.ds(at, NZ)] = b
        return carry

    hi[:, :PLANE] = jnp.zeros((RANK, PLANE), bf16)
    lo[:, :PLANE] = jnp.zeros((RANK, PLANE), bf16)
    lax.fori_loop(0, OWN, load, 0)

    def body(p, carry):
        t, c = carry
        at = pl.multiple_of(p * PLANE, 128)

        def stack(main, turned):
            here = main[:, pl.ds(at + PLANE, PLANE)]
            wrapped = jnp.concatenate([here[:, PLANE - NZ :], here[:, : PLANE - NZ]], axis=1)
            return jnp.concatenate(
                [here, main[:, pl.ds(at, PLANE)], wrapped, turned[:, pl.ds(at, PLANE)]], axis=0
            )

        sh, sl = stack(hi, zh), stack(lo, zl)
        both = jnp.concatenate([sh[:RANK], sl[:RANK]], axis=0)
        part = dot_t(both, jnp.concatenate([sh, ch[:, pl.ds(at, PLANE)]], axis=0))
        part = part[:RANK] + part[RANK:] + dot_t(sh[:RANK], jnp.concatenate([sl, cl[:, pl.ds(at, PLANE)]], axis=0))
        return t + part[:, :128], c + part[:, 128:]

    t, c = lax.fori_loop(0, OWN, body, (jnp.zeros((RANK, 128), f32), jnp.zeros((RANK, RANK), f32)))
    out[:, :128] = t
    out[:, 128:] = jnp.concatenate([c, jnp.zeros((RANK, 96), f32)], axis=1)


def space_sums(values, rates):
    own = (RANK, OWN * PLANE)
    return call(
        space_sums_kernel, [((RANK, 256), f32), (own, f32)], "vv", (values, rates),
        [pltpu.VMEM((RANK, (OWN + 1) * PLANE), bf16)] * 2 + [pltpu.VMEM(own, bf16)] * 4, mib=12,
    )


def edge_sums_kernel(own, below, inner, out, edge):
    empty = jnp.zeros((RANK, PLANE), bf16)
    other = jnp.concatenate([below[pl.ds(y, RANK, stride=NY), :] for y in range(NY)], axis=1)
    edge[...] = other
    oh, ol = split(other)
    lh, ll = split(own[:, :PLANE])
    part = dot_t(jnp.concatenate([lh, ll], axis=0), jnp.concatenate([empty, oh], axis=0))
    t = part[:RANK] + part[RANK:] + dot_t(lh, jnp.concatenate([empty, ol], axis=0))
    out[:, :128] = inner[:, :128] + jnp.concatenate([t, jnp.zeros((RANK, 64), f32)], axis=1)
    out[:, 128:] = inner[:, 128:]


def edge_sums(own, below, inner):
    return call(edge_sums_kernel, [((RANK, 256), f32), ((RANK, PLANE), f32)], "vvv", (own, below, inner))


def factor_pair(first, second):
    zeros = jnp.zeros((RANK, 64), f32)
    works = [jnp.concatenate([g, eye(), zeros], axis=1) for g in (first, second)]
    pivots = [jnp.ones((RANK, 128), f32)] * 2
    row = sublanes((RANK, 128))
    for k in range(0, RANK, 2):
        for n in range(2):
            w = works[n]
            c0 = jnp.broadcast_to(w[:, k : k + 1], (RANK, 128))
            c1 = jnp.broadcast_to(w[:, k + 1 : k + 2], (RANK, 128))
            r0, r1 = w[k : k + 1, :], w[k + 1 : k + 2, :]
            a, b, d = c0[k : k + 1, :], c1[k : k + 1, :], c1[k + 1 : k + 2, :]
            over = 1.0 / a
            ratio = b * over
            d = d - b * ratio
            r1 = r1 - ratio * r0
            c1 = c1 - ratio * c0
            step = w - c0 * (r0 * over) - c1 * (r1 * (1.0 / d))
            works[n] = jnp.where(row > k + 1, step, jnp.where(row == k + 1, r1, w))
            pivots[n] = jnp.where(row == k, a, jnp.where(row == k + 1, d, pivots[n]))
    done = [works[n] * lax.rsqrt(pivots[n]) for n in range(2)]
    return [(w[:, :RANK], w[:, RANK : 2 * RANK]) for w in done]


def transposed(x):
    return mm_t(eye(), x)


def point_blocks(tiles, points_total):
    t = tiles * (1.0 / points_total)
    gram = t[:, 0:32]
    plus = [t[:, 192:224], t[:, 160:192], t[:, 64:96]]
    minus = [t[:, 128:160], t[:, 32:64], t[:, 96:128]]
    return gram, plus, minus, t[:, 224:256]


def four(parts):
    return (parts[0][...] + parts[2][...]) + (parts[1][...] + parts[3][...])


def small_first_kernel(cells_total, points_total, p0, p1, p2, p3, core, select, means, wk, wl, src, moment):
    both = four((p0, p1, p2, p3))
    s = both[:RANK] * (1.0 / cells_total)
    gram = s[:, 0:32]
    gram_v, _, _, raw = point_blocks(both[RANK:], points_total)
    (upper, inverse), (upper_v, inverse_v) = factor_pair(gram, gram_v)
    identity = eye()
    raw_a = [gram - s[:, 32 * (d + 1) : 32 * (d + 2)] for d in range(3)]
    to_spread = mm(upper, core[...])
    to_kinetic_t = mm_t(core[...], upper_v)
    zeros = jnp.zeros((RANK, 32), f32)
    inverse_t = transposed(inverse)
    triple = jnp.concatenate([inverse_t] * 3 + [zeros], axis=1)
    left = (
        [mm(inverse, s[:, 128:160])] + [mm(inverse, a) for a in raw_a] + [mm_t(inverse, a) for a in raw_a]
    )
    turned = mm(jnp.concatenate(left, axis=0), triple)
    one = jnp.concatenate([identity] * 3 + [zeros], axis=1)
    e_wide = turned[:RANK]
    mixers = [one - e_wide] + [-turned[RANK * (d + 1) : RANK * (d + 2)] for d in range(3)]
    mixers = mixers + [turned[RANK * (d + 4) : RANK * (d + 5)] for d in range(3)]
    stack = jnp.concatenate(mixers, axis=0)
    wl[1] = stack
    wl[0] = mm(stack[:, :RANK], jnp.concatenate([to_spread] * 3 + [zeros], axis=1))
    square = [m[:, :RANK] for m in mixers]
    e = e_wide[:, :RANK]
    moved = mm(mm(to_spread, raw), select[...])
    groups = [moved[:, 128 * j : 128 * (j + 1)] for j in range(7)]
    lane = lanes((RANK, 128))
    source = [mm(e, groups[0])[:, 0:1]]
    following = mm(square[0], groups[0]) + source[0] * means[0:1, :]
    for j in range(1, 7):
        following = following + mm(square[j], groups[j])
    source.append(mm(e, following)[:, 0:1])
    third = mm(square[0], jnp.where(lane == 0, following, 0.0))
    for j in range(1, 7):
        third = third + mm(square[j], jnp.where(lane == j, following, 0.0))
    third = jnp.sum(third, axis=1, keepdims=True) + source[1] * means[0:1, 0:1]
    source.append(mm(e, jnp.broadcast_to(third, (RANK, 128)))[:, 0:1])
    for n in range(3):
        src[n] = jnp.broadcast_to(source[n], (RANK, 128))
    half = mm(inverse_v, both[RANK:, :] * (1.0 / points_total))
    turned_raw = half[:, 224:256]
    weights_row = transposed(turned_raw)[0:1, :]
    blocks = [half[:, 192:224], half[:, 128:160], half[:, 160:192], half[:, 32:64], half[:, 64:96], half[:, 96:128]]
    flux = mm(jnp.concatenate(blocks, axis=0), transposed(inverse_v))
    flux = [flux[k * RANK : (k + 1) * RANK] * (1.0 if k % 2 == 0 else -1.0) for k in range(6)]
    row = sublanes((16, RANK))
    column = jnp.concatenate([identity] + flux + [jnp.where(row == 0, weights_row, 0.0)], axis=0)
    to_kinetic = transposed(to_kinetic_t)
    wk[0] = mm(column, jnp.concatenate([to_kinetic] * 3 + [zeros], axis=1))
    wk[1] = jnp.concatenate([column] * 3 + [jnp.zeros((ROWS_K, 32), f32)], axis=1)
    moment[...] = jnp.broadcast_to(turned_raw[:, LAST : LAST + 1], (RANK, 128))


def small_first(parts, core, cells_total, points_total):
    def kernel(*refs):
        small_first_kernel(cells_total, points_total, *refs)

    return call(
        kernel, [((2, ROWS_K, 128), f32), ((2, 224, 128), f32), ((3, RANK, 128), f32), ((RANK, 128), f32)], "vvvvvvv",
        (*parts, core, SELECT, MEANS),
    )


def evolve_point_kernel(v_ref, speeds, rows, wl, src, values, after, new, out):
    q0 = v_ref[0] * Q1
    lane_w = lanes((RANK, 128))
    low_lane = (lane_w >= 64) & (lane_w < 96)

    def weights_of(w):
        hi = w.astype(bf16).astype(f32)
        return jnp.where(low_lane, w - hi, hi).astype(bf16)

    def piece(kind, n):
        return wl[kind, n * RANK : (n + 1) * RANK, :]

    fixed = [jnp.concatenate([weights_of(piece(kind, n)) for n in (3, 6)], axis=0) for kind in range(2)]
    turning = [[weights_of(piece(kind, n)) for n in (5, 2)] for kind in range(2)]
    aux = []
    for h in range(2):
        gh, gl = split(rows[h, 3:4, :])
        row = sublanes((16, HALF))
        gh, gl = gh.astype(f32), gl.astype(f32)
        aux.append(jnp.where(row == 0, 1.0, jnp.where(row == 1, gh, jnp.where(row == 2, gl, 0.0))).astype(bf16))
    inside = HALF // 256 * 256
    cuts = [(0, inside, (0,)), (inside, 2 * HALF - inside, (0, 1)), (2 * HALF - inside, 2 * HALF, (1,))]

    def body(b, carry):
        sums, y, cross, ones_sum = list(carry[:2]), carry[2], carry[3], carry[4]
        up = speeds[q0 + b]
        um = speeds[NVD + q0 + b]
        g1 = speeds[2 * NVD + q0 + b]
        u = up + um
        moving = [piece(kind, 0) + up * piece(kind, 1) + um * piece(kind, 4) for kind in range(2)]
        heads = [weights_of(m) for m in moving]
        first = pl.multiple_of(b * (2 * HALF), 128)
        states = [values[:, pl.ds(first, HALF)], values[:, pl.ds(first + HALF, HALF)]]
        raws = [split(state) for state in states]
        for n in range(SUB):
            kind = min(n, 1)
            parts = raws if n == 0 else [split(state) for state in states]
            operand = jnp.concatenate(
                [jnp.concatenate([parts[0][k], parts[1][k]], axis=1) for k in (0, 1, 0)], axis=0
            )
            source = src[n] * g1
            mixed = []
            for low, high, sides in cuts:
                w = jnp.concatenate([heads[kind], fixed[kind]] + [turning[kind][h] for h in sides], axis=0)[:, :96]
                mixed.append(dot(w, operand[:, low:high]))
            rest = HALF - inside
            middle = mixed[1]
            ends = [
                jnp.concatenate([mixed[0], middle[: 4 * RANK, :rest]], axis=1),
                jnp.concatenate([jnp.concatenate([middle[: 3 * RANK, rest:], middle[4 * RANK :, rest:]], axis=0), mixed[2]], axis=1),
            ]
            states = [
                ends[h][:RANK]
                + rows[h, 3:4, :] * source[:, 0:1]
                + rows[h, 1:2, :] * ends[h][RANK : 2 * RANK]
                + rows[h, 2:3, :] * ends[h][2 * RANK : 3 * RANK]
                + rows[h, 0:1, :] * ends[h][3 * RANK :]
                for h in range(2)
            ]
        for h in range(2):
            start = pl.multiple_of(b * (2 * HALF) + h * HALF, 128)
            state = states[h]
            raw_hi, raw_lo = raws[h]
            new[:, pl.ds(start, HALF)] = state
            sh, sl = split(stacked(state, rows, h))
            lh, ll = sh[:RANK], sl[:RANK]
            t = dot_t(jnp.concatenate([lh, ll, aux[h]], axis=0), jnp.concatenate([sh, raw_hi], axis=0))
            t2 = dot_t(jnp.concatenate([lh, aux[h]], axis=0), jnp.concatenate([sl, raw_lo], axis=0))
            t_main = t[:RANK] + t[RANK : 2 * RANK] + t2[:RANK]
            cross = cross + t_main[:, 128:]
            t_main = t_main[:, :128]
            a = t[2 * RANK : 2 * RANK + 8, :128]
            a2 = t2[RANK : RANK + 8, :128]
            row8 = sublanes((8, 128))
            a = a + jnp.where(row8 < 2, a2, 0.0)
            ones_sum = ones_sum + jnp.where(row8 == 0, a, a * g1)
            sums[h] = sums[h] + t_main
            y = y + u * t_main
        return sums[0], sums[1], y, cross, ones_sum

    zero = jnp.zeros((RANK, 128), f32)
    first, second, y, cross, ones_sum = lax.fori_loop(
        0, Q1, body, (zero, zero, zero, jnp.zeros((RANK, RANK), f32), jnp.zeros((8, 128), f32))
    )
    cross = jnp.concatenate([jnp.zeros((RANK, 96), f32), cross], axis=1)
    tile_a, tile_b = point_tiles(first, second, y, v_ref[0] >= 4, cross)
    out[:RANK, :128] = tile_a
    out[:RANK, 128:] = tile_b
    out[RANK:, :128] = ones_sum
    out[RANK:, 128:] = jnp.zeros((8, 128), f32)


def evolve_point(v, wl, src, values, after):
    return call(
        evolve_point_kernel, [(values.shape, f32), ((RANK + 8, 256), f32)], "ssvvvva",
        (v, SPEEDS, ROWS, wl, src, values, after), mib=16,
    )


RATES = (LOW - 1 + OWN + HIGH - 1) * NY
HALO = RANK * HIGH * NY


def fill_kernel(v_ref, own, edge, mine, other, after, state, rates_low, rates_high):
    core = v_ref[0] % 2
    state[:, LOW * PLANE : (LOW + OWN) * PLANE] = own[...]
    state[:, (LOW - 1) * PLANE : LOW * PLANE] = edge[...]
    for source, place in ((mine, core), (other, 1 - core)):

        def load(p, carry, source=source, place=place):
            for y in range(NY):
                at = pl.multiple_of((p + place * (LOW + OWN)) * PLANE + y * NZ, 128)
                state[:, pl.ds(at, NZ)] = source[pl.ds(p * NY + y, RANK, stride=HIGH * NY), :]
            return carry

        lax.fori_loop(0, HIGH, load, 0)
    first, second = mine[HALO:, :], other[HALO:, :]
    rates_low[...] = jnp.where(core == 0, first, second)
    rates_high[...] = jnp.where(core == 0, second, first)


def fill_planes(v, own, edge, mine, other, after):
    part = ((HIGH * NY, NZ), f32)
    return call(
        fill_kernel, [((RANK, WIDE * PLANE), f32), part, part], "svvvva", (v, own, edge, mine, other, after),
        mib=12,
    )


def evolve_space_kernel(wk, moment, raw, rates, rates_low, rates_high, new, out, rates_all, partial, passed, *bufs):
    sources, targets = [raw, bufs[0], bufs[1]], [bufs[0], bufs[1], new]
    low, own = (LOW - 1) * NY, OWN * NY
    rates_all[:low, :] = rates_low[...]
    rates_all[low : low + own, :] = rates[...]
    rates_all[low + own :, :] = rates_high[: (HIGH - 1) * NY, :]
    lane = lanes((ROWS_K, 128))
    low_lane = (lane >= 64) & (lane < 96)

    for n in range(SUB):
        w = wk[min(n, 1)]
        w_hi = w.astype(bf16).astype(f32)
        w = jnp.where(low_lane, w - w_hi, w_hi).astype(bf16)[:, :96]
        if n > 0:
            w = w[RANK:]
        skip = w.shape[0] - ROWS_K + RANK
        src, dst = sources[n], targets[n]
        shift = 2 if n == SUB - 1 else 0
        begin, end = 1 + n, WIDE - 1 - n

        def tile(t, j, src=src):
            cells = src[:, pl.ds(pl.multiple_of(t * PLANE + j * 256, 256), 256)]
            a, b = split(cells)
            return cells, jnp.concatenate([a, b, a], axis=0)

        def put(t, y, block, dst=dst, shift=shift):
            dst[:, pl.ds(pl.multiple_of((t - shift) * PLANE + y * NZ, 128), NZ)] = block

        def step(t, carry, w=w, tile=tile, put=put, skip=skip):
            scale = moment[...]
            bases, ups, downs = [], [], []
            for j in range(NY // 2):
                cells, operand = tile(t, j)
                mixed = dot(w, operand)
                for i in range(2):
                    y = 2 * j + i
                    cell = slice(y * NZ, (y + 1) * NZ)
                    half = slice(i * NZ, (i + 1) * NZ)
                    part = [mixed[skip + k * RANK : skip + (k + 1) * RANK, half] for k in range(6)]
                    here = mixed[:RANK, half] if skip else cells[:, half]
                    density = mixed[skip + 6 * RANK : skip + 6 * RANK + 1, half]
                    put(t - 1, y, partial[:, cell] + part[1])
                    rate = rates_all[pl.ds((t - 1) * NY + y, 1), :]
                    base = here + rate * (scale * density - here) + passed[:, cell]
                    passed[:, cell] = part[0]
                    base = base - ((part[0] + part[1]) + (part[2] + part[3]) + (part[4] + part[5]))
                    bases.append(base + roll_lanes(part[4], 1) + roll_lanes(part[5], -1))
                    ups.append(part[2])
                    downs.append(part[3])
                    if y >= 2:
                        partial[:, (y - 1) * NZ : y * NZ] = bases[y - 1] + ups[y - 2] + downs[y]
            partial[:, (NY - 1) * NZ :] = bases[NY - 1] + ups[NY - 2] + downs[0]
            partial[:, :NZ] = bases[0] + ups[NY - 1] + downs[1]
            return carry

        for j in range(NY // 2):
            passed[:, j * 256 : (j + 1) * 256] = dot(w[skip : skip + RANK], tile(begin - 1, j)[1])
        lax.fori_loop(begin, end, step, 0)
        for j in range(NY // 2):
            mixed = dot(w[skip + RANK : skip + 2 * RANK], tile(end, j)[1])
            for i in range(2):
                y = 2 * j + i
                put(end - 1, y, partial[:, y * NZ : (y + 1) * NZ] + mixed[:, i * NZ : (i + 1) * NZ])

    def body(p, carry):
        t, c = carry
        turned, relaxed = [], []
        for y in range(NY):
            block = new[:, pl.ds(pl.multiple_of((p + 2) * PLANE + y * NZ, 128), NZ)]
            turned.append(split(roll_lanes(block, 1)))
            relaxed.append(split(block * rates[pl.ds(p * NY + y, 1), :]))
        here = split(new[:, pl.ds(pl.multiple_of((p + 2) * PLANE, 128), PLANE)])
        behind = split(new[:, pl.ds(pl.multiple_of((p + 1) * PLANE, 128), PLANE)])
        old = split(raw[:, pl.ds(pl.multiple_of((p + LOW) * PLANE, 128), PLANE)])

        def stack(k):
            wrapped = jnp.concatenate([here[k][:, PLANE - NZ :], here[k][:, : PLANE - NZ]], axis=1)
            rolled = jnp.concatenate([block[k] for block in turned], axis=1)
            scaled = jnp.concatenate([block[k] for block in relaxed], axis=1)
            return jnp.concatenate([here[k], behind[k], wrapped, rolled, scaled, old[k]], axis=0)

        part = dot_t(jnp.concatenate(here, axis=0), stack(0))
        part = part[:RANK] + part[RANK:] + dot_t(here[0], stack(1))
        return t + part[:, :128], c + part[:, 128:]

    t, c = lax.fori_loop(0, OWN, body, (jnp.zeros((RANK, 128), f32), jnp.zeros((RANK, 64), f32)))
    out[:, :128] = t
    out[:, 128:] = jnp.concatenate([c, jnp.zeros((RANK, 64), f32)], axis=1)


def evolve_space(wk, moment, filled, rates):
    return call(
        evolve_space_kernel, [((RANK, (OWN + 2) * PLANE), f32), ((RANK, 256), f32)], "v" * 6,
        (wk, moment, filled[0], rates, filled[1], filled[2]),
        [pltpu.VMEM((RATES, NZ), f32)]
        + [pltpu.VMEM((RANK, PLANE), f32)] * 2
        + [pltpu.VMEM((RANK, WIDE * PLANE), f32)] * 2,
        mib=16,
    )


def finish_kernel(
    cells_total, points_total, p0, p1, p2, p3, core, kinetic, spread, space_out, fresh_core, point_out, fresh_space, fresh_point, sems
):
    both = four((p0, p1, p2, p3))
    s = both[:RANK] * (1.0 / cells_total)
    q = both[RANK:] * (1.0 / points_total)
    gram, gram_v = s[:, 0:32], q[:RANK, 0:32]
    (_, inverse), (_, inverse_v) = factor_pair(gram, gram_v)
    zeros = jnp.zeros((RANK, 32), f32)
    lane = lanes((RANK, 128))

    def wide(matrix):
        w = jnp.concatenate([matrix] * 3 + [zeros], axis=1)
        hi = w.astype(bf16).astype(f32)
        return jnp.where((lane >= 64) & (lane < 96), w - hi, hi).astype(bf16)[:, :96]

    w_space, w_point = wide(inverse), wide(inverse_v)

    def out_space(p, carry):
        for half in range(2):
            size = PLANE // 2
            at = pl.multiple_of((p + 2) * PLANE + half * size, 128)
            hi, lo = split(kinetic[:, pl.ds(at, size)])
            made = dot(w_space, jnp.concatenate([hi, lo, hi], axis=0))
            for y in range(NY // 2):
                fresh_space[pl.ds(p * NY + half * (NY // 2) + y, RANK, stride=OWN * NY), :] = made[:, y * NZ : (y + 1) * NZ]
        return carry

    lax.fori_loop(0, OWN, out_space, 0)
    copies = [pltpu.make_async_copy(fresh_space, space_out, sems.at[0])]
    copies[0].start()
    third = 2 * Q1 * HALF // 3

    def out_point(i, carry):
        at = pl.multiple_of(i * 1536, 512)
        hi, lo = split(spread[:, pl.ds(at, 1536)])
        fresh_point[:, pl.ds(at, 1536)] = dot(w_point, jnp.concatenate([hi, lo, hi], axis=0))
        return carry

    for k in range(3):
        lax.fori_loop(3 * k, 3 * k + 3, out_point, 0)
        cells = pl.ds(k * third, third)
        copies.append(pltpu.make_async_copy(fresh_point.at[:, cells], point_out.at[:, cells], sems.at[k + 1]))
        copies[-1].start()

    inverse_t = transposed(inverse)
    inverse_vt = transposed(inverse_v)
    turned = mm(inverse, s)
    turned_v = mm(inverse_v, q[:RANK])
    aux = mm(q[RANK:, 0:32], inverse_vt)
    weights_row = aux[0:1, :]
    moments_row = aux[1:2, :] + aux[2:3, :]
    left = [turned[:, 128:160]]
    for d in range(3):
        left.append(turned[:, 0:32] - turned[:, 32 * (d + 1) : 32 * (d + 2)])
    for d in range(3):
        left.append(mm_t(inverse, gram - s[:, 32 * (d + 1) : 32 * (d + 2)]))
    stack = mm(jnp.concatenate(left, axis=0), inverse_t)
    lines = [turned_v[:, 192:224], turned_v[:, 160:192], turned_v[:, 64:96]]
    lines += [-turned_v[:, 128:160], -turned_v[:, 32:64], -turned_v[:, 96:128]]
    flux = mm(jnp.concatenate(lines, axis=0), inverse_vt)
    current = mm_t(mm(turned[:, 160:192], core[...]), turned_v[:, 224:256])
    for _ in range(SUB):
        moved = mm(stack, current)
        scaled = moved[:RANK]
        change = -scaled + jnp.sum(scaled * weights_row, axis=1, keepdims=True) * moments_row
        across = jnp.concatenate([moved[(k + 1) * RANK : (k + 2) * RANK] for k in range(6)], axis=1)
        current = current + (change - mm(across, flux))
    fresh_core[...] = current
    for copy in copies:
        copy.wait()


def finish(parts, core, kinetic, spread, cells_total, points_total):
    def kernel(*refs):
        finish_kernel(cells_total, points_total, *refs)

    flat = (RANK * OWN * NY, NZ)
    return call(
        kernel, [(flat, f32), ((RANK, RANK), f32), (spread.shape, f32)], "vvvvvvv",
        (*parts, core, kinetic, spread),
        [pltpu.VMEM(flat, f32), pltpu.VMEM(spread.shape, f32), pltpu.SemaphoreType.DMA((4,))],
        mib=12, out_spaces="ava",
    )


def spread_pairs(space_part):
    moved = []
    for k in range(2):
        route = [((s ^ (2 * v + k)) * 8 + v, s * 8 + v) for s in range(16) for v in range(8)]
        moved.append(lax.ppermute(space_part, ("space", "vel"), route))
    return moved


def vel_parts(moved, point_part):
    joint = jnp.concatenate([moved[0] + moved[1], point_part], axis=0)
    pair = [(2 * z + c, 2 * z + 1 - c) for z in range(4) for c in range(2)]
    joint = joint + lax.ppermute(joint, "vel", pair)
    routes = [[(2 * z + c, 2 * ((z + d) % 4) + c) for z in range(4) for c in range(2)] for d in (1, 2, 3)]
    parts = [joint]
    for route in routes:
        parts.append(lax.ppermute(joint, "vel", route))
    return parts


def per_device(space_factor, core_matrix, velocity_factor, collision_rates):
    devices = lax.axis_size("space")
    up = [(i, (i + 1) % devices) for i in range(devices)]
    below1 = lax.ppermute(space_factor[:, OWN - 1 :], "space", up).reshape(-1, NZ)
    rates = collision_rates.reshape(-1, NZ)
    values = space_factor.reshape(-1, NZ)
    cells_total = OWN * PLANE * devices
    points_total = velocity_factor.shape[1] * lax.axis_size("vel")
    place = lax.axis_index("vel").astype(jnp.int32)
    v = place.reshape(1)
    planes = jnp.where(place % 2 == 0, space_factor[:, : OWN - 1], space_factor[:, :HIGH])
    lines = jnp.where(place % 2 == 0, collision_rates[1:], collision_rates[:HIGH])
    halo = jnp.concatenate([planes, lines[None]], axis=0)
    route = [(s * 8 + w, (s + 1 - 2 * (w % 2)) % devices * 8 + w) for s in range(devices) for w in range(8)]
    pair = [(w, w ^ 1) for w in range(8)]

    inner, own = space_sums(values, rates)
    point = point_sums(v, velocity_factor, inner)
    space, edge = edge_sums(own, below1, inner)
    moved = spread_pairs(space)
    halo, space = lax.optimization_barrier((halo, space))
    mine = lax.ppermute(halo, ("space", "vel"), route)
    parts = vel_parts(moved, point)
    mine, parts[0] = lax.optimization_barrier((mine, parts[0]))
    other = lax.ppermute(mine, "vel", pair)
    wk, wl, src, moment = small_first(parts, core_matrix, cells_total, points_total)
    filled = fill_planes(v, own, edge, mine.reshape(-1, NZ), other.reshape(-1, NZ), moment)
    kinetic, space = evolve_space(wk, moment, filled, rates)
    moved = spread_pairs(space)
    spread, point = evolve_point(v, wl, src, velocity_factor, space)
    parts = vel_parts(moved, point)
    fresh_space, fresh_core, fresh_point = finish(parts, core_matrix, kinetic, spread, cells_total, points_total)
    return fresh_space.reshape(space_factor.shape), fresh_core, fresh_point


def solution(mesh):
    return jax.shard_map(
        per_device,
        mesh=mesh,
        in_specs=(P(None, "space", None, None), P(), P(None, "vel"), P("space", None, None)),
        out_specs=(P(None, "space", None, None), P(), P(None, "vel")),
        check_vma=False,
    )
```

```python
import jax
import jax.numpy as jnp
import numpy as np
from jax import lax
from jax.experimental import pallas as pl
from jax.experimental.pallas import tpu as pltpu
from jax.sharding import PartitionSpec as P


RANK = 32
NVD = 48
SUB = 3
LOW = SUB + 1
HIGH = SUB
NY = 16
NZ = 128
OWN = 4
Q1 = 6
HALF = NVD * NVD // 2
PLANE = NY * NZ
WIDE = LOW + OWN + HIGH
ROWS_K = 7 * RANK + 16
INTERPRET = False

f32 = jnp.float32
bf16 = jnp.bfloat16


def tables():
    t = np.float32(0.25) * ((2 * np.arange(NVD) + 1).astype(np.float32) / np.float32(NVD) - np.float32(1.0))
    t = t.astype(np.float32)
    shape = np.exp(-(t.astype(np.float64) ** 2) / (2.0 * 0.125 * 0.125))
    shape = shape / shape.mean()
    plus, minus = np.maximum(t, 0), np.minimum(t, 0)
    u2, u3 = np.repeat(t, NVD), np.tile(t, NVD)
    g23 = np.repeat(shape, NVD) * np.tile(shape, NVD)
    sides = [(1, "p"), (2, "p"), (3, "p"), (1, "m"), (2, "m"), (3, "m")]
    names = [()] + [(s,) for s in sides]
    where = {(): 0}
    for k in range(6):
        where[(k,)] = k + 1
    for j in range(6):
        for k in range(j, 6):
            if k != j and sides[j][0] == sides[k][0]:
                continue
            where[(j, k)] = len(names)
            names.append((sides[j], sides[k]))
    base = np.zeros((2, 32, HALF))
    scale = np.zeros((NVD, 128))
    value = {"p": np.maximum, "m": np.minimum}
    for row, name in enumerate(names):
        b = np.ones(NVD * NVD)
        c = np.ones(NVD)
        for d, sign in name:
            if d == 1:
                c = c * value[sign](t.astype(np.float64), 0)
            elif d == 2:
                b = b * value[sign](u2.astype(np.float64), 0)
            else:
                b = b * value[sign](u3.astype(np.float64), 0)
        base[:, row] = b.reshape(2, HALF)
        scale[:, row] = c
    last = len(names)
    base[:, last] = g23.reshape(2, HALF)
    scale[:, last] = shape
    select = np.zeros((32, 7 * 128), np.float32)
    for j in range(7):
        for k in range(7):
            pair = tuple(sorted([i - 1 for i in (j, k) if i > 0]))
            if pair in where:
                select[where[pair], j * 128 + k] = 1.0
    means = np.zeros((8, 128), np.float32)
    means[:, 0] = 1.0
    means[:, 1:4] = (shape * plus).mean()
    means[:, 4:7] = (shape * minus).mean()
    rows = np.zeros((2, 8, HALF), np.float32)
    rows[:, 0] = u2.reshape(2, HALF)
    rows[:, 1] = np.maximum(u3, 0).reshape(2, HALF)
    rows[:, 2] = np.minimum(u3, 0).reshape(2, HALF)
    rows[:, 3] = g23.reshape(2, HALF)
    speeds = np.concatenate([plus, minus, shape]).astype(np.float32)
    return rows, base.astype(np.float32), scale.astype(np.float32), select, means, speeds, last


ROWS, PHI, PHI_SCALE, SELECT, MEANS, SPEEDS, LAST = tables()


def split(x):
    hi = x.astype(bf16)
    return hi, (x - hi.astype(f32)).astype(bf16)


def dot(a, b):
    return jnp.dot(a, b, preferred_element_type=f32)


def dot_t(a, b):
    return lax.dot_general(a, b, (((1,), (1,)), ((), ())), preferred_element_type=f32)


def mm(a, b, form=dot):
    rows = a.shape[0]
    ah, al = split(a)
    bh, bl = split(b)
    main = form(jnp.concatenate([ah, al], axis=0), bh)
    return main[:rows] + main[rows:] + form(ah, bl)


def mm_t(a, b):
    return mm(a, b, dot_t)


def aligned(index, size):
    return index if isinstance(index, int) else pl.multiple_of(index, size)


def lanes(shape):
    return lax.broadcasted_iota(jnp.int32, shape, len(shape) - 1)


def sublanes(shape):
    return lax.broadcasted_iota(jnp.int32, shape, len(shape) - 2)


def eye():
    return (lanes((RANK, RANK)) == sublanes((RANK, RANK))).astype(f32)


def call(kernel, outs, ins, args, scratch=(), mib=8, out_spaces=None):
    spaces = {"v": pltpu.VMEM, "s": pltpu.SMEM, "a": pl.ANY}
    out_spaces = out_spaces or "v" * len(outs)
    return pl.pallas_call(
        kernel,
        out_shape=[jax.ShapeDtypeStruct(s, d) for s, d in outs],
        in_specs=[pl.BlockSpec(memory_space=spaces[c]) for c in ins],
        out_specs=[pl.BlockSpec(memory_space=spaces[c]) for c in out_spaces],
        scratch_shapes=list(scratch),
        compiler_params=pltpu.CompilerParams(vmem_limit_bytes=mib * 1024 * 1024),
        interpret=INTERPRET,
    )(*args)


def point_tiles(first, second, y, positive, extra):
    lane = lanes((RANK, 128))
    middle = (lane >= 32) & (lane < 64)
    tile_a = first + jnp.where(middle, 0.0, second)
    y = jnp.where(lane < 32, y, 0.0)
    y = jnp.where(positive, pltpu.roll(y, 64, 1) if not INTERPRET else jnp.roll(y, 64, 1), y)
    return tile_a, jnp.where(middle, second, 0.0) + y + extra


def roll_lanes(x, shift):
    return jnp.roll(x, shift, 1) if INTERPRET else pltpu.roll(x, shift % x.shape[1], 1)


def stacked(values, rows, h):
    return jnp.concatenate(
        [values, values * rows[h, 0:1, :], values * rows[h, 1:2, :], values * rows[h, 2:3, :]], axis=0
    )


def point_sums_kernel(low, high, v_ref, speeds, rows, phi, scale, values, after, out):
    q0 = v_ref[0] * Q1
    phi_parts = [split(phi[h]) for h in range(2)]

    def body(b, carry):
        sums, y, moments = list(carry[:2]), carry[2], carry[3]
        u = speeds[q0 + b] + speeds[NVD + q0 + b]
        for h in range(2):
            start = aligned(b * (2 * HALF) + h * HALF, 128)
            sh, sl = split(stacked(values[:, pl.ds(start, HALF)], rows, h))
            lh, ll = sh[:RANK], sl[:RANK]
            ph, plo = phi_parts[h]
            both = jnp.concatenate([lh, ll], axis=0)
            t = dot_t(both, jnp.concatenate([sh, ph], axis=0))
            t = t[:RANK] + t[RANK:] + dot_t(lh, jnp.concatenate([sl, plo], axis=0))
            t, m = t[:, :128], t[:, 128:]
            sums[h] = sums[h] + t
            y = y + u * t
            moments = moments + m * scale[pl.ds(q0 + b, 1), :RANK]
        return sums[0], sums[1], y, moments

    zero = jnp.zeros((RANK, 128), f32)
    first, second, y, moments = lax.fori_loop(low, high, body, (zero, zero, zero, jnp.zeros((RANK, RANK), f32)))
    moments = jnp.concatenate([jnp.zeros((RANK, 96), f32), moments], axis=1)
    tile_a, tile_b = point_tiles(first, second, y, v_ref[0] >= 4, moments)
    if low > 0:
        tile_a, tile_b = tile_a + after[:, :128], tile_b + after[:, 128:]
    out[:, :128] = tile_a
    out[:, 128:] = tile_b


def point_sums(v, values, low, high, after):
    def kernel(*refs):
        point_sums_kernel(low, high, *refs)

    return call(
        kernel, [((RANK, 256), f32)], "ssvvvvv",
        (v, SPEEDS, ROWS, PHI, PHI_SCALE, values, after), mib=12,
    )[0]


def space_sums_kernel(values, rates, out, own, hi, lo, zh, zl, ch, cl):
    def load(p, carry):
        for y in range(NY):
            block = values[pl.ds(p * NY + y, RANK, stride=OWN * NY), :]
            at = aligned(p * PLANE + y * NZ, 128)
            a, b = split(block)
            hi[:, pl.ds(at + PLANE, NZ)] = a
            lo[:, pl.ds(at + PLANE, NZ)] = b
            own[:, pl.ds(at, NZ)] = block
            a, b = split(roll_lanes(block, 1))
            zh[:, pl.ds(at, NZ)] = a
            zl[:, pl.ds(at, NZ)] = b
            a, b = split(block * rates[pl.ds(p * NY + y, 1), :])
            ch[:, pl.ds(at, NZ)] = a
            cl[:, pl.ds(at, NZ)] = b
        return carry

    hi[:, :PLANE] = jnp.zeros((RANK, PLANE), bf16)
    lo[:, :PLANE] = jnp.zeros((RANK, PLANE), bf16)
    lax.fori_loop(0, OWN, load, 0)

    def body(p, carry):
        t, c = carry
        at = aligned(p * PLANE, 128)

        def stack(main, turned):
            here = main[:, pl.ds(at + PLANE, PLANE)]
            wrapped = jnp.concatenate([here[:, PLANE - NZ :], here[:, : PLANE - NZ]], axis=1)
            return jnp.concatenate(
                [here, main[:, pl.ds(at, PLANE)], wrapped, turned[:, pl.ds(at, PLANE)]], axis=0
            )

        sh, sl = stack(hi, zh), stack(lo, zl)
        both = jnp.concatenate([sh[:RANK], sl[:RANK]], axis=0)
        part = dot_t(both, jnp.concatenate([sh, ch[:, pl.ds(at, PLANE)]], axis=0))
        part = part[:RANK] + part[RANK:] + dot_t(sh[:RANK], jnp.concatenate([sl, cl[:, pl.ds(at, PLANE)]], axis=0))
        return t + part[:, :128], c + part[:, 128:]

    t, c = lax.fori_loop(0, OWN, body, (jnp.zeros((RANK, 128), f32), jnp.zeros((RANK, RANK), f32)))
    out[:, :128] = t
    out[:, 128:] = jnp.concatenate([c, jnp.zeros((RANK, 96), f32)], axis=1)


def space_sums(values, rates):
    own = (RANK, OWN * PLANE)
    return call(
        space_sums_kernel, [((RANK, 256), f32), (own, f32)], "vv", (values, rates),
        [pltpu.VMEM((RANK, (OWN + 1) * PLANE), bf16)] * 2 + [pltpu.VMEM(own, bf16)] * 4, mib=12,
    )


def edge_sums_kernel(own, below, inner, out, edge):
    empty = jnp.zeros((RANK, PLANE), bf16)
    other = jnp.concatenate([below[pl.ds(y, RANK, stride=NY), :] for y in range(NY)], axis=1)
    edge[...] = other
    oh, ol = split(other)
    lh, ll = split(own[:, :PLANE])
    part = dot_t(jnp.concatenate([lh, ll], axis=0), jnp.concatenate([empty, oh], axis=0))
    t = part[:RANK] + part[RANK:] + dot_t(lh, jnp.concatenate([empty, ol], axis=0))
    out[:, :128] = inner[:, :128] + jnp.concatenate([t, jnp.zeros((RANK, 64), f32)], axis=1)
    out[:, 128:] = inner[:, 128:]


def edge_sums(own, below, inner):
    return call(edge_sums_kernel, [((RANK, 256), f32), ((RANK, PLANE), f32)], "vvv", (own, below, inner))


def factor_pair(first, second):
    zeros = jnp.zeros((RANK, 64), f32)
    works = [jnp.concatenate([g, eye(), zeros], axis=1) for g in (first, second)]
    pivots = [jnp.ones((RANK, 128), f32)] * 2
    row = sublanes((RANK, 128))
    for k in range(0, RANK, 2):
        for n in range(2):
            w = works[n]
            c0 = jnp.broadcast_to(w[:, k : k + 1], (RANK, 128))
            c1 = jnp.broadcast_to(w[:, k + 1 : k + 2], (RANK, 128))
            r0, r1 = w[k : k + 1, :], w[k + 1 : k + 2, :]
            a, b, d = c0[k : k + 1, :], c1[k : k + 1, :], c1[k + 1 : k + 2, :]
            over = 1.0 / a
            ratio = b * over
            d = d - b * ratio
            r1 = r1 - ratio * r0
            c1 = c1 - ratio * c0
            step = w - c0 * (r0 * over) - c1 * (r1 * (1.0 / d))
            works[n] = jnp.where(row > k + 1, step, jnp.where(row == k + 1, r1, w))
            pivots[n] = jnp.where(row == k, a, jnp.where(row == k + 1, d, pivots[n]))
    done = [works[n] * lax.rsqrt(pivots[n]) for n in range(2)]
    return [(w[:, :RANK], w[:, RANK : 2 * RANK]) for w in done]


def transposed(x):
    return mm_t(eye(), x)


def point_blocks(tiles, points_total):
    t = tiles * (1.0 / points_total)
    gram = t[:, 0:32]
    plus = [t[:, 192:224], t[:, 160:192], t[:, 64:96]]
    minus = [t[:, 128:160], t[:, 32:64], t[:, 96:128]]
    return gram, plus, minus, t[:, 224:256]


def four(parts):
    return (parts[0][...] + parts[2][...]) + (parts[1][...] + parts[3][...])


def small_first_kernel(cells_total, points_total, p0, p1, p2, p3, core, select, means, wk, wl, src, moment):
    both = four((p0, p1, p2, p3))
    s = both[:RANK] * (1.0 / cells_total)
    gram = s[:, 0:32]
    gram_v, _, _, raw = point_blocks(both[RANK:], points_total)
    (upper, inverse), (upper_v, inverse_v) = factor_pair(gram, gram_v)
    identity = eye()
    raw_a = [gram - s[:, 32 * (d + 1) : 32 * (d + 2)] for d in range(3)]
    to_spread = mm(upper, core[...])
    to_kinetic_t = mm_t(core[...], upper_v)
    zeros = jnp.zeros((RANK, 32), f32)
    inverse_t = transposed(inverse)
    triple = jnp.concatenate([inverse_t] * 3 + [zeros], axis=1)
    left = (
        [mm(inverse, s[:, 128:160])] + [mm(inverse, a) for a in raw_a] + [mm_t(inverse, a) for a in raw_a]
    )
    turned = mm(jnp.concatenate(left, axis=0), triple)
    one = jnp.concatenate([identity] * 3 + [zeros], axis=1)
    e_wide = turned[:RANK]
    mixers = [one - e_wide] + [-turned[RANK * (d + 1) : RANK * (d + 2)] for d in range(3)]
    mixers = mixers + [turned[RANK * (d + 4) : RANK * (d + 5)] for d in range(3)]
    stack = jnp.concatenate(mixers, axis=0)
    wl[1] = stack
    wl[0] = mm(stack[:, :RANK], jnp.concatenate([to_spread] * 3 + [zeros], axis=1))
    square = [m[:, :RANK] for m in mixers]
    e = e_wide[:, :RANK]
    moved = mm(mm(to_spread, raw), select[...])
    groups = [moved[:, 128 * j : 128 * (j + 1)] for j in range(7)]
    lane = lanes((RANK, 128))
    source = [mm(e, groups[0])[:, 0:1]]
    following = mm(square[0], groups[0]) + source[0] * means[0:1, :]
    for j in range(1, 7):
        following = following + mm(square[j], groups[j])
    source.append(mm(e, following)[:, 0:1])
    third = mm(square[0], jnp.where(lane == 0, following, 0.0))
    for j in range(1, 7):
        third = third + mm(square[j], jnp.where(lane == j, following, 0.0))
    third = jnp.sum(third, axis=1, keepdims=True) + source[1] * means[0:1, 0:1]
    source.append(mm(e, jnp.broadcast_to(third, (RANK, 128)))[:, 0:1])
    for n in range(3):
        src[n] = jnp.broadcast_to(source[n], (RANK, 128))
    half = mm(inverse_v, both[RANK:, :] * (1.0 / points_total))
    turned_raw = half[:, 224:256]
    weights_row = transposed(turned_raw)[0:1, :]
    blocks = [half[:, 192:224], half[:, 128:160], half[:, 160:192], half[:, 32:64], half[:, 64:96], half[:, 96:128]]
    flux = mm(jnp.concatenate(blocks, axis=0), transposed(inverse_v))
    flux = [flux[k * RANK : (k + 1) * RANK] * (1.0 if k % 2 == 0 else -1.0) for k in range(6)]
    row = sublanes((16, RANK))
    column = jnp.concatenate([identity] + flux + [jnp.where(row == 0, weights_row, 0.0)], axis=0)
    to_kinetic = transposed(to_kinetic_t)
    wk[0] = mm(column, jnp.concatenate([to_kinetic] * 3 + [zeros], axis=1))
    wk[1] = jnp.concatenate([column] * 3 + [jnp.zeros((ROWS_K, 32), f32)], axis=1)
    moment[...] = jnp.broadcast_to(turned_raw[:, LAST : LAST + 1], (RANK, 128))


def small_first(parts, core, cells_total, points_total):
    def kernel(*refs):
        small_first_kernel(cells_total, points_total, *refs)

    return call(
        kernel, [((2, ROWS_K, 128), f32), ((2, 224, 128), f32), ((3, RANK, 128), f32), ((RANK, 128), f32)], "vvvvvvv",
        (*parts, core, SELECT, MEANS),
    )


def evolve_point_kernel(v_ref, speeds, rows, wl, src, values, after, new, out):
    q0 = v_ref[0] * Q1
    lane_w = lanes((RANK, 128))
    low_lane = (lane_w >= 64) & (lane_w < 96)

    def weights_of(w):
        hi = w.astype(bf16).astype(f32)
        return jnp.where(low_lane, w - hi, hi).astype(bf16)

    def piece(kind, n):
        return wl[kind, n * RANK : (n + 1) * RANK, :]

    fixed = [jnp.concatenate([weights_of(piece(kind, n)) for n in (3, 6)], axis=0) for kind in range(2)]
    turning = [[weights_of(piece(kind, n)) for n in (5, 2)] for kind in range(2)]
    aux = []
    for h in range(2):
        gh, gl = split(rows[h, 3:4, :])
        row = sublanes((16, HALF))
        gh, gl = gh.astype(f32), gl.astype(f32)
        aux.append(jnp.where(row == 0, 1.0, jnp.where(row == 1, gh, jnp.where(row == 2, gl, 0.0))).astype(bf16))
    inside = HALF // 256 * 256
    cuts = [(0, inside, (0,)), (inside, 2 * HALF - inside, (0, 1)), (2 * HALF - inside, 2 * HALF, (1,))]

    def body(b, carry):
        sums, y, cross, ones_sum = list(carry[:2]), carry[2], carry[3], carry[4]
        up = speeds[q0 + b]
        um = speeds[NVD + q0 + b]
        g1 = speeds[2 * NVD + q0 + b]
        u = up + um
        moving = [piece(kind, 0) + up * piece(kind, 1) + um * piece(kind, 4) for kind in range(2)]
        heads = [weights_of(m) for m in moving]
        first = aligned(b * (2 * HALF), 128)
        states = [values[:, pl.ds(first, HALF)], values[:, pl.ds(first + HALF, HALF)]]
        raws = [split(state) for state in states]
        for n in range(SUB):
            kind = min(n, 1)
            parts = raws if n == 0 else [split(state) for state in states]
            operand = jnp.concatenate(
                [jnp.concatenate([parts[0][k], parts[1][k]], axis=1) for k in (0, 1, 0)], axis=0
            )
            source = src[n] * g1
            mixed = []
            for low, high, sides in cuts:
                w = jnp.concatenate([heads[kind], fixed[kind]] + [turning[kind][h] for h in sides], axis=0)[:, :96]
                mixed.append(dot(w, operand[:, low:high]))
            rest = HALF - inside
            middle = mixed[1]
            ends = [
                jnp.concatenate([mixed[0], middle[: 4 * RANK, :rest]], axis=1),
                jnp.concatenate([jnp.concatenate([middle[: 3 * RANK, rest:], middle[4 * RANK :, rest:]], axis=0), mixed[2]], axis=1),
            ]
            states = [
                ends[h][:RANK]
                + rows[h, 3:4, :] * source[:, 0:1]
                + rows[h, 1:2, :] * ends[h][RANK : 2 * RANK]
                + rows[h, 2:3, :] * ends[h][2 * RANK : 3 * RANK]
                + rows[h, 0:1, :] * ends[h][3 * RANK :]
                for h in range(2)
            ]
        for h in range(2):
            start = aligned(b * (2 * HALF) + h * HALF, 128)
            state = states[h]
            raw_hi, raw_lo = raws[h]
            new[:, pl.ds(start, HALF)] = state
            sh, sl = split(stacked(state, rows, h))
            lh, ll = sh[:RANK], sl[:RANK]
            t = dot_t(jnp.concatenate([lh, ll, aux[h]], axis=0), jnp.concatenate([sh, raw_hi], axis=0))
            t2 = dot_t(jnp.concatenate([lh, aux[h]], axis=0), jnp.concatenate([sl, raw_lo], axis=0))
            t_main = t[:RANK] + t[RANK : 2 * RANK] + t2[:RANK]
            cross = cross + t_main[:, 128:]
            t_main = t_main[:, :128]
            a = t[2 * RANK : 2 * RANK + 8, :128]
            a2 = t2[RANK : RANK + 8, :128]
            row8 = sublanes((8, 128))
            a = a + jnp.where(row8 < 2, a2, 0.0)
            ones_sum = ones_sum + jnp.where(row8 == 0, a, a * g1)
            sums[h] = sums[h] + t_main
            y = y + u * t_main
        return sums[0], sums[1], y, cross, ones_sum

    zero = jnp.zeros((RANK, 128), f32)
    first, second, y, cross, ones_sum = lax.fori_loop(
        0, Q1, body, (zero, zero, zero, jnp.zeros((RANK, RANK), f32), jnp.zeros((8, 128), f32))
    )
    cross = jnp.concatenate([jnp.zeros((RANK, 96), f32), cross], axis=1)
    tile_a, tile_b = point_tiles(first, second, y, v_ref[0] >= 4, cross)
    out[:RANK, :128] = tile_a
    out[:RANK, 128:] = tile_b
    out[RANK:, :128] = ones_sum
    out[RANK:, 128:] = jnp.zeros((8, 128), f32)


def evolve_point(v, wl, src, values, after):
    return call(
        evolve_point_kernel, [(values.shape, f32), ((RANK + 8, 256), f32)], "ssvvvva",
        (v, SPEEDS, ROWS, wl, src, values, after), mib=16,
    )


RATES = (LOW - 1 + OWN + HIGH - 1) * NY
HALO = RANK * HIGH * NY


def fill_kernel(v_ref, own, edge, mine, other, after, state, rates_low, rates_high):
    core = v_ref[0] % 2
    state[:, LOW * PLANE : (LOW + OWN) * PLANE] = own[...]
    state[:, (LOW - 1) * PLANE : LOW * PLANE] = edge[...]
    for source, place in ((mine, core), (other, 1 - core)):

        def load(p, carry, source=source, place=place):
            for y in range(NY):
                at = aligned((p + place * (LOW + OWN)) * PLANE + y * NZ, 128)
                state[:, pl.ds(at, NZ)] = source[pl.ds(p * NY + y, RANK, stride=HIGH * NY), :]
            return carry

        lax.fori_loop(0, HIGH, load, 0)
    first, second = mine[HALO:, :], other[HALO:, :]
    rates_low[...] = jnp.where(core == 0, first, second)
    rates_high[...] = jnp.where(core == 0, second, first)


def fill_planes(v, own, edge, mine, other, after):
    part = ((HIGH * NY, NZ), f32)
    return call(
        fill_kernel, [((RANK, WIDE * PLANE), f32), part, part], "svvvva", (v, own, edge, mine, other, after),
        mib=12,
    )


def evolve_space_kernel(wk, moment, raw, rates, rates_low, rates_high, new, out, rates_all, partial, passed, *bufs):
    sources, targets = [raw, bufs[0], bufs[1]], [bufs[0], bufs[1], new]
    low, own = (LOW - 1) * NY, OWN * NY
    rates_all[:low, :] = rates_low[...]
    rates_all[low : low + own, :] = rates[...]
    rates_all[low + own :, :] = rates_high[: (HIGH - 1) * NY, :]
    lane = lanes((ROWS_K, 128))
    low_lane = (lane >= 64) & (lane < 96)

    for n in range(SUB):
        w = wk[min(n, 1)]
        w_hi = w.astype(bf16).astype(f32)
        w = jnp.where(low_lane, w - w_hi, w_hi).astype(bf16)[:, :96]
        if n > 0:
            w = w[RANK:]
        skip = w.shape[0] - ROWS_K + RANK
        src, dst = sources[n], targets[n]
        shift = 2 if n == SUB - 1 else 0
        begin, end = 1 + n, WIDE - 1 - n

        def tile(t, j, src=src):
            cells = src[:, pl.ds(aligned(t * PLANE + j * 256, 256), 256)]
            a, b = split(cells)
            return cells, jnp.concatenate([a, b, a], axis=0)

        def put(t, y, block, dst=dst, shift=shift):
            dst[:, pl.ds(aligned((t - shift) * PLANE + y * NZ, 128), NZ)] = block

        def step(t, carry, w=w, tile=tile, put=put, skip=skip):
            scale = moment[...]
            bases, ups, downs = [], [], []
            for j in range(NY // 2):
                cells, operand = tile(t, j)
                mixed = dot(w, operand)
                for i in range(2):
                    y = 2 * j + i
                    cell = slice(y * NZ, (y + 1) * NZ)
                    half = slice(i * NZ, (i + 1) * NZ)
                    part = [mixed[skip + k * RANK : skip + (k + 1) * RANK, half] for k in range(6)]
                    here = mixed[:RANK, half] if skip else cells[:, half]
                    density = mixed[skip + 6 * RANK : skip + 6 * RANK + 1, half]
                    put(t - 1, y, partial[:, cell] + part[1])
                    rate = rates_all[pl.ds((t - 1) * NY + y, 1), :]
                    base = here + rate * (scale * density - here) + passed[:, cell]
                    passed[:, cell] = part[0]
                    base = base - ((part[0] + part[1]) + (part[2] + part[3]) + (part[4] + part[5]))
                    bases.append(base + roll_lanes(part[4], 1) + roll_lanes(part[5], -1))
                    ups.append(part[2])
                    downs.append(part[3])
                    if y >= 2:
                        partial[:, (y - 1) * NZ : y * NZ] = bases[y - 1] + ups[y - 2] + downs[y]
            partial[:, (NY - 1) * NZ :] = bases[NY - 1] + ups[NY - 2] + downs[0]
            partial[:, :NZ] = bases[0] + ups[NY - 1] + downs[1]
            return carry

        for j in range(NY // 2):
            passed[:, j * 256 : (j + 1) * 256] = dot(w[skip : skip + RANK], tile(begin - 1, j)[1])
        for t in range(begin, end):
            step(t, 0)
        for j in range(NY // 2):
            mixed = dot(w[skip + RANK : skip + 2 * RANK], tile(end, j)[1])
            for i in range(2):
                y = 2 * j + i
                put(end - 1, y, partial[:, y * NZ : (y + 1) * NZ] + mixed[:, i * NZ : (i + 1) * NZ])

    def body(p, carry):
        t, c = carry
        turned, relaxed = [], []
        for y in range(NY):
            block = new[:, pl.ds(aligned((p + 2) * PLANE + y * NZ, 128), NZ)]
            turned.append(split(roll_lanes(block, 1)))
            relaxed.append(split(block * rates[pl.ds(p * NY + y, 1), :]))
        here = split(new[:, pl.ds(aligned((p + 2) * PLANE, 128), PLANE)])
        behind = split(new[:, pl.ds(aligned((p + 1) * PLANE, 128), PLANE)])
        old = split(raw[:, pl.ds(aligned((p + LOW) * PLANE, 128), PLANE)])

        def stack(k):
            wrapped = jnp.concatenate([here[k][:, PLANE - NZ :], here[k][:, : PLANE - NZ]], axis=1)
            rolled = jnp.concatenate([block[k] for block in turned], axis=1)
            scaled = jnp.concatenate([block[k] for block in relaxed], axis=1)
            return jnp.concatenate([here[k], behind[k], wrapped, rolled, scaled, old[k]], axis=0)

        part = dot_t(jnp.concatenate(here, axis=0), stack(0))
        part = part[:RANK] + part[RANK:] + dot_t(here[0], stack(1))
        return t + part[:, :128], c + part[:, 128:]

    carry = (jnp.zeros((RANK, 128), f32), jnp.zeros((RANK, 64), f32))
    for p in range(OWN):
        carry = body(p, carry)
    t, c = carry
    out[:, :128] = t
    out[:, 128:] = jnp.concatenate([c, jnp.zeros((RANK, 64), f32)], axis=1)


def evolve_space(wk, moment, filled, rates):
    return call(
        evolve_space_kernel, [((RANK, (OWN + 2) * PLANE), f32), ((RANK, 256), f32)], "v" * 6,
        (wk, moment, filled[0], rates, filled[1], filled[2]),
        [pltpu.VMEM((RATES, NZ), f32)]
        + [pltpu.VMEM((RANK, PLANE), f32)] * 2
        + [pltpu.VMEM((RANK, WIDE * PLANE), f32)] * 2,
        mib=16,
    )


def finish_kernel(
    cells_total, points_total, p0, p1, p2, p3, core, kinetic, spread, space_out, fresh_core, point_out, fresh_space, fresh_point, sems
):
    both = four((p0, p1, p2, p3))
    s = both[:RANK] * (1.0 / cells_total)
    q = both[RANK:] * (1.0 / points_total)
    gram, gram_v = s[:, 0:32], q[:RANK, 0:32]
    (_, inverse), (_, inverse_v) = factor_pair(gram, gram_v)
    zeros = jnp.zeros((RANK, 32), f32)
    lane = lanes((RANK, 128))

    def wide(matrix):
        w = jnp.concatenate([matrix] * 3 + [zeros], axis=1)
        hi = w.astype(bf16).astype(f32)
        return jnp.where((lane >= 64) & (lane < 96), w - hi, hi).astype(bf16)[:, :96]

    w_space, w_point = wide(inverse), wide(inverse_v)

    def out_space(p, carry):
        for half in range(2):
            size = PLANE // 2
            at = aligned((p + 2) * PLANE + half * size, 128)
            hi, lo = split(kinetic[:, pl.ds(at, size)])
            made = dot(w_space, jnp.concatenate([hi, lo, hi], axis=0))
            for y in range(NY // 2):
                fresh_space[pl.ds(p * NY + half * (NY // 2) + y, RANK, stride=OWN * NY), :] = made[:, y * NZ : (y + 1) * NZ]
        return carry

    third = 2 * Q1 * HALF // 3
    copies = []

    def out_point(i, carry):
        at = aligned(i * 1536, 512)
        hi, lo = split(spread[:, pl.ds(at, 1536)])
        fresh_point[:, pl.ds(at, 1536)] = dot(w_point, jnp.concatenate([hi, lo, hi], axis=0))
        return carry

    for k in range(3):
        lax.fori_loop(3 * k, 3 * k + 3, out_point, 0)
        cells = pl.ds(k * third, third)
        copies.append(pltpu.make_async_copy(fresh_point.at[:, cells], point_out.at[:, cells], sems.at[k + 1]))
        copies[-1].start()

    lax.fori_loop(0, OWN, out_space, 0)
    copies.append(pltpu.make_async_copy(fresh_space, space_out, sems.at[0]))
    copies[-1].start()

    inverse_t = transposed(inverse)
    inverse_vt = transposed(inverse_v)
    turned = mm(inverse, s)
    turned_v = mm(inverse_v, q[:RANK])
    aux = mm(q[RANK:, 0:32], inverse_vt)
    weights_row = aux[0:1, :]
    moments_row = aux[1:2, :] + aux[2:3, :]
    left = [turned[:, 128:160]]
    for d in range(3):
        left.append(turned[:, 0:32] - turned[:, 32 * (d + 1) : 32 * (d + 2)])
    for d in range(3):
        left.append(mm_t(inverse, gram - s[:, 32 * (d + 1) : 32 * (d + 2)]))
    stack = mm(jnp.concatenate(left, axis=0), inverse_t)
    lines = [turned_v[:, 192:224], turned_v[:, 160:192], turned_v[:, 64:96]]
    lines += [-turned_v[:, 128:160], -turned_v[:, 32:64], -turned_v[:, 96:128]]
    flux = mm(jnp.concatenate(lines, axis=0), inverse_vt)
    current = mm_t(mm(turned[:, 160:192], core[...]), turned_v[:, 224:256])
    for _ in range(SUB):
        moved = mm(stack, current)
        scaled = moved[:RANK]
        change = -scaled + jnp.sum(scaled * weights_row, axis=1, keepdims=True) * moments_row
        across = jnp.concatenate([moved[(k + 1) * RANK : (k + 2) * RANK] for k in range(6)], axis=1)
        current = current + (change - mm(across, flux))
    fresh_core[...] = current
    for copy in copies:
        copy.wait()


def finish(parts, core, kinetic, spread, cells_total, points_total):
    def kernel(*refs):
        finish_kernel(cells_total, points_total, *refs)

    flat = (RANK * OWN * NY, NZ)
    return call(
        kernel, [(flat, f32), ((RANK, RANK), f32), (spread.shape, f32)], "vvvvvvv",
        (*parts, core, kinetic, spread),
        [pltpu.VMEM(flat, f32), pltpu.VMEM(spread.shape, f32), pltpu.SemaphoreType.DMA((4,))],
        mib=12, out_spaces="ava",
    )


def spread_pairs(space_part):
    moved = []
    for k in range(2):
        route = [((s ^ (2 * v + k)) * 8 + v, s * 8 + v) for s in range(16) for v in range(8)]
        moved.append(lax.ppermute(space_part, ("space", "vel"), route))
    return moved


def vel_parts(moved, point_part):
    joint = jnp.concatenate([moved[0] + moved[1], point_part], axis=0)
    pair = [(2 * z + c, 2 * z + 1 - c) for z in range(4) for c in range(2)]
    joint = joint + lax.ppermute(joint, "vel", pair)
    routes = [[(2 * z + c, 2 * ((z + d) % 4) + c) for z in range(4) for c in range(2)] for d in (1, 2, 3)]
    parts = [joint]
    for route in routes:
        parts.append(lax.ppermute(joint, "vel", route))
    return parts


def per_device(space_factor, core_matrix, velocity_factor, collision_rates):
    devices = lax.axis_size("space")
    up = [(i, (i + 1) % devices) for i in range(devices)]
    below1 = lax.ppermute(space_factor[:, OWN - 1 :], "space", up).reshape(-1, NZ)
    rates = collision_rates.reshape(-1, NZ)
    values = space_factor.reshape(-1, NZ)
    cells_total = OWN * PLANE * devices
    points_total = velocity_factor.shape[1] * lax.axis_size("vel")
    place = lax.axis_index("vel").astype(jnp.int32)
    v = place.reshape(1)
    planes = jnp.where(place % 2 == 0, space_factor[:, : OWN - 1], space_factor[:, :HIGH])
    lines = jnp.where(place % 2 == 0, collision_rates[1:], collision_rates[:HIGH])
    halo = jnp.concatenate([planes, lines[None]], axis=0)
    route = [(s * 8 + w, (s + 1 - 2 * (w % 2)) % devices * 8 + w) for s in range(devices) for w in range(8)]
    pair = [(w, w ^ 1) for w in range(8)]

    inner, own = space_sums(values, rates)
    point = point_sums(v, velocity_factor, 0, Q1 // 2, inner)
    space, edge = edge_sums(own, below1, inner)
    moved = spread_pairs(space)
    halo, space = lax.optimization_barrier((halo, space))
    mine = lax.ppermute(halo, ("space", "vel"), route)
    point = point_sums(v, velocity_factor, Q1 // 2, Q1, point)
    parts = vel_parts(moved, point)
    mine, parts[0] = lax.optimization_barrier((mine, parts[0]))
    other = lax.ppermute(mine, "vel", pair)
    wk, wl, src, moment = small_first(parts, core_matrix, cells_total, points_total)
    filled = fill_planes(v, own, edge, mine.reshape(-1, NZ), other.reshape(-1, NZ), moment)
    kinetic, space = evolve_space(wk, moment, filled, rates)
    moved = spread_pairs(space)
    spread, point = evolve_point(v, wl, src, velocity_factor, space)
    parts = vel_parts(moved, point)
    fresh_space, fresh_core, fresh_point = finish(parts, core_matrix, kinetic, spread, cells_total, points_total)
    return fresh_space.reshape(space_factor.shape), fresh_core, fresh_point


def solution(mesh):
    return jax.shard_map(
        per_device,
        mesh=mesh,
        in_specs=(P(None, "space", None, None), P(), P(None, "vel"), P("space", None, None)),
        out_specs=(P(None, "space", None, None), P(), P(None, "vel")),
        check_vma=False,
    )
```

```python
import jax
import jax.numpy as jnp
import numpy as np
from jax import lax
from jax.experimental import pallas as pl
from jax.experimental.pallas import tpu as pltpu
from jax.sharding import PartitionSpec as P


RANK = 32
NVD = 48
SUB = 3
LOW = SUB + 1
HIGH = SUB
NY = 16
NZ = 128
OWN = 4
Q1 = 6
HALF = NVD * NVD // 2
PLANE = NY * NZ
WIDE = LOW + OWN + HIGH
ROWS_K = 7 * RANK + 16
INTERPRET = False

f32 = jnp.float32
bf16 = jnp.bfloat16


def tables():
    t = np.float32(0.25) * ((2 * np.arange(NVD) + 1).astype(np.float32) / np.float32(NVD) - np.float32(1.0))
    t = t.astype(np.float32)
    shape = np.exp(-(t.astype(np.float64) ** 2) / (2.0 * 0.125 * 0.125))
    shape = shape / shape.mean()
    plus, minus = np.maximum(t, 0), np.minimum(t, 0)
    u2, u3 = np.repeat(t, NVD), np.tile(t, NVD)
    g23 = np.repeat(shape, NVD) * np.tile(shape, NVD)
    sides = [(1, "p"), (2, "p"), (3, "p"), (1, "m"), (2, "m"), (3, "m")]
    names = [()] + [(s,) for s in sides]
    where = {(): 0}
    for k in range(6):
        where[(k,)] = k + 1
    for j in range(6):
        for k in range(j, 6):
            if k != j and sides[j][0] == sides[k][0]:
                continue
            where[(j, k)] = len(names)
            names.append((sides[j], sides[k]))
    base = np.zeros((2, 32, HALF))
    scale = np.zeros((NVD, 128))
    value = {"p": np.maximum, "m": np.minimum}
    for row, name in enumerate(names):
        b = np.ones(NVD * NVD)
        c = np.ones(NVD)
        for d, sign in name:
            if d == 1:
                c = c * value[sign](t.astype(np.float64), 0)
            elif d == 2:
                b = b * value[sign](u2.astype(np.float64), 0)
            else:
                b = b * value[sign](u3.astype(np.float64), 0)
        base[:, row] = b.reshape(2, HALF)
        scale[:, row] = c
    last = len(names)
    base[:, last] = g23.reshape(2, HALF)
    scale[:, last] = shape
    select = np.zeros((32, 7 * 128), np.float32)
    for j in range(7):
        for k in range(7):
            pair = tuple(sorted([i - 1 for i in (j, k) if i > 0]))
            if pair in where:
                select[where[pair], j * 128 + k] = 1.0
    means = np.zeros((8, 128), np.float32)
    means[:, 0] = 1.0
    means[:, 1:4] = (shape * plus).mean()
    means[:, 4:7] = (shape * minus).mean()
    rows = np.zeros((2, 8, HALF), np.float32)
    rows[:, 0] = u2.reshape(2, HALF)
    rows[:, 1] = np.maximum(u3, 0).reshape(2, HALF)
    rows[:, 2] = np.minimum(u3, 0).reshape(2, HALF)
    rows[:, 3] = g23.reshape(2, HALF)
    speeds = np.concatenate([plus, minus, shape]).astype(np.float32)
    return rows, base.astype(np.float32), scale.astype(np.float32), select, means, speeds, last


ROWS, PHI, PHI_SCALE, SELECT, MEANS, SPEEDS, LAST = tables()


def split(x):
    hi = x.astype(bf16)
    return hi, (x - hi.astype(f32)).astype(bf16)


def dot(a, b):
    return jnp.dot(a, b, preferred_element_type=f32)


def dot_t(a, b):
    return lax.dot_general(a, b, (((1,), (1,)), ((), ())), preferred_element_type=f32)


def mm(a, b, form=dot):
    rows = a.shape[0]
    ah, al = split(a)
    bh, bl = split(b)
    main = form(jnp.concatenate([ah, al], axis=0), bh)
    return main[:rows] + main[rows:] + form(ah, bl)


def mm_t(a, b):
    return mm(a, b, dot_t)


def aligned(index, size):
    return index if isinstance(index, int) else pl.multiple_of(index, size)


def lanes(shape):
    return lax.broadcasted_iota(jnp.int32, shape, len(shape) - 1)


def sublanes(shape):
    return lax.broadcasted_iota(jnp.int32, shape, len(shape) - 2)


def eye():
    return (lanes((RANK, RANK)) == sublanes((RANK, RANK))).astype(f32)


def call(kernel, outs, ins, args, scratch=(), mib=8, out_spaces=None):
    spaces = {"v": pltpu.VMEM, "s": pltpu.SMEM, "a": pl.ANY}
    out_spaces = out_spaces or "v" * len(outs)
    return pl.pallas_call(
        kernel,
        out_shape=[jax.ShapeDtypeStruct(s, d) for s, d in outs],
        in_specs=[pl.BlockSpec(memory_space=spaces[c]) for c in ins],
        out_specs=[pl.BlockSpec(memory_space=spaces[c]) for c in out_spaces],
        scratch_shapes=list(scratch),
        compiler_params=pltpu.CompilerParams(vmem_limit_bytes=mib * 1024 * 1024),
        interpret=INTERPRET,
    )(*args)


def point_tiles(first, second, y, positive, extra):
    lane = lanes((RANK, 128))
    middle = (lane >= 32) & (lane < 64)
    tile_a = first + jnp.where(middle, 0.0, second)
    y = jnp.where(lane < 32, y, 0.0)
    y = jnp.where(positive, pltpu.roll(y, 64, 1) if not INTERPRET else jnp.roll(y, 64, 1), y)
    return tile_a, jnp.where(middle, second, 0.0) + y + extra


def roll_lanes(x, shift):
    return jnp.roll(x, shift, 1) if INTERPRET else pltpu.roll(x, shift % x.shape[1], 1)


def stacked(values, rows, h):
    return jnp.concatenate(
        [values, values * rows[h, 0:1, :], values * rows[h, 1:2, :], values * rows[h, 2:3, :]], axis=0
    )


def point_sums_kernel(low, high, v_ref, speeds, rows, phi, scale, values, after, out):
    q0 = v_ref[0] * Q1
    phi_parts = [split(phi[h]) for h in range(2)]

    def body(b, carry):
        sums, y, moments = list(carry[:2]), carry[2], carry[3]
        u = speeds[q0 + b] + speeds[NVD + q0 + b]
        for h in range(2):
            start = aligned(b * (2 * HALF) + h * HALF, 128)
            sh, sl = split(stacked(values[:, pl.ds(start, HALF)], rows, h))
            lh, ll = sh[:RANK], sl[:RANK]
            ph, plo = phi_parts[h]
            both = jnp.concatenate([lh, ll], axis=0)
            t = dot_t(both, jnp.concatenate([sh, ph], axis=0))
            t = t[:RANK] + t[RANK:] + dot_t(lh, jnp.concatenate([sl, plo], axis=0))
            t, m = t[:, :128], t[:, 128:]
            sums[h] = sums[h] + t
            y = y + u * t
            moments = moments + m * scale[pl.ds(q0 + b, 1), :RANK]
        return sums[0], sums[1], y, moments

    zero = jnp.zeros((RANK, 128), f32)
    first, second, y, moments = lax.fori_loop(low, high, body, (zero, zero, zero, jnp.zeros((RANK, RANK), f32)))
    moments = jnp.concatenate([jnp.zeros((RANK, 96), f32), moments], axis=1)
    tile_a, tile_b = point_tiles(first, second, y, v_ref[0] >= 4, moments)
    if low > 0:
        tile_a, tile_b = tile_a + after[:, :128], tile_b + after[:, 128:]
    out[:, :128] = tile_a
    out[:, 128:] = tile_b


def point_sums(v, values, low, high, after):
    def kernel(*refs):
        point_sums_kernel(low, high, *refs)

    return call(
        kernel, [((RANK, 256), f32)], "ssvvvvv",
        (v, SPEEDS, ROWS, PHI, PHI_SCALE, values, after), mib=12,
    )[0]


def space_sums_kernel(values, rates, out, own, hi, lo, zh, zl, ch, cl):
    def load(p, carry):
        for y in range(NY):
            block = values[pl.ds(p * NY + y, RANK, stride=OWN * NY), :]
            at = aligned(p * PLANE + y * NZ, 128)
            a, b = split(block)
            hi[:, pl.ds(at + PLANE, NZ)] = a
            lo[:, pl.ds(at + PLANE, NZ)] = b
            own[:, pl.ds(at, NZ)] = block
            a, b = split(roll_lanes(block, 1))
            zh[:, pl.ds(at, NZ)] = a
            zl[:, pl.ds(at, NZ)] = b
            a, b = split(block * rates[pl.ds(p * NY + y, 1), :])
            ch[:, pl.ds(at, NZ)] = a
            cl[:, pl.ds(at, NZ)] = b
        return carry

    hi[:, :PLANE] = jnp.zeros((RANK, PLANE), bf16)
    lo[:, :PLANE] = jnp.zeros((RANK, PLANE), bf16)
    lax.fori_loop(0, OWN, load, 0)

    def body(p, carry):
        t, c = carry
        at = aligned(p * PLANE, 128)

        def stack(main, turned):
            here = main[:, pl.ds(at + PLANE, PLANE)]
            wrapped = jnp.concatenate([here[:, PLANE - NZ :], here[:, : PLANE - NZ]], axis=1)
            return jnp.concatenate(
                [here, main[:, pl.ds(at, PLANE)], wrapped, turned[:, pl.ds(at, PLANE)]], axis=0
            )

        sh, sl = stack(hi, zh), stack(lo, zl)
        both = jnp.concatenate([sh[:RANK], sl[:RANK]], axis=0)
        part = dot_t(both, jnp.concatenate([sh, ch[:, pl.ds(at, PLANE)]], axis=0))
        part = part[:RANK] + part[RANK:] + dot_t(sh[:RANK], jnp.concatenate([sl, cl[:, pl.ds(at, PLANE)]], axis=0))
        return t + part[:, :128], c + part[:, 128:]

    t, c = lax.fori_loop(0, OWN, body, (jnp.zeros((RANK, 128), f32), jnp.zeros((RANK, RANK), f32)))
    out[:, :128] = t
    out[:, 128:] = jnp.concatenate([c, jnp.zeros((RANK, 96), f32)], axis=1)


def space_sums(values, rates):
    own = (RANK, OWN * PLANE)
    return call(
        space_sums_kernel, [((RANK, 256), f32), (own, f32)], "vv", (values, rates),
        [pltpu.VMEM((RANK, (OWN + 1) * PLANE), bf16)] * 2 + [pltpu.VMEM(own, bf16)] * 4, mib=12,
    )


def edge_sums_kernel(own, below, inner, out, edge):
    empty = jnp.zeros((RANK, PLANE), bf16)
    other = jnp.concatenate([below[pl.ds(y, RANK, stride=NY), :] for y in range(NY)], axis=1)
    edge[...] = other
    oh, ol = split(other)
    lh, ll = split(own[:, :PLANE])
    part = dot_t(jnp.concatenate([lh, ll], axis=0), jnp.concatenate([empty, oh], axis=0))
    t = part[:RANK] + part[RANK:] + dot_t(lh, jnp.concatenate([empty, ol], axis=0))
    out[:, :128] = inner[:, :128] + jnp.concatenate([t, jnp.zeros((RANK, 64), f32)], axis=1)
    out[:, 128:] = inner[:, 128:]


def edge_sums(own, below, inner):
    return call(edge_sums_kernel, [((RANK, 256), f32), ((RANK, PLANE), f32)], "vvv", (own, below, inner))


def factor_pair(first, second):
    zeros = jnp.zeros((RANK, 64), f32)
    works = [jnp.concatenate([g, eye(), zeros], axis=1) for g in (first, second)]
    pivots = [jnp.ones((RANK, 128), f32)] * 2
    row = sublanes((RANK, 128))
    for k in range(0, RANK, 2):
        for n in range(2):
            w = works[n]
            c0 = jnp.broadcast_to(w[:, k : k + 1], (RANK, 128))
            c1 = jnp.broadcast_to(w[:, k + 1 : k + 2], (RANK, 128))
            r0, r1 = w[k : k + 1, :], w[k + 1 : k + 2, :]
            a, b, d = c0[k : k + 1, :], c1[k : k + 1, :], c1[k + 1 : k + 2, :]
            over = 1.0 / a
            ratio = b * over
            d = d - b * ratio
            r1 = r1 - ratio * r0
            c1 = c1 - ratio * c0
            step = w - c0 * (r0 * over) - c1 * (r1 * (1.0 / d))
            works[n] = jnp.where(row > k + 1, step, jnp.where(row == k + 1, r1, w))
            pivots[n] = jnp.where(row == k, a, jnp.where(row == k + 1, d, pivots[n]))
    done = [works[n] * lax.rsqrt(pivots[n]) for n in range(2)]
    return [(w[:, :RANK], w[:, RANK : 2 * RANK]) for w in done]


def transposed(x):
    return mm_t(eye(), x)


def point_blocks(tiles, points_total):
    t = tiles * (1.0 / points_total)
    gram = t[:, 0:32]
    plus = [t[:, 192:224], t[:, 160:192], t[:, 64:96]]
    minus = [t[:, 128:160], t[:, 32:64], t[:, 96:128]]
    return gram, plus, minus, t[:, 224:256]


def four(parts):
    return (parts[0][...] + parts[2][...]) + (parts[1][...] + parts[3][...])


def small_first_kernel(cells_total, points_total, p0, p1, p2, p3, core, select, means, wk, wl, src, moment):
    both = four((p0, p1, p2, p3))
    s = both[:RANK] * (1.0 / cells_total)
    gram = s[:, 0:32]
    gram_v, _, _, raw = point_blocks(both[RANK:], points_total)
    (upper, inverse), (upper_v, inverse_v) = factor_pair(gram, gram_v)
    identity = eye()
    raw_a = [gram - s[:, 32 * (d + 1) : 32 * (d + 2)] for d in range(3)]
    to_spread = mm(upper, core[...])
    to_kinetic_t = mm_t(core[...], upper_v)
    zeros = jnp.zeros((RANK, 32), f32)
    inverse_t = transposed(inverse)
    triple = jnp.concatenate([inverse_t] * 3 + [zeros], axis=1)
    left = (
        [mm(inverse, s[:, 128:160])] + [mm(inverse, a) for a in raw_a] + [mm_t(inverse, a) for a in raw_a]
    )
    turned = mm(jnp.concatenate(left, axis=0), triple)
    one = jnp.concatenate([identity] * 3 + [zeros], axis=1)
    e_wide = turned[:RANK]
    mixers = [one - e_wide] + [-turned[RANK * (d + 1) : RANK * (d + 2)] for d in range(3)]
    mixers = mixers + [turned[RANK * (d + 4) : RANK * (d + 5)] for d in range(3)]
    stack = jnp.concatenate(mixers, axis=0)
    wl[1] = stack
    wl[0] = mm(stack[:, :RANK], jnp.concatenate([to_spread] * 3 + [zeros], axis=1))
    square = [m[:, :RANK] for m in mixers]
    e = e_wide[:, :RANK]
    moved = mm(mm(to_spread, raw), select[...])
    groups = [moved[:, 128 * j : 128 * (j + 1)] for j in range(7)]
    lane = lanes((RANK, 128))
    source = [mm(e, groups[0])[:, 0:1]]
    following = mm(square[0], groups[0]) + source[0] * means[0:1, :]
    for j in range(1, 7):
        following = following + mm(square[j], groups[j])
    source.append(mm(e, following)[:, 0:1])
    third = mm(square[0], jnp.where(lane == 0, following, 0.0))
    for j in range(1, 7):
        third = third + mm(square[j], jnp.where(lane == j, following, 0.0))
    third = jnp.sum(third, axis=1, keepdims=True) + source[1] * means[0:1, 0:1]
    source.append(mm(e, jnp.broadcast_to(third, (RANK, 128)))[:, 0:1])
    for n in range(3):
        src[n] = jnp.broadcast_to(source[n], (RANK, 128))
    half = mm(inverse_v, both[RANK:, :] * (1.0 / points_total))
    turned_raw = half[:, 224:256]
    weights_row = transposed(turned_raw)[0:1, :]
    blocks = [half[:, 192:224], half[:, 128:160], half[:, 160:192], half[:, 32:64], half[:, 64:96], half[:, 96:128]]
    flux = mm(jnp.concatenate(blocks, axis=0), transposed(inverse_v))
    flux = [flux[k * RANK : (k + 1) * RANK] * (1.0 if k % 2 == 0 else -1.0) for k in range(6)]
    row = sublanes((16, RANK))
    column = jnp.concatenate([identity] + flux + [jnp.where(row == 0, weights_row, 0.0)], axis=0)
    to_kinetic = transposed(to_kinetic_t)
    wk[0] = mm(column, jnp.concatenate([to_kinetic] * 3 + [zeros], axis=1))
    wk[1] = jnp.concatenate([column] * 3 + [jnp.zeros((ROWS_K, 32), f32)], axis=1)
    moment[...] = jnp.broadcast_to(turned_raw[:, LAST : LAST + 1], (RANK, 128))


def small_first(parts, core, cells_total, points_total):
    def kernel(*refs):
        small_first_kernel(cells_total, points_total, *refs)

    return call(
        kernel, [((2, ROWS_K, 128), f32), ((2, 224, 128), f32), ((3, RANK, 128), f32), ((RANK, 128), f32)], "vvvvvvv",
        (*parts, core, SELECT, MEANS),
    )


def evolve_point_kernel(v_ref, speeds, rows, wl, src, values, after, new, out):
    q0 = v_ref[0] * Q1
    lane_w = lanes((RANK, 128))
    low_lane = (lane_w >= 64) & (lane_w < 96)

    def weights_of(w):
        hi = w.astype(bf16).astype(f32)
        return jnp.where(low_lane, w - hi, hi).astype(bf16)

    def piece(kind, n):
        return wl[kind, n * RANK : (n + 1) * RANK, :]

    fixed = [jnp.concatenate([weights_of(piece(kind, n)) for n in (3, 6)], axis=0) for kind in range(2)]
    turning = [[weights_of(piece(kind, n)) for n in (5, 2)] for kind in range(2)]
    aux = []
    for h in range(2):
        gh, gl = split(rows[h, 3:4, :])
        row = sublanes((16, HALF))
        gh, gl = gh.astype(f32), gl.astype(f32)
        aux.append(jnp.where(row == 0, 1.0, jnp.where(row == 1, gh, jnp.where(row == 2, gl, 0.0))).astype(bf16))
    inside = HALF // 256 * 256
    cuts = [(0, inside, (0,)), (inside, 2 * HALF - inside, (0, 1)), (2 * HALF - inside, 2 * HALF, (1,))]

    def body(b, carry):
        sums, y, cross, ones_sum = list(carry[:2]), carry[2], carry[3], carry[4]
        up = speeds[q0 + b]
        um = speeds[NVD + q0 + b]
        g1 = speeds[2 * NVD + q0 + b]
        u = up + um
        moving = [piece(kind, 0) + up * piece(kind, 1) + um * piece(kind, 4) for kind in range(2)]
        heads = [weights_of(m) for m in moving]
        first = aligned(b * (2 * HALF), 128)
        states = [values[:, pl.ds(first, HALF)], values[:, pl.ds(first + HALF, HALF)]]
        raws = [split(state) for state in states]
        for n in range(SUB):
            kind = min(n, 1)
            parts = raws if n == 0 else [split(state) for state in states]
            operand = jnp.concatenate(
                [jnp.concatenate([parts[0][k], parts[1][k]], axis=1) for k in (0, 1, 0)], axis=0
            )
            source = src[n] * g1
            mixed = []
            for low, high, sides in cuts:
                w = jnp.concatenate([heads[kind], fixed[kind]] + [turning[kind][h] for h in sides], axis=0)[:, :96]
                mixed.append(dot(w, operand[:, low:high]))
            rest = HALF - inside
            middle = mixed[1]
            ends = [
                jnp.concatenate([mixed[0], middle[: 4 * RANK, :rest]], axis=1),
                jnp.concatenate([jnp.concatenate([middle[: 3 * RANK, rest:], middle[4 * RANK :, rest:]], axis=0), mixed[2]], axis=1),
            ]
            states = [
                ends[h][:RANK]
                + rows[h, 3:4, :] * source[:, 0:1]
                + rows[h, 1:2, :] * ends[h][RANK : 2 * RANK]
                + rows[h, 2:3, :] * ends[h][2 * RANK : 3 * RANK]
                + rows[h, 0:1, :] * ends[h][3 * RANK :]
                for h in range(2)
            ]
        for h in range(2):
            start = aligned(b * (2 * HALF) + h * HALF, 128)
            state = states[h]
            raw_hi, raw_lo = raws[h]
            new[:, pl.ds(start, HALF)] = state
            sh, sl = split(stacked(state, rows, h))
            lh, ll = sh[:RANK], sl[:RANK]
            t = dot_t(jnp.concatenate([lh, ll, aux[h]], axis=0), jnp.concatenate([sh, raw_hi], axis=0))
            t2 = dot_t(jnp.concatenate([lh, aux[h]], axis=0), jnp.concatenate([sl, raw_lo], axis=0))
            t_main = t[:RANK] + t[RANK : 2 * RANK] + t2[:RANK]
            cross = cross + t_main[:, 128:]
            t_main = t_main[:, :128]
            a = t[2 * RANK : 2 * RANK + 8, :128]
            a2 = t2[RANK : RANK + 8, :128]
            row8 = sublanes((8, 128))
            a = a + jnp.where(row8 < 2, a2, 0.0)
            ones_sum = ones_sum + jnp.where(row8 == 0, a, a * g1)
            sums[h] = sums[h] + t_main
            y = y + u * t_main
        return sums[0], sums[1], y, cross, ones_sum

    zero = jnp.zeros((RANK, 128), f32)
    first, second, y, cross, ones_sum = lax.fori_loop(
        0, Q1, body, (zero, zero, zero, jnp.zeros((RANK, RANK), f32), jnp.zeros((8, 128), f32))
    )
    cross = jnp.concatenate([jnp.zeros((RANK, 96), f32), cross], axis=1)
    tile_a, tile_b = point_tiles(first, second, y, v_ref[0] >= 4, cross)
    out[:RANK, :128] = tile_a
    out[:RANK, 128:] = tile_b
    out[RANK:, :128] = ones_sum
    out[RANK:, 128:] = jnp.zeros((8, 128), f32)


def evolve_point(v, wl, src, values, after):
    return call(
        evolve_point_kernel, [(values.shape, f32), ((RANK + 8, 256), f32)], "ssvvvva",
        (v, SPEEDS, ROWS, wl, src, values, after), mib=16,
    )


RATES = (LOW - 1 + OWN + HIGH - 1) * NY
HALO = RANK * HIGH * NY


def fill_kernel(v_ref, own, edge, mine, other, after, state, rates_low, rates_high):
    core = v_ref[0] % 2
    state[:, LOW * PLANE : (LOW + OWN) * PLANE] = own[...]
    state[:, (LOW - 1) * PLANE : LOW * PLANE] = edge[...]
    for source, place in ((mine, core), (other, 1 - core)):

        def load(p, carry, source=source, place=place):
            for y in range(NY):
                at = aligned((p + place * (LOW + OWN)) * PLANE + y * NZ, 128)
                state[:, pl.ds(at, NZ)] = source[pl.ds(p * NY + y, RANK, stride=HIGH * NY), :]
            return carry

        lax.fori_loop(0, HIGH, load, 0)
    first, second = mine[HALO:, :], other[HALO:, :]
    rates_low[...] = jnp.where(core == 0, first, second)
    rates_high[...] = jnp.where(core == 0, second, first)


def fill_planes(v, own, edge, mine, other, after):
    part = ((HIGH * NY, NZ), f32)
    return call(
        fill_kernel, [((RANK, WIDE * PLANE), f32), part, part], "svvvva", (v, own, edge, mine, other, after),
        mib=12,
    )


def evolve_space_kernel(wk, moment, raw, rates, rates_low, rates_high, new, out, rates_all, partial, passed, *bufs):
    sources, targets = [raw, bufs[0], bufs[1]], [bufs[0], bufs[1], new]
    low, own = (LOW - 1) * NY, OWN * NY
    rates_all[:low, :] = rates_low[...]
    rates_all[low : low + own, :] = rates[...]
    rates_all[low + own :, :] = rates_high[: (HIGH - 1) * NY, :]
    lane = lanes((ROWS_K, 128))
    low_lane = (lane >= 64) & (lane < 96)

    for n in range(SUB):
        w = wk[min(n, 1)]
        w_hi = w.astype(bf16).astype(f32)
        w = jnp.where(low_lane, w - w_hi, w_hi).astype(bf16)[:, :96]
        if n > 0:
            w = w[RANK:]
        skip = w.shape[0] - ROWS_K + RANK
        src, dst = sources[n], targets[n]
        shift = 2 if n == SUB - 1 else 0
        begin, end = 1 + n, WIDE - 1 - n

        def tile(t, j, src=src):
            cells = src[:, pl.ds(aligned(t * PLANE + j * 256, 256), 256)]
            a, b = split(cells)
            return cells, jnp.concatenate([a, b, a], axis=0)

        def put(t, y, block, dst=dst, shift=shift):
            dst[:, pl.ds(aligned((t - shift) * PLANE + y * NZ, 128), NZ)] = block

        def step(t, carry, w=w, tile=tile, put=put, skip=skip):
            scale = moment[...]
            bases, ups, downs = [], [], []
            for j in range(NY // 2):
                cells, operand = tile(t, j)
                mixed = dot(w, operand)
                for i in range(2):
                    y = 2 * j + i
                    cell = slice(y * NZ, (y + 1) * NZ)
                    half = slice(i * NZ, (i + 1) * NZ)
                    part = [mixed[skip + k * RANK : skip + (k + 1) * RANK, half] for k in range(6)]
                    here = mixed[:RANK, half] if skip else cells[:, half]
                    density = mixed[skip + 6 * RANK : skip + 6 * RANK + 1, half]
                    put(t - 1, y, partial[:, cell] + part[1])
                    rate = rates_all[pl.ds((t - 1) * NY + y, 1), :]
                    base = here + rate * (scale * density - here) + passed[:, cell]
                    passed[:, cell] = part[0]
                    base = base - ((part[0] + part[1]) + (part[2] + part[3]) + (part[4] + part[5]))
                    bases.append(base + roll_lanes(part[4], 1) + roll_lanes(part[5], -1))
                    ups.append(part[2])
                    downs.append(part[3])
                    if y >= 2:
                        partial[:, (y - 1) * NZ : y * NZ] = bases[y - 1] + ups[y - 2] + downs[y]
            partial[:, (NY - 1) * NZ :] = bases[NY - 1] + ups[NY - 2] + downs[0]
            partial[:, :NZ] = bases[0] + ups[NY - 1] + downs[1]
            return carry

        for j in range(NY // 2):
            passed[:, j * 256 : (j + 1) * 256] = dot(w[skip : skip + RANK], tile(begin - 1, j)[1])
        for t in range(begin, end):
            step(t, 0)
        for j in range(NY // 2):
            mixed = dot(w[skip + RANK : skip + 2 * RANK], tile(end, j)[1])
            for i in range(2):
                y = 2 * j + i
                put(end - 1, y, partial[:, y * NZ : (y + 1) * NZ] + mixed[:, i * NZ : (i + 1) * NZ])

    def body(p, carry):
        t, c = carry
        turned, relaxed = [], []
        for y in range(NY):
            block = new[:, pl.ds(aligned((p + 2) * PLANE + y * NZ, 128), NZ)]
            turned.append(split(roll_lanes(block, 1)))
            relaxed.append(split(block * rates[pl.ds(p * NY + y, 1), :]))
        here = split(new[:, pl.ds(aligned((p + 2) * PLANE, 128), PLANE)])
        behind = split(new[:, pl.ds(aligned((p + 1) * PLANE, 128), PLANE)])
        old = split(raw[:, pl.ds(aligned((p + LOW) * PLANE, 128), PLANE)])

        def stack(k):
            wrapped = jnp.concatenate([here[k][:, PLANE - NZ :], here[k][:, : PLANE - NZ]], axis=1)
            rolled = jnp.concatenate([block[k] for block in turned], axis=1)
            scaled = jnp.concatenate([block[k] for block in relaxed], axis=1)
            return jnp.concatenate([here[k], behind[k], wrapped, rolled, scaled, old[k]], axis=0)

        part = dot_t(jnp.concatenate(here, axis=0), stack(0))
        part = part[:RANK] + part[RANK:] + dot_t(here[0], stack(1))
        return t + part[:, :128], c + part[:, 128:]

    carry = (jnp.zeros((RANK, 128), f32), jnp.zeros((RANK, 64), f32))
    for p in range(OWN):
        carry = body(p, carry)
    t, c = carry
    out[:, :128] = t
    out[:, 128:] = jnp.concatenate([c, jnp.zeros((RANK, 64), f32)], axis=1)


def evolve_space(wk, moment, filled, rates):
    return call(
        evolve_space_kernel, [((RANK, (OWN + 2) * PLANE), f32), ((RANK, 256), f32)], "v" * 6,
        (wk, moment, filled[0], rates, filled[1], filled[2]),
        [pltpu.VMEM((RATES, NZ), f32)]
        + [pltpu.VMEM((RANK, PLANE), f32)] * 2
        + [pltpu.VMEM((RANK, WIDE * PLANE), f32)] * 2,
        mib=16,
    )


def finish_kernel(
    cells_total, points_total, p0, p1, p2, p3, core, kinetic, spread, space_out, fresh_core, point_out, fresh_space, fresh_point, sems
):
    both = four((p0, p1, p2, p3))
    s = both[:RANK] * (1.0 / cells_total)
    q = both[RANK:] * (1.0 / points_total)
    gram, gram_v = s[:, 0:32], q[:RANK, 0:32]
    (_, inverse), (_, inverse_v) = factor_pair(gram, gram_v)
    zeros = jnp.zeros((RANK, 32), f32)
    lane = lanes((RANK, 128))

    def wide(matrix):
        w = jnp.concatenate([matrix] * 3 + [zeros], axis=1)
        hi = w.astype(bf16).astype(f32)
        return jnp.where((lane >= 64) & (lane < 96), w - hi, hi).astype(bf16)[:, :96]

    w_space, w_point = wide(inverse), wide(inverse_v)

    def out_space(n):
        size = PLANE // 2
        at = 2 * PLANE + n * size
        hi, lo = split(kinetic[:, at : at + size])
        made = dot(w_space, jnp.concatenate([hi, lo, hi], axis=0))
        for y in range(NY // 2):
            fresh_space[pl.ds(n * (NY // 2) + y, RANK, stride=OWN * NY), :] = made[:, y * NZ : (y + 1) * NZ]

    def out_point(n):
        cells = slice(n * 1536, (n + 1) * 1536)
        hi, lo = split(spread[:, cells])
        fresh_point[:, cells] = dot(w_point, jnp.concatenate([hi, lo, hi], axis=0))

    third = 2 * Q1 * HALF // 3
    copies = []

    def outputs():
        for k in range(3):
            for n in range(3):
                out_point(3 * k + n)
                if n == 2:
                    cells = pl.ds(k * third, third)
                    copies.append(pltpu.make_async_copy(fresh_point.at[:, cells], point_out.at[:, cells], sems.at[k + 1]))
                    copies[-1].start()
                yield
        for n in range(2 * OWN):
            out_space(n)
            if n == 2 * OWN - 1:
                copies.append(pltpu.make_async_copy(fresh_space, space_out, sems.at[0]))
                copies[-1].start()
            yield

    writing = outputs()

    def write(count):
        for _ in range(count):
            next(writing, None)

    inverse_t = transposed(inverse)
    inverse_vt = transposed(inverse_v)
    turned = mm(inverse, s)
    turned_v = mm(inverse_v, q[:RANK])
    write(4)
    aux = mm(q[RANK:, 0:32], inverse_vt)
    weights_row = aux[0:1, :]
    moments_row = aux[1:2, :] + aux[2:3, :]
    left = [turned[:, 128:160]]
    for d in range(3):
        left.append(turned[:, 0:32] - turned[:, 32 * (d + 1) : 32 * (d + 2)])
    for d in range(3):
        left.append(mm_t(inverse, gram - s[:, 32 * (d + 1) : 32 * (d + 2)]))
    half = mm(turned[:, 160:192], core[...])
    write(3)
    stack = mm(jnp.concatenate(left, axis=0), inverse_t)
    lines = [turned_v[:, 192:224], turned_v[:, 160:192], turned_v[:, 64:96]]
    lines += [-turned_v[:, 128:160], -turned_v[:, 32:64], -turned_v[:, 96:128]]
    flux = mm(jnp.concatenate(lines, axis=0), inverse_vt)
    current = mm_t(half, turned_v[:, 224:256])
    for _ in range(SUB):
        write(2)
        moved = mm(stack, current)
        scaled = moved[:RANK]
        change = -scaled + jnp.sum(scaled * weights_row, axis=1, keepdims=True) * moments_row
        across = jnp.concatenate([moved[(k + 1) * RANK : (k + 2) * RANK] for k in range(6)], axis=1)
        write(2)
        current = current + (change - mm(across, flux))
    write(20)
    fresh_core[...] = current
    for copy in copies:
        copy.wait()


def finish(parts, core, kinetic, spread, cells_total, points_total):
    def kernel(*refs):
        finish_kernel(cells_total, points_total, *refs)

    flat = (RANK * OWN * NY, NZ)
    return call(
        kernel, [(flat, f32), ((RANK, RANK), f32), (spread.shape, f32)], "vvvvvvv",
        (*parts, core, kinetic, spread),
        [pltpu.VMEM(flat, f32), pltpu.VMEM(spread.shape, f32), pltpu.SemaphoreType.DMA((4,))],
        mib=12, out_spaces="ava",
    )


def spread_pairs(space_part):
    moved = []
    for k in range(2):
        route = [((s ^ (2 * v + k)) * 8 + v, s * 8 + v) for s in range(16) for v in range(8)]
        moved.append(lax.ppermute(space_part, ("space", "vel"), route))
    return moved


def vel_parts(moved, point_part):
    joint = jnp.concatenate([moved[0] + moved[1], point_part], axis=0)
    pair = [(2 * z + c, 2 * z + 1 - c) for z in range(4) for c in range(2)]
    joint = joint + lax.ppermute(joint, "vel", pair)
    routes = [[(2 * z + c, 2 * ((z + d) % 4) + c) for z in range(4) for c in range(2)] for d in (1, 2, 3)]
    parts = [joint]
    for route in routes:
        parts.append(lax.ppermute(joint, "vel", route))
    return parts


def per_device(space_factor, core_matrix, velocity_factor, collision_rates):
    devices = lax.axis_size("space")
    up = [(i, (i + 1) % devices) for i in range(devices)]
    below1 = lax.ppermute(space_factor[:, OWN - 1 :], "space", up).reshape(-1, NZ)
    rates = collision_rates.reshape(-1, NZ)
    values = space_factor.reshape(-1, NZ)
    cells_total = OWN * PLANE * devices
    points_total = velocity_factor.shape[1] * lax.axis_size("vel")
    place = lax.axis_index("vel").astype(jnp.int32)
    v = place.reshape(1)
    planes = jnp.where(place % 2 == 0, space_factor[:, : OWN - 1], space_factor[:, :HIGH])
    lines = jnp.where(place % 2 == 0, collision_rates[1:], collision_rates[:HIGH])
    halo = jnp.concatenate([planes, lines[None]], axis=0)
    route = [(s * 8 + w, (s + 1 - 2 * (w % 2)) % devices * 8 + w) for s in range(devices) for w in range(8)]
    pair = [(w, w ^ 1) for w in range(8)]

    inner, own = space_sums(values, rates)
    point = point_sums(v, velocity_factor, 0, Q1 // 2, inner)
    space, edge = edge_sums(own, below1, inner)
    moved = spread_pairs(space)
    halo, space = lax.optimization_barrier((halo, space))
    mine = lax.ppermute(halo, ("space", "vel"), route)
    point = point_sums(v, velocity_factor, Q1 // 2, Q1, point)
    parts = vel_parts(moved, point)
    mine, parts[0] = lax.optimization_barrier((mine, parts[0]))
    other = lax.ppermute(mine, "vel", pair)
    wk, wl, src, moment = small_first(parts, core_matrix, cells_total, points_total)
    filled = fill_planes(v, own, edge, mine.reshape(-1, NZ), other.reshape(-1, NZ), moment)
    kinetic, space = evolve_space(wk, moment, filled, rates)
    moved = spread_pairs(space)
    spread, point = evolve_point(v, wl, src, velocity_factor, space)
    parts = vel_parts(moved, point)
    fresh_space, fresh_core, fresh_point = finish(parts, core_matrix, kinetic, spread, cells_total, points_total)
    return fresh_space.reshape(space_factor.shape), fresh_core, fresh_point


def solution(mesh):
    return jax.shard_map(
        per_device,
        mesh=mesh,
        in_specs=(P(None, "space", None, None), P(), P(None, "vel"), P("space", None, None)),
        out_specs=(P(None, "space", None, None), P(), P(None, "vel")),
        check_vma=False,
    )
```

```python
import jax
import jax.numpy as jnp
import numpy as np
from jax import lax
from jax.experimental import pallas as pl
from jax.experimental.pallas import tpu as pltpu
from jax.sharding import PartitionSpec as P


RANK = 32
NVD = 48
SUB = 3
LOW = SUB + 1
HIGH = SUB
NY = 16
NZ = 128
OWN = 4
Q1 = 6
HALF = NVD * NVD // 2
PLANE = NY * NZ
WIDE = LOW + OWN + HIGH
ROWS_K = 7 * RANK + 16
INTERPRET = False

f32 = jnp.float32
bf16 = jnp.bfloat16


def tables():
    t = np.float32(0.25) * ((2 * np.arange(NVD) + 1).astype(np.float32) / np.float32(NVD) - np.float32(1.0))
    t = t.astype(np.float32)
    shape = np.exp(-(t.astype(np.float64) ** 2) / (2.0 * 0.125 * 0.125))
    shape = shape / shape.mean()
    plus, minus = np.maximum(t, 0), np.minimum(t, 0)
    u2, u3 = np.repeat(t, NVD), np.tile(t, NVD)
    g23 = np.repeat(shape, NVD) * np.tile(shape, NVD)
    sides = [(1, "p"), (2, "p"), (3, "p"), (1, "m"), (2, "m"), (3, "m")]
    names = [()] + [(s,) for s in sides]
    where = {(): 0}
    for k in range(6):
        where[(k,)] = k + 1
    for j in range(6):
        for k in range(j, 6):
            if k != j and sides[j][0] == sides[k][0]:
                continue
            where[(j, k)] = len(names)
            names.append((sides[j], sides[k]))
    base = np.zeros((2, 32, HALF))
    scale = np.zeros((NVD, 128))
    value = {"p": np.maximum, "m": np.minimum}
    for row, name in enumerate(names):
        b = np.ones(NVD * NVD)
        c = np.ones(NVD)
        for d, sign in name:
            if d == 1:
                c = c * value[sign](t.astype(np.float64), 0)
            elif d == 2:
                b = b * value[sign](u2.astype(np.float64), 0)
            else:
                b = b * value[sign](u3.astype(np.float64), 0)
        base[:, row] = b.reshape(2, HALF)
        scale[:, row] = c
    last = len(names)
    base[:, last] = g23.reshape(2, HALF)
    scale[:, last] = shape
    select = np.zeros((32, 7 * 128), np.float32)
    for j in range(7):
        for k in range(7):
            pair = tuple(sorted([i - 1 for i in (j, k) if i > 0]))
            if pair in where:
                select[where[pair], j * 128 + k] = 1.0
    means = np.zeros((8, 128), np.float32)
    means[:, 0] = 1.0
    means[:, 1:4] = (shape * plus).mean()
    means[:, 4:7] = (shape * minus).mean()
    rows = np.zeros((2, 8, HALF), np.float32)
    rows[:, 0] = u2.reshape(2, HALF)
    rows[:, 1] = np.maximum(u3, 0).reshape(2, HALF)
    rows[:, 2] = np.minimum(u3, 0).reshape(2, HALF)
    rows[:, 3] = g23.reshape(2, HALF)
    speeds = np.concatenate([plus, minus, shape]).astype(np.float32)
    return rows, base.astype(np.float32), scale.astype(np.float32), select, means, speeds, last


ROWS, PHI, PHI_SCALE, SELECT, MEANS, SPEEDS, LAST = tables()


def split(x):
    hi = x.astype(bf16)
    return hi, (x - hi.astype(f32)).astype(bf16)


def dot(a, b):
    return jnp.dot(a, b, preferred_element_type=f32)


def dot_t(a, b):
    return lax.dot_general(a, b, (((1,), (1,)), ((), ())), preferred_element_type=f32)


def mm(a, b, form=dot):
    rows = a.shape[0]
    ah, al = split(a)
    bh, bl = split(b)
    main = form(jnp.concatenate([ah, al], axis=0), bh)
    return main[:rows] + main[rows:] + form(ah, bl)


def mm_t(a, b):
    return mm(a, b, dot_t)


def aligned(index, size):
    return index if isinstance(index, int) else pl.multiple_of(index, size)


def lanes(shape):
    return lax.broadcasted_iota(jnp.int32, shape, len(shape) - 1)


def sublanes(shape):
    return lax.broadcasted_iota(jnp.int32, shape, len(shape) - 2)


def eye():
    return (lanes((RANK, RANK)) == sublanes((RANK, RANK))).astype(f32)


def call(kernel, outs, ins, args, scratch=(), mib=8, out_spaces=None):
    spaces = {"v": pltpu.VMEM, "s": pltpu.SMEM, "a": pl.ANY}
    out_spaces = out_spaces or "v" * len(outs)
    return pl.pallas_call(
        kernel,
        out_shape=[jax.ShapeDtypeStruct(s, d) for s, d in outs],
        in_specs=[pl.BlockSpec(memory_space=spaces[c]) for c in ins],
        out_specs=[pl.BlockSpec(memory_space=spaces[c]) for c in out_spaces],
        scratch_shapes=list(scratch),
        compiler_params=pltpu.CompilerParams(vmem_limit_bytes=mib * 1024 * 1024),
        interpret=INTERPRET,
    )(*args)


def point_tiles(first, second, y, positive, extra):
    lane = lanes((RANK, 128))
    middle = (lane >= 32) & (lane < 64)
    tile_a = first + jnp.where(middle, 0.0, second)
    y = jnp.where(lane < 32, y, 0.0)
    y = jnp.where(positive, pltpu.roll(y, 64, 1) if not INTERPRET else jnp.roll(y, 64, 1), y)
    return tile_a, jnp.where(middle, second, 0.0) + y + extra


def roll_lanes(x, shift):
    return jnp.roll(x, shift, 1) if INTERPRET else pltpu.roll(x, shift % x.shape[1], 1)


def stacked(values, rows, h):
    return jnp.concatenate(
        [values, values * rows[h, 0:1, :], values * rows[h, 1:2, :], values * rows[h, 2:3, :]], axis=0
    )


def point_sums_kernel(low, high, v_ref, speeds, rows, phi, scale, values, after, out):
    q0 = v_ref[0] * Q1
    phi_parts = [split(phi[h]) for h in range(2)]

    def body(b, carry):
        sums, y, moments = list(carry[:2]), carry[2], carry[3]
        u = speeds[q0 + b] + speeds[NVD + q0 + b]
        for h in range(2):
            start = aligned(b * (2 * HALF) + h * HALF, 128)
            sh, sl = split(stacked(values[:, pl.ds(start, HALF)], rows, h))
            lh, ll = sh[:RANK], sl[:RANK]
            ph, plo = phi_parts[h]
            both = jnp.concatenate([lh, ll], axis=0)
            t = dot_t(both, jnp.concatenate([sh, ph], axis=0))
            t = t[:RANK] + t[RANK:] + dot_t(lh, jnp.concatenate([sl, plo], axis=0))
            t, m = t[:, :128], t[:, 128:]
            sums[h] = sums[h] + t
            y = y + u * t
            moments = moments + m * scale[pl.ds(q0 + b, 1), :RANK]
        return sums[0], sums[1], y, moments

    zero = jnp.zeros((RANK, 128), f32)
    first, second, y, moments = lax.fori_loop(low, high, body, (zero, zero, zero, jnp.zeros((RANK, RANK), f32)))
    moments = jnp.concatenate([jnp.zeros((RANK, 96), f32), moments], axis=1)
    tile_a, tile_b = point_tiles(first, second, y, v_ref[0] >= 4, moments)
    if low > 0:
        tile_a, tile_b = tile_a + after[:, :128], tile_b + after[:, 128:]
    out[:, :128] = tile_a
    out[:, 128:] = tile_b


def point_sums(v, values, low, high, after):
    def kernel(*refs):
        point_sums_kernel(low, high, *refs)

    return call(
        kernel, [((RANK, 256), f32)], "ssvvvvv",
        (v, SPEEDS, ROWS, PHI, PHI_SCALE, values, after), mib=12,
    )[0]


def space_sums_kernel(values, rates, out, own, hi, lo, zh, zl, ch, cl):
    def load(p, carry):
        for y in range(NY):
            block = values[pl.ds(p * NY + y, RANK, stride=OWN * NY), :]
            at = aligned(p * PLANE + y * NZ, 128)
            a, b = split(block)
            hi[:, pl.ds(at + PLANE, NZ)] = a
            lo[:, pl.ds(at + PLANE, NZ)] = b
            own[:, pl.ds(at, NZ)] = block
            a, b = split(roll_lanes(block, 1))
            zh[:, pl.ds(at, NZ)] = a
            zl[:, pl.ds(at, NZ)] = b
            a, b = split(block * rates[pl.ds(p * NY + y, 1), :])
            ch[:, pl.ds(at, NZ)] = a
            cl[:, pl.ds(at, NZ)] = b
        return carry

    hi[:, :PLANE] = jnp.zeros((RANK, PLANE), bf16)
    lo[:, :PLANE] = jnp.zeros((RANK, PLANE), bf16)
    lax.fori_loop(0, OWN, load, 0)

    def body(p, carry):
        t, c = carry
        at = aligned(p * PLANE, 128)

        def stack(main, turned):
            here = main[:, pl.ds(at + PLANE, PLANE)]
            wrapped = jnp.concatenate([here[:, PLANE - NZ :], here[:, : PLANE - NZ]], axis=1)
            return jnp.concatenate(
                [here, main[:, pl.ds(at, PLANE)], wrapped, turned[:, pl.ds(at, PLANE)]], axis=0
            )

        sh, sl = stack(hi, zh), stack(lo, zl)
        both = jnp.concatenate([sh[:RANK], sl[:RANK]], axis=0)
        part = dot_t(both, jnp.concatenate([sh, ch[:, pl.ds(at, PLANE)]], axis=0))
        part = part[:RANK] + part[RANK:] + dot_t(sh[:RANK], jnp.concatenate([sl, cl[:, pl.ds(at, PLANE)]], axis=0))
        return t + part[:, :128], c + part[:, 128:]

    t, c = lax.fori_loop(0, OWN, body, (jnp.zeros((RANK, 128), f32), jnp.zeros((RANK, RANK), f32)))
    out[:, :128] = t
    out[:, 128:] = jnp.concatenate([c, jnp.zeros((RANK, 96), f32)], axis=1)


def space_sums(values, rates):
    own = (RANK, OWN * PLANE)
    return call(
        space_sums_kernel, [((RANK, 256), f32), (own, f32)], "vv", (values, rates),
        [pltpu.VMEM((RANK, (OWN + 1) * PLANE), bf16)] * 2 + [pltpu.VMEM(own, bf16)] * 4, mib=12,
    )


def edge_sums_kernel(own, below, inner, out, edge):
    empty = jnp.zeros((RANK, PLANE), bf16)
    other = jnp.concatenate([below[pl.ds(y, RANK, stride=NY), :] for y in range(NY)], axis=1)
    edge[...] = other
    oh, ol = split(other)
    lh, ll = split(own[:, :PLANE])
    part = dot_t(jnp.concatenate([lh, ll], axis=0), jnp.concatenate([empty, oh], axis=0))
    t = part[:RANK] + part[RANK:] + dot_t(lh, jnp.concatenate([empty, ol], axis=0))
    out[:, :128] = inner[:, :128] + jnp.concatenate([t, jnp.zeros((RANK, 64), f32)], axis=1)
    out[:, 128:] = inner[:, 128:]


def edge_sums(own, below, inner):
    return call(edge_sums_kernel, [((RANK, 256), f32), ((RANK, PLANE), f32)], "vvv", (own, below, inner))


def factor_pair(first, second):
    zeros = jnp.zeros((RANK, 64), f32)
    works = [jnp.concatenate([g, eye(), zeros], axis=1) for g in (first, second)]
    pivots = [jnp.ones((RANK, 128), f32)] * 2
    row = sublanes((RANK, 128))
    for k in range(0, RANK, 2):
        for n in range(2):
            w = works[n]
            c0 = jnp.broadcast_to(w[:, k : k + 1], (RANK, 128))
            c1 = jnp.broadcast_to(w[:, k + 1 : k + 2], (RANK, 128))
            r0, r1 = w[k : k + 1, :], w[k + 1 : k + 2, :]
            a, b, d = c0[k : k + 1, :], c1[k : k + 1, :], c1[k + 1 : k + 2, :]
            over = 1.0 / a
            ratio = b * over
            d = d - b * ratio
            r1 = r1 - ratio * r0
            c1 = c1 - ratio * c0
            step = w - c0 * (r0 * over) - c1 * (r1 * (1.0 / d))
            works[n] = jnp.where(row > k + 1, step, jnp.where(row == k + 1, r1, w))
            pivots[n] = jnp.where(row == k, a, jnp.where(row == k + 1, d, pivots[n]))
    done = [works[n] * lax.rsqrt(pivots[n]) for n in range(2)]
    return [(w[:, :RANK], w[:, RANK : 2 * RANK]) for w in done]


def transposed(x):
    return mm_t(eye(), x)


def point_blocks(tiles, points_total):
    t = tiles * (1.0 / points_total)
    gram = t[:, 0:32]
    plus = [t[:, 192:224], t[:, 160:192], t[:, 64:96]]
    minus = [t[:, 128:160], t[:, 32:64], t[:, 96:128]]
    return gram, plus, minus, t[:, 224:256]


def four(parts):
    return (parts[0][...] + parts[2][...]) + (parts[1][...] + parts[3][...])


def small_first_kernel(cells_total, points_total, p0, p1, p2, p3, core, select, means, wk, wl, src, moment):
    both = four((p0, p1, p2, p3))
    s = both[:RANK] * (1.0 / cells_total)
    gram = s[:, 0:32]
    gram_v, _, _, raw = point_blocks(both[RANK:], points_total)
    (upper, inverse), (upper_v, inverse_v) = factor_pair(gram, gram_v)
    identity = eye()
    raw_a = [gram - s[:, 32 * (d + 1) : 32 * (d + 2)] for d in range(3)]
    to_spread = mm(upper, core[...])
    to_kinetic_t = mm_t(core[...], upper_v)
    zeros = jnp.zeros((RANK, 32), f32)
    inverse_t = transposed(inverse)
    triple = jnp.concatenate([inverse_t] * 3 + [zeros], axis=1)
    left = (
        [mm(inverse, s[:, 128:160])] + [mm(inverse, a) for a in raw_a] + [mm_t(inverse, a) for a in raw_a]
    )
    turned = mm(jnp.concatenate(left, axis=0), triple)
    one = jnp.concatenate([identity] * 3 + [zeros], axis=1)
    e_wide = turned[:RANK]
    mixers = [one - e_wide] + [-turned[RANK * (d + 1) : RANK * (d + 2)] for d in range(3)]
    mixers = mixers + [turned[RANK * (d + 4) : RANK * (d + 5)] for d in range(3)]
    stack = jnp.concatenate(mixers, axis=0)
    wl[1] = stack
    wl[0] = mm(stack[:, :RANK], jnp.concatenate([to_spread] * 3 + [zeros], axis=1))
    square = [m[:, :RANK] for m in mixers]
    e = e_wide[:, :RANK]
    moved = mm(mm(to_spread, raw), select[...])
    groups = [moved[:, 128 * j : 128 * (j + 1)] for j in range(7)]
    lane = lanes((RANK, 128))
    source = [mm(e, groups[0])[:, 0:1]]
    following = mm(square[0], groups[0]) + source[0] * means[0:1, :]
    for j in range(1, 7):
        following = following + mm(square[j], groups[j])
    source.append(mm(e, following)[:, 0:1])
    third = mm(square[0], jnp.where(lane == 0, following, 0.0))
    for j in range(1, 7):
        third = third + mm(square[j], jnp.where(lane == j, following, 0.0))
    third = jnp.sum(third, axis=1, keepdims=True) + source[1] * means[0:1, 0:1]
    source.append(mm(e, jnp.broadcast_to(third, (RANK, 128)))[:, 0:1])
    for n in range(3):
        src[n] = jnp.broadcast_to(source[n], (RANK, 128))
    half = mm(inverse_v, both[RANK:, :] * (1.0 / points_total))
    turned_raw = half[:, 224:256]
    weights_row = transposed(turned_raw)[0:1, :]
    blocks = [half[:, 192:224], half[:, 128:160], half[:, 160:192], half[:, 32:64], half[:, 64:96], half[:, 96:128]]
    flux = mm(jnp.concatenate(blocks, axis=0), transposed(inverse_v))
    flux = [flux[k * RANK : (k + 1) * RANK] * (1.0 if k % 2 == 0 else -1.0) for k in range(6)]
    row = sublanes((16, RANK))
    column = jnp.concatenate([identity] + flux + [jnp.where(row == 0, weights_row, 0.0)], axis=0)
    to_kinetic = transposed(to_kinetic_t)
    wk[0] = mm(column, jnp.concatenate([to_kinetic] * 3 + [zeros], axis=1))
    wk[1] = jnp.concatenate([column] * 3 + [jnp.zeros((ROWS_K, 32), f32)], axis=1)
    moment[...] = jnp.broadcast_to(turned_raw[:, LAST : LAST + 1], (RANK, 128))


def small_first(parts, core, cells_total, points_total):
    def kernel(*refs):
        small_first_kernel(cells_total, points_total, *refs)

    return call(
        kernel, [((2, ROWS_K, 128), f32), ((2, 224, 128), f32), ((3, RANK, 128), f32), ((RANK, 128), f32)], "vvvvvvv",
        (*parts, core, SELECT, MEANS),
    )


def evolve_point_kernel(v_ref, speeds, rows, wl, src, values, after, new, out):
    q0 = v_ref[0] * Q1
    lane_w = lanes((RANK, 128))
    low_lane = (lane_w >= 64) & (lane_w < 96)

    def weights_of(w):
        hi = w.astype(bf16).astype(f32)
        return jnp.where(low_lane, w - hi, hi).astype(bf16)

    def piece(kind, n):
        return wl[kind, n * RANK : (n + 1) * RANK, :]

    fixed = [jnp.concatenate([weights_of(piece(kind, n)) for n in (3, 6)], axis=0) for kind in range(2)]
    turning = [[weights_of(piece(kind, n)) for n in (5, 2)] for kind in range(2)]
    aux = []
    for h in range(2):
        gh, gl = split(rows[h, 3:4, :])
        row = sublanes((16, HALF))
        gh, gl = gh.astype(f32), gl.astype(f32)
        aux.append(jnp.where(row == 0, 1.0, jnp.where(row == 1, gh, jnp.where(row == 2, gl, 0.0))).astype(bf16))
    inside = HALF // 256 * 256
    cuts = [(0, inside, (0,)), (inside, 2 * HALF - inside, (0, 1)), (2 * HALF - inside, 2 * HALF, (1,))]

    def body(b, carry):
        sums, y, cross, ones_sum = list(carry[:2]), carry[2], carry[3], carry[4]
        up = speeds[q0 + b]
        um = speeds[NVD + q0 + b]
        g1 = speeds[2 * NVD + q0 + b]
        u = up + um
        moving = [piece(kind, 0) + up * piece(kind, 1) + um * piece(kind, 4) for kind in range(2)]
        heads = [weights_of(m) for m in moving]
        first = aligned(b * (2 * HALF), 128)
        states = [values[:, pl.ds(first, HALF)], values[:, pl.ds(first + HALF, HALF)]]
        raws = [split(state) for state in states]
        for n in range(SUB):
            kind = min(n, 1)
            parts = raws if n == 0 else [split(state) for state in states]
            operand = jnp.concatenate(
                [jnp.concatenate([parts[0][k], parts[1][k]], axis=1) for k in (0, 1, 0)], axis=0
            )
            source = src[n] * g1
            mixed = []
            for low, high, sides in cuts:
                w = jnp.concatenate([heads[kind], fixed[kind]] + [turning[kind][h] for h in sides], axis=0)[:, :96]
                mixed.append(dot(w, operand[:, low:high]))
            rest = HALF - inside
            middle = mixed[1]
            ends = [
                jnp.concatenate([mixed[0], middle[: 4 * RANK, :rest]], axis=1),
                jnp.concatenate([jnp.concatenate([middle[: 3 * RANK, rest:], middle[4 * RANK :, rest:]], axis=0), mixed[2]], axis=1),
            ]
            states = [
                ends[h][:RANK]
                + rows[h, 3:4, :] * source[:, 0:1]
                + rows[h, 1:2, :] * ends[h][RANK : 2 * RANK]
                + rows[h, 2:3, :] * ends[h][2 * RANK : 3 * RANK]
                + rows[h, 0:1, :] * ends[h][3 * RANK :]
                for h in range(2)
            ]
        for h in range(2):
            start = aligned(b * (2 * HALF) + h * HALF, 128)
            state = states[h]
            raw_hi, raw_lo = raws[h]
            new[:, pl.ds(start, HALF)] = state
            sh, sl = split(stacked(state, rows, h))
            lh, ll = sh[:RANK], sl[:RANK]
            t = dot_t(jnp.concatenate([lh, ll, aux[h]], axis=0), jnp.concatenate([sh, raw_hi], axis=0))
            t2 = dot_t(jnp.concatenate([lh, aux[h]], axis=0), jnp.concatenate([sl, raw_lo], axis=0))
            t_main = t[:RANK] + t[RANK : 2 * RANK] + t2[:RANK]
            cross = cross + t_main[:, 128:]
            t_main = t_main[:, :128]
            a = t[2 * RANK : 2 * RANK + 8, :128]
            a2 = t2[RANK : RANK + 8, :128]
            row8 = sublanes((8, 128))
            a = a + jnp.where(row8 < 2, a2, 0.0)
            ones_sum = ones_sum + jnp.where(row8 == 0, a, a * g1)
            sums[h] = sums[h] + t_main
            y = y + u * t_main
        return sums[0], sums[1], y, cross, ones_sum

    zero = jnp.zeros((RANK, 128), f32)
    first, second, y, cross, ones_sum = lax.fori_loop(
        0, Q1, body, (zero, zero, zero, jnp.zeros((RANK, RANK), f32), jnp.zeros((8, 128), f32))
    )
    cross = jnp.concatenate([jnp.zeros((RANK, 96), f32), cross], axis=1)
    tile_a, tile_b = point_tiles(first, second, y, v_ref[0] >= 4, cross)
    out[:RANK, :128] = tile_a
    out[:RANK, 128:] = tile_b
    out[RANK:, :128] = ones_sum
    out[RANK:, 128:] = jnp.zeros((8, 128), f32)


def evolve_point(v, wl, src, values, after):
    return call(
        evolve_point_kernel, [(values.shape, f32), ((RANK + 8, 256), f32)], "ssvvvva",
        (v, SPEEDS, ROWS, wl, src, values, after), mib=16,
    )


RATES = (LOW - 1 + OWN + HIGH - 1) * NY
HALO = RANK * HIGH * NY


def fill_kernel(v_ref, own, edge, mine, other, after, state, rates_low, rates_high):
    core = v_ref[0] % 2
    state[:, LOW * PLANE : (LOW + OWN) * PLANE] = own[...]
    state[:, (LOW - 1) * PLANE : LOW * PLANE] = edge[...]
    for source, place in ((mine, core), (other, 1 - core)):

        def load(p, carry, source=source, place=place):
            for y in range(NY):
                at = aligned((p + place * (LOW + OWN)) * PLANE + y * NZ, 128)
                state[:, pl.ds(at, NZ)] = source[pl.ds(p * NY + y, RANK, stride=HIGH * NY), :]
            return carry

        lax.fori_loop(0, HIGH, load, 0)
    first, second = mine[HALO:, :], other[HALO:, :]
    rates_low[...] = jnp.where(core == 0, first, second)
    rates_high[...] = jnp.where(core == 0, second, first)


def fill_planes(v, own, edge, mine, other, after):
    part = ((HIGH * NY, NZ), f32)
    return call(
        fill_kernel, [((RANK, WIDE * PLANE), f32), part, part], "svvvva", (v, own, edge, mine, other, after),
        mib=12,
    )


def evolve_space_kernel(wk, moment, raw, rates, rates_low, rates_high, new, out, rates_all, partial, passed, *bufs):
    sources, targets = [raw, bufs[0], bufs[1]], [bufs[0], bufs[1], new]
    low, own = (LOW - 1) * NY, OWN * NY
    rates_all[:low, :] = rates_low[...]
    rates_all[low : low + own, :] = rates[...]
    rates_all[low + own :, :] = rates_high[: (HIGH - 1) * NY, :]
    lane = lanes((ROWS_K, 128))
    low_lane = (lane >= 64) & (lane < 96)

    for n in range(SUB):
        w = wk[min(n, 1)]
        w_hi = w.astype(bf16).astype(f32)
        w = jnp.where(low_lane, w - w_hi, w_hi).astype(bf16)[:, :96]
        if n > 0:
            w = w[RANK:]
        skip = w.shape[0] - ROWS_K + RANK
        src, dst = sources[n], targets[n]
        shift = 2 if n == SUB - 1 else 0
        begin, end = 1 + n, WIDE - 1 - n

        def tile(t, j, src=src):
            cells = src[:, pl.ds(aligned(t * PLANE + j * 256, 256), 256)]
            a, b = split(cells)
            return cells, jnp.concatenate([a, b, a], axis=0)

        def put(t, y, block, dst=dst, shift=shift):
            dst[:, pl.ds(aligned((t - shift) * PLANE + y * NZ, 128), NZ)] = block

        def step(t, carry, w=w, tile=tile, put=put, skip=skip):
            scale = moment[...]
            bases, ups, downs = [], [], []
            for j in range(NY // 2):
                cells, operand = tile(t, j)
                cut = skip + 2 * RANK
                mixed = dot(jnp.concatenate([w[skip + 6 * RANK :], w[:cut]], axis=0), operand)
                for i in range(2):
                    y = 2 * j + i
                    cell = slice(y * NZ, (y + 1) * NZ)
                    half = slice(i * NZ, (i + 1) * NZ)
                    up, down = mixed[16 + skip : 16 + skip + RANK, half], mixed[16 + skip + RANK :, half]
                    here = mixed[16 : 16 + RANK, half] if skip else cells[:, half]
                    density = mixed[:1, half]
                    put(t - 1, y, partial[:, cell] + down)
                    rate = rates_all[pl.ds((t - 1) * NY + y, 1), :]
                    bases.append(here + rate * (scale * density - here) + passed[:, cell] - (up + down))
                    passed[:, cell] = up
                mixed = dot(w[cut + 2 * RANK : cut + 4 * RANK], operand)
                for i in range(2):
                    y = 2 * j + i
                    half = slice(i * NZ, (i + 1) * NZ)
                    up, down = mixed[:RANK, half], mixed[RANK:, half]
                    bases[y] = bases[y] - (up + down) + roll_lanes(up, 1) + roll_lanes(down, -1)
                mixed = dot(w[cut : cut + 2 * RANK], operand)
                for i in range(2):
                    y = 2 * j + i
                    half = slice(i * NZ, (i + 1) * NZ)
                    part = [None, None] + [mixed[k * RANK : (k + 1) * RANK, half] for k in range(2)]
                    bases[y] = bases[y] - (part[2] + part[3])
                    ups.append(part[2])
                    downs.append(part[3])
                    if y >= 2:
                        partial[:, (y - 1) * NZ : y * NZ] = bases[y - 1] + ups[y - 2] + downs[y]
            partial[:, (NY - 1) * NZ :] = bases[NY - 1] + ups[NY - 2] + downs[0]
            partial[:, :NZ] = bases[0] + ups[NY - 1] + downs[1]
            return carry

        for j in range(NY // 2):
            passed[:, j * 256 : (j + 1) * 256] = dot(w[skip : skip + RANK], tile(begin - 1, j)[1])
        for t in range(begin, end):
            step(t, 0)
        for j in range(NY // 2):
            mixed = dot(w[skip + RANK : skip + 2 * RANK], tile(end, j)[1])
            for i in range(2):
                y = 2 * j + i
                put(end - 1, y, partial[:, y * NZ : (y + 1) * NZ] + mixed[:, i * NZ : (i + 1) * NZ])

    def body(p, carry):
        t, c = carry
        turned, relaxed = [], []
        for y in range(NY):
            block = new[:, pl.ds(aligned((p + 2) * PLANE + y * NZ, 128), NZ)]
            turned.append(split(roll_lanes(block, 1)))
            relaxed.append(split(block * rates[pl.ds(p * NY + y, 1), :]))
        here = split(new[:, pl.ds(aligned((p + 2) * PLANE, 128), PLANE)])
        behind = split(new[:, pl.ds(aligned((p + 1) * PLANE, 128), PLANE)])
        old = split(raw[:, pl.ds(aligned((p + LOW) * PLANE, 128), PLANE)])

        def stack(k):
            wrapped = jnp.concatenate([here[k][:, PLANE - NZ :], here[k][:, : PLANE - NZ]], axis=1)
            rolled = jnp.concatenate([block[k] for block in turned], axis=1)
            scaled = jnp.concatenate([block[k] for block in relaxed], axis=1)
            return jnp.concatenate([here[k], behind[k], wrapped, rolled, scaled, old[k]], axis=0)

        part = dot_t(jnp.concatenate(here, axis=0), stack(0))
        part = part[:RANK] + part[RANK:] + dot_t(here[0], stack(1))
        return t + part[:, :128], c + part[:, 128:]

    carry = (jnp.zeros((RANK, 128), f32), jnp.zeros((RANK, 64), f32))
    for p in range(OWN):
        carry = body(p, carry)
    t, c = carry
    out[:, :128] = t
    out[:, 128:] = jnp.concatenate([c, jnp.zeros((RANK, 64), f32)], axis=1)


def evolve_space(wk, moment, filled, rates):
    return call(
        evolve_space_kernel, [((RANK, (OWN + 2) * PLANE), f32), ((RANK, 256), f32)], "v" * 6,
        (wk, moment, filled[0], rates, filled[1], filled[2]),
        [pltpu.VMEM((RATES, NZ), f32)]
        + [pltpu.VMEM((RANK, PLANE), f32)] * 2
        + [pltpu.VMEM((RANK, WIDE * PLANE), f32)] * 2,
        mib=16,
    )


def finish_kernel(
    cells_total, points_total, p0, p1, p2, p3, core, kinetic, spread, space_out, fresh_core, point_out, fresh_space, fresh_point, sems
):
    both = four((p0, p1, p2, p3))
    s = both[:RANK] * (1.0 / cells_total)
    q = both[RANK:] * (1.0 / points_total)
    gram, gram_v = s[:, 0:32], q[:RANK, 0:32]
    (_, inverse), (_, inverse_v) = factor_pair(gram, gram_v)
    zeros = jnp.zeros((RANK, 32), f32)
    lane = lanes((RANK, 128))

    def wide(matrix):
        w = jnp.concatenate([matrix] * 3 + [zeros], axis=1)
        hi = w.astype(bf16).astype(f32)
        return jnp.where((lane >= 64) & (lane < 96), w - hi, hi).astype(bf16)[:, :96]

    w_space, w_point = wide(inverse), wide(inverse_v)

    def out_space(n):
        size = PLANE // 2
        at = 2 * PLANE + n * size
        hi, lo = split(kinetic[:, at : at + size])
        made = dot(w_space, jnp.concatenate([hi, lo, hi], axis=0))
        for y in range(NY // 2):
            fresh_space[pl.ds(n * (NY // 2) + y, RANK, stride=OWN * NY), :] = made[:, y * NZ : (y + 1) * NZ]

    def out_point(n):
        cells = slice(n * 1536, (n + 1) * 1536)
        hi, lo = split(spread[:, cells])
        fresh_point[:, cells] = dot(w_point, jnp.concatenate([hi, lo, hi], axis=0))

    third = 2 * Q1 * HALF // 3
    copies = []

    def outputs():
        for k in range(3):
            for n in range(3):
                out_point(3 * k + n)
                if n == 2:
                    cells = pl.ds(k * third, third)
                    copies.append(pltpu.make_async_copy(fresh_point.at[:, cells], point_out.at[:, cells], sems.at[k + 1]))
                    copies[-1].start()
                yield
        for n in range(2 * OWN):
            out_space(n)
            if n == 2 * OWN - 1:
                copies.append(pltpu.make_async_copy(fresh_space, space_out, sems.at[0]))
                copies[-1].start()
            yield

    writing = outputs()

    def write(count):
        for _ in range(count):
            next(writing, None)

    inverse_t = transposed(inverse)
    inverse_vt = transposed(inverse_v)
    turned = mm(inverse, s)
    turned_v = mm(inverse_v, q[:RANK])
    write(4)
    aux = mm(q[RANK:, 0:32], inverse_vt)
    weights_row = aux[0:1, :]
    moments_row = aux[1:2, :] + aux[2:3, :]
    left = [turned[:, 128:160]]
    for d in range(3):
        left.append(turned[:, 0:32] - turned[:, 32 * (d + 1) : 32 * (d + 2)])
    for d in range(3):
        left.append(mm_t(inverse, gram - s[:, 32 * (d + 1) : 32 * (d + 2)]))
    half = mm(turned[:, 160:192], core[...])
    write(3)
    stack = mm(jnp.concatenate(left, axis=0), inverse_t)
    lines = [turned_v[:, 192:224], turned_v[:, 160:192], turned_v[:, 64:96]]
    lines += [-turned_v[:, 128:160], -turned_v[:, 32:64], -turned_v[:, 96:128]]
    flux = mm(jnp.concatenate(lines, axis=0), inverse_vt)
    current = mm_t(half, turned_v[:, 224:256])
    for _ in range(SUB):
        write(2)
        moved = mm(stack, current)
        scaled = moved[:RANK]
        change = -scaled + jnp.sum(scaled * weights_row, axis=1, keepdims=True) * moments_row
        across = jnp.concatenate([moved[(k + 1) * RANK : (k + 2) * RANK] for k in range(6)], axis=1)
        write(2)
        current = current + (change - mm(across, flux))
    write(20)
    fresh_core[...] = current
    for copy in copies:
        copy.wait()


def finish(parts, core, kinetic, spread, cells_total, points_total):
    def kernel(*refs):
        finish_kernel(cells_total, points_total, *refs)

    flat = (RANK * OWN * NY, NZ)
    return call(
        kernel, [(flat, f32), ((RANK, RANK), f32), (spread.shape, f32)], "vvvvvvv",
        (*parts, core, kinetic, spread),
        [pltpu.VMEM(flat, f32), pltpu.VMEM(spread.shape, f32), pltpu.SemaphoreType.DMA((4,))],
        mib=12, out_spaces="ava",
    )


def spread_pairs(space_part):
    moved = []
    for k in range(2):
        route = [((s ^ (2 * v + k)) * 8 + v, s * 8 + v) for s in range(16) for v in range(8)]
        moved.append(lax.ppermute(space_part, ("space", "vel"), route))
    return moved


def vel_parts(moved, point_part):
    joint = jnp.concatenate([moved[0] + moved[1], point_part], axis=0)
    pair = [(2 * z + c, 2 * z + 1 - c) for z in range(4) for c in range(2)]
    joint = joint + lax.ppermute(joint, "vel", pair)
    routes = [[(2 * z + c, 2 * ((z + d) % 4) + c) for z in range(4) for c in range(2)] for d in (1, 2, 3)]
    parts = [joint]
    for route in routes:
        parts.append(lax.ppermute(joint, "vel", route))
    return parts


def per_device(space_factor, core_matrix, velocity_factor, collision_rates):
    devices = lax.axis_size("space")
    up = [(i, (i + 1) % devices) for i in range(devices)]
    below1 = lax.ppermute(space_factor[:, OWN - 1 :], "space", up).reshape(-1, NZ)
    rates = collision_rates.reshape(-1, NZ)
    values = space_factor.reshape(-1, NZ)
    cells_total = OWN * PLANE * devices
    points_total = velocity_factor.shape[1] * lax.axis_size("vel")
    place = lax.axis_index("vel").astype(jnp.int32)
    v = place.reshape(1)
    planes = jnp.where(place % 2 == 0, space_factor[:, : OWN - 1], space_factor[:, :HIGH])
    lines = jnp.where(place % 2 == 0, collision_rates[1:], collision_rates[:HIGH])
    halo = jnp.concatenate([planes, lines[None]], axis=0)
    route = [(s * 8 + w, (s + 1 - 2 * (w % 2)) % devices * 8 + w) for s in range(devices) for w in range(8)]
    pair = [(w, w ^ 1) for w in range(8)]

    inner, own = space_sums(values, rates)
    point = point_sums(v, velocity_factor, 0, 4, inner)
    space, edge = edge_sums(own, below1, inner)
    moved = spread_pairs(space)
    halo, space = lax.optimization_barrier((halo, space))
    mine = lax.ppermute(halo, ("space", "vel"), route)
    point = point_sums(v, velocity_factor, 4, Q1, point)
    parts = vel_parts(moved, point)
    mine, parts[0] = lax.optimization_barrier((mine, parts[0]))
    other = lax.ppermute(mine, "vel", pair)
    wk, wl, src, moment = small_first(parts, core_matrix, cells_total, points_total)
    filled = fill_planes(v, own, edge, mine.reshape(-1, NZ), other.reshape(-1, NZ), moment)
    kinetic, space = evolve_space(wk, moment, filled, rates)
    moved = spread_pairs(space)
    spread, point = evolve_point(v, wl, src, velocity_factor, space)
    parts = vel_parts(moved, point)
    fresh_space, fresh_core, fresh_point = finish(parts, core_matrix, kinetic, spread, cells_total, points_total)
    return fresh_space.reshape(space_factor.shape), fresh_core, fresh_point


def solution(mesh):
    return jax.shard_map(
        per_device,
        mesh=mesh,
        in_specs=(P(None, "space", None, None), P(), P(None, "vel"), P("space", None, None)),
        out_specs=(P(None, "space", None, None), P(), P(None, "vel")),
        check_vma=False,
    )
```
